256 devices in a mesh: tm: 64 (over y, z, core), head: 4 (over x).
Axes of the slice: x: 4, y: 4, z: 8, core: 2. Of those that a mesh axis runs over, the one named last changes fastest.
Arguments:
- series: bfloat16 [16384, 512], P('tm'), may hold values from -16 to 16
- in_weight: bfloat16 [512, 3, 1024], P(None, None, 'head'), may hold values from -0.25 to 0.25
- step_weight: bfloat16 [512, 16], P(None, 'head'), may hold values from -0.25 to 0.25
- step_bias: float32 [16], P('head'), may hold values from -7 to -6
- log_rate: float32 [16], P('head'), as said below
- conv_weight: float32 [4, 2, 1024], P(None, None, 'head'), may hold values from -3 to 3
- conv_bias: float32 [2, 1024], P(None, 'head'), may hold values from -3 to 3
- skip_gain: float32 [16], P('head'), may hold values from 0.5 to 1.5
- norm_gain: float32 [1024], P('head'), may hold values from 0.1 to 1.9
- out_weight: bfloat16 [512, 1024], P(None, 'head'), may hold values from -0.1875 to 0.1875
- cotangent: bfloat16 [16384, 512], P('tm'), may hold values from -6 to 6
Outputs:
- layer_out: bfloat16 [16384, 512], P(('tm', 'head'))
- series_grad: float32 [16384, 512], P(('tm', 'head'))
- w_in_grad: float32 [512, 3, 1024], P('tm', None, 'head')
- w_dt_grad: float32 [512, 16], P('tm', 'head')
- w_out_grad: float32 [512, 1024], P('tm', 'head')
The draws below stay inside these ranges and needn't reach their ends.
Inputs may be any that keep to these rules, and one draw needn't show every extreme that they name: `log_rate`: each head's logarithm of its decay rate.
All inputs are finite; a program needn't handle non-finite values.
Results may differ from the reference program's by a relative error of at most 0.0076.
Values may be sent and summed in bfloat16 or wider, within the bound.
A program may use at most 64 MiB of HBM per device.

```python
import math
import jax
import jax.numpy as jnp
from jax import lax

D = 512
E = 1024
H = 16
P_SIZE = 64
N = 128
GROUPS = 4
KW = 4
BLOCK = 256
TOKENS = 16384


def draw_log_rate(key, part):
    share = jax.random.uniform(key, (H,), jnp.float32)
    slowest = math.log(1.0 / (40.0 * TOKENS))
    fastest = math.log(1.0 / 30.0)
    return slowest + share * (fastest - slowest) - math.log(0.0025)


def spiked(entries, key, source, target, shards_of, factor):
    owner, partner = [(jnp.arange(entries.shape[position]) // (entries.shape[position] // shards_of)).reshape([-1 if axis == position else 1 for axis in range(entries.ndim)]) for position in (source, target)]
    chosen = jax.random.permutation(key, shards_of)[partner]
    strong = (owner == chosen) | (owner == (partner + shards_of // 2) % shards_of)
    return jnp.where(strong, factor * entries, entries)


def level_of(stream_key, shape, shards, low, top_value):
    factor_of, own = 1.0, jax.random.fold_in(stream_key, 6)
    for dim, blocks in shards:
        steps = jnp.exp(jax.random.uniform(jax.random.fold_in(own, dim), (blocks,), jnp.float32, low / len(shards), top_value / len(shards)))
        factor_of = factor_of * jnp.repeat(steps, shape[dim] // blocks).reshape([-1 if axis == dim else 1 for axis in range(len(shape))])
    return factor_of


def centred(key, shape, spread, bound, cuts=(), held_as=jnp.bfloat16):
    loudness = level_of(key, shape, cuts, -0.22, 0.18) if cuts else 1.0
    array = jax.random.normal(key, shape, jnp.float32) * spread * loudness
    return jnp.minimum(jnp.maximum(array, -bound), bound).astype(held_as)


def noise_with(stream_key, extent, scale, most, pieces, heavy, kind=jnp.bfloat16):
    drawn = scale * jax.random.normal(stream_key, extent, jnp.float32)
    if pieces:
        drawn = drawn * level_of(stream_key, extent, pieces, -0.22, 0.18)
    return jnp.clip(spiked(drawn, jax.random.fold_in(stream_key, 3), *heavy), -most, most).astype(kind)


def setup_inputs(seed: int = 0) -> dict:
    splits = jax.random.split(jax.random.key(seed), 12)
    series = noise_with(splits[0], (TOKENS, D), 1.0, 16.0, ((0, 64),), (0, 1, 64, 4.0))
    in_weight = centred(splits[1], (D, 3, E), D ** -0.5, 0.25, ((2, 4),))
    step_weight = centred(splits[2], (D, H), D ** -0.5, 0.25, ((1, 4),))
    step_bias = jnp.clip(-7.0 + 1.0 * jax.random.uniform(splits[3], (H,), jnp.float32) ** level_of(splits[3], (H,), ((0, 4),), -0.2, 0.2), -7.0, -6.0)
    log_rate = draw_log_rate(jax.random.fold_in(splits[11], 71), 0)
    conv_weight = centred(splits[5], (KW, 2, E), 0.5, 3.0, ((2, 4),), jnp.float32)
    conv_bias = centred(splits[6], (2, E), 0.5, 3.0, ((1, 4),), jnp.float32)
    skip_gain = jnp.clip(0.5 + 1.0 * jax.random.uniform(splits[7], (H,), jnp.float32) ** level_of(splits[7], (H,), ((0, 4),), -0.2, 0.2), 0.5, 1.5)
    norm_gain = jnp.clip(1.0 + 0.18 * jax.random.normal(splits[8], (E,), jnp.float32), 0.1, 1.9)
    out_weight = centred(splits[9], (D, E), E ** -0.5, 0.1875, ((1, 4),))
    cotangent = centred(splits[10], (TOKENS, D), 1.0, 6.0, ((0, 64),))
    return dict(series=series, in_weight=in_weight, step_weight=step_weight, step_bias=step_bias, log_rate=log_rate, conv_weight=conv_weight, conv_bias=conv_bias, skip_gain=skip_gain, norm_gain=norm_gain, out_weight=out_weight, cotangent=cotangent)


NORM_EPSILON = 1e-05
HIGHEST_PRECISION = lax.Precision.HIGHEST
HIGH_PRECISION = lax.Precision.HIGH

def contract(left_side, right_side, left_dim, right_dim):
    return lax.dot_general(left_side, right_side, (((left_dim,), (right_dim,)), ((), ())), preferred_element_type=jnp.float32)

def silu_grad(values):
    sigmoid_v = jax.nn.sigmoid(values)
    return sigmoid_v * (1.0 + values * (1.0 - sigmoid_v))

def decay_table(log_block):
    running = jnp.cumsum(log_block, axis=0)
    length = log_block.shape[0]
    row_ids = lax.broadcasted_iota(jnp.int32, (length, length), 0)
    col_ids = lax.broadcasted_iota(jnp.int32, (length, length), 1)
    log_gap = running.T[:, :, None] - running.T[:, None, :]
    decays = jnp.exp(jnp.where((col_ids <= row_ids)[None], log_gap, -1e+30))
    return (running, decays)

def block_forward(x_block, b_block, c_block, step_block, log_block, start_state, skip_gain):
    per_group = x_block.shape[1] // b_block.shape[1]
    x_wide = x_block.astype(jnp.float32)
    b_wide = b_block.astype(jnp.float32)
    c_wide = c_block.astype(jnp.float32)
    b_heads = jnp.repeat(b_wide, per_group, axis=1)
    c_heads = jnp.repeat(c_wide, per_group, axis=1)
    running, decays = decay_table(log_block)
    scores = jnp.einsum('ign,jgn->gij', c_block, b_block, preferred_element_type=jnp.float32)
    mixing = jnp.repeat(scores, per_group, axis=0) * decays * step_block.T[:, None, :]
    inside = jnp.einsum('hij,jhp->ihp', mixing, x_wide, precision=HIGH_PRECISION)
    from_state = jnp.exp(running)[:, :, None] * jnp.einsum('ihn,hpn->ihp', c_heads, start_state, precision=HIGH_PRECISION)
    output = inside + from_state + skip_gain[None, :, None] * x_wide
    remain = jnp.exp(running[-1][None, :] - running) * step_block
    end_state = jnp.exp(running[-1])[:, None, None] * start_state + jnp.einsum('jh,jhp,jhn->hpn', remain, x_wide, b_heads, precision=HIGH_PRECISION)
    return (output, end_state)

def block_backward(x_block, b_block, c_block, step_block, log_block, start_state, skip_gain, grad_y, ssm_out, after_state):
    group_count = b_block.shape[1]
    per_group = x_block.shape[1] // group_count
    length = x_block.shape[0]
    x_wide = x_block.astype(jnp.float32)
    b_wide = b_block.astype(jnp.float32)
    c_wide = c_block.astype(jnp.float32)
    b_heads = jnp.repeat(b_wide, per_group, axis=1)
    c_heads = jnp.repeat(c_wide, per_group, axis=1)
    running, decays = decay_table(log_block)
    scores = jnp.einsum('ign,jgn->gij', c_block, b_block, preferred_element_type=jnp.float32)
    weighted = jnp.repeat(scores, per_group, axis=0) * decays
    remain = jnp.exp(running[-1][None, :] - running)
    back_b = jnp.einsum('hit,ihp->thp', weighted, grad_y, precision=HIGH_PRECISION)
    back_b = back_b + remain[:, :, None] * jnp.einsum('thn,hpn->thp', b_heads, after_state, precision=HIGH_PRECISION)
    grad_x = skip_gain[None, :, None] * grad_y + step_block[:, :, None] * back_b
    x_back = lax.optimization_barrier(jnp.sum(x_wide * back_b, axis=2))
    grad_cum = lax.optimization_barrier(jnp.sum(grad_y * ssm_out, axis=2)) - step_block * x_back
    pair_terms = decays * jnp.einsum('ihp,jhp->hij', grad_y, x_wide, precision=HIGH_PRECISION) * step_block.T[:, None, :]
    group_terms = pair_terms.reshape(group_count, per_group, length, length).sum(axis=1)
    state_c = jnp.exp(running)[:, :, None] * jnp.einsum('ihp,hpn->ihn', grad_y, start_state, precision=HIGH_PRECISION)
    grad_c = jnp.einsum('gij,jgn->ign', group_terms, b_wide, precision=HIGH_PRECISION) + state_c.reshape(length, group_count, per_group, -1).sum(axis=2)
    state_b = (step_block * remain)[:, :, None] * jnp.einsum('jhp,hpn->jhn', x_wide, after_state, precision=HIGH_PRECISION)
    grad_b = jnp.einsum('gij,ign->jgn', group_terms, c_wide, precision=HIGH_PRECISION) + state_b.reshape(length, group_count, per_group, -1).sum(axis=2)
    before = jnp.exp(running[-1])[:, None, None] * after_state + jnp.einsum('ih,ihp,ihn->hpn', jnp.exp(running), grad_y, c_heads, precision=HIGH_PRECISION)
    return (grad_x, grad_b, grad_c, x_back, grad_cum, before)

def reference(series, in_weight, step_weight, step_bias, log_rate, conv_weight, conv_bias, skip_gain, norm_gain, out_weight, cotangent):
    margin = KW - 1
    block_total = TOKENS // BLOCK
    w_flat = in_weight.reshape(D, 3 * E)
    padded = jnp.concatenate([jnp.zeros((margin, D), jnp.bfloat16), series], axis=0)
    decay_rates = jnp.exp(log_rate)

    def front(block_index, start_state):
        rows_wide = lax.dynamic_slice_in_dim(padded, block_index * BLOCK, BLOCK + margin, 0)
        rows_here = rows_wide[margin:]
        projected = jnp.dot(rows_wide, w_flat, preferred_element_type=jnp.float32).astype(jnp.bfloat16).reshape(BLOCK + margin, 3, E)
        pre_wide = projected[:, 1:, :].astype(jnp.float32)
        conv_out = conv_bias[None] + conv_weight[0][None] * pre_wide[0:BLOCK]
        for offset in range(1, KW):
            conv_out = conv_out + conv_weight[offset][None] * pre_wide[offset:offset + BLOCK]
        activated = jax.nn.silu(conv_out)
        x_heads = activated[:, 0].astype(jnp.bfloat16).reshape(BLOCK, H, P_SIZE)
        bc_values = activated[:, 1].astype(jnp.bfloat16).reshape(BLOCK, GROUPS, 2, N)
        gate_raw = projected[margin:, 0].astype(jnp.float32)
        step_raw = jnp.dot(rows_here, step_weight, preferred_element_type=jnp.float32)
        step_size = jax.nn.softplus(step_raw + step_bias[None])
        log_decay = -step_size * decay_rates[None]
        output, end_state = block_forward(x_heads, bc_values[:, :, 0], bc_values[:, :, 1], step_size, log_decay, start_state, skip_gain)
        y_flat = output.reshape(BLOCK, E)
        gate_act = jax.nn.silu(gate_raw)
        gated_out = y_flat * gate_act
        inv_rms = lax.rsqrt(lax.optimization_barrier(jnp.sum(gated_out * gated_out, axis=1)) / E + NORM_EPSILON)
        normed = (gated_out * inv_rms[:, None] * norm_gain[None]).astype(jnp.bfloat16)
        return (rows_here, conv_out, x_heads, bc_values, gate_raw, step_raw, step_size, log_decay, output, end_state, y_flat, gate_act, gated_out, inv_rms, normed)

    def forward_step(carried, block_index):
        parts = front(block_index, carried)
        layer_block = contract(parts[14], out_weight, 1, 1).astype(jnp.bfloat16)
        return (parts[9], (layer_block, carried))
    block_ids = jnp.arange(block_total, dtype=jnp.int32)
    _, (layer_blocks, starts) = lax.scan(forward_step, jnp.zeros((H, P_SIZE, N), jnp.float32), block_ids)

    def backward_step(carried, inputs):
        block_index, start_state = inputs
        after_state, later_sum, next_rows, in_sum, dt_sum, out_sum = carried
        rows_here, conv_out, x_heads, bc_values, gate_raw, step_raw, step_size, log_decay, output, end_state, y_flat, gate_act, gated_out, inv_rms, normed = front(block_index, start_state)
        grad_here = lax.dynamic_slice_in_dim(cotangent, block_index * BLOCK, BLOCK, 0)
        grad_normed = jnp.dot(grad_here, out_weight, preferred_element_type=jnp.float32)
        out_sum = out_sum + contract(grad_here, normed, 0, 0)
        gain_grad = norm_gain[None] * grad_normed
        inner_sum = lax.optimization_barrier(jnp.sum(gated_out * gain_grad, axis=1))
        grad_gated = inv_rms[:, None] * gain_grad - gated_out * (inv_rms ** 3 * inner_sum / E)[:, None]
        grad_y = (grad_gated * gate_act).reshape(BLOCK, H, P_SIZE)
        grad_gate = grad_gated * y_flat * silu_grad(gate_raw)
        ssm_out = output - skip_gain[None, :, None] * x_heads.astype(jnp.float32)
        grad_x, grad_b, grad_c, x_back, grad_cum, before = block_backward(x_heads, bc_values[:, :, 0], bc_values[:, :, 1], step_size, log_decay, start_state, skip_gain, grad_y, ssm_out, after_state)
        grad_log = lax.cumsum(grad_cum, axis=0, reverse=True) + later_sum[None]
        grad_step = x_back - decay_rates[None] * grad_log
        grad_raw = (grad_step * jax.nn.sigmoid(step_raw + step_bias[None])).astype(jnp.bfloat16)
        grad_bc = jnp.stack([grad_b, grad_c], axis=2).reshape(BLOCK, E)
        grad_act = jnp.stack([grad_x.reshape(BLOCK, E), grad_bc], axis=1)
        grad_conv = grad_act * silu_grad(conv_out)
        grad_wide = jnp.concatenate([grad_conv, next_rows], axis=0)
        grad_pre = conv_weight[0][None] * grad_wide[margin:margin + BLOCK]
        for offset in range(1, KW):
            grad_pre = grad_pre + conv_weight[offset][None] * grad_wide[margin - offset:margin - offset + BLOCK]
        grad_proj = jnp.concatenate([grad_gate[:, None], grad_pre], axis=1).astype(jnp.bfloat16).reshape(BLOCK, 3 * E)
        in_sum = in_sum + contract(rows_here, grad_proj, 0, 0)
        dt_sum = dt_sum + contract(rows_here, grad_raw, 0, 0)
        grad_rows = contract(grad_proj, w_flat, 1, 1) + contract(grad_raw, step_weight, 1, 1)
        carried = (before, later_sum + lax.optimization_barrier(jnp.sum(grad_cum, axis=0)), grad_conv[:margin], in_sum, dt_sum, out_sum)
        return (carried, grad_rows)
    initial = (jnp.zeros((H, P_SIZE, N), jnp.float32), jnp.zeros((H,), jnp.float32), jnp.zeros((margin, 2, E), jnp.float32), jnp.zeros((D, 3 * E), jnp.float32), jnp.zeros((D, H), jnp.float32), jnp.zeros((D, E), jnp.float32))
    finals, grad_blocks = lax.scan(backward_step, initial, (block_ids, starts), reverse=True)
    layer_out = layer_blocks.reshape(TOKENS, D)
    series_grad = grad_blocks.reshape(TOKENS, D)
    return (layer_out, series_grad, finals[3].reshape(D, 3, E), finals[4], finals[5])
```

```python
import functools

import jax
import jax.numpy as jnp
from jax import lax
from jax.experimental import pallas as pl
from jax.experimental.pallas import tpu as pltpu
from jax.sharding import PartitionSpec as P

N = 128
KW = 4
E = 1024
EPS = 1e-05
MESH = pl.DeviceIdType.MESH
F32 = jnp.float32
BF16 = jnp.bfloat16

RIM, DEC, SCAN1, BACK1, NORM, LAYER, SCAN2, BACK2, RIM2, WSUM1, WSUM2, ROWS = range(12)


def bf(v):
    return v.astype(BF16)


def mm(a, b, ca=1, cb=0):
    return lax.dot_general(
        bf(a), bf(b), (((ca,), (cb,)), ((), ())), preferred_element_type=F32
    )


def parts_of(v, count):
    parts = []
    for _ in range(count):
        head = bf(v)
        parts.append(head)
        v = v - head.astype(F32)
    return parts


def mm_left(exact, v, ca=1, cb=0, count=3):
    total = None
    for part in parts_of(v, count):
        term = mm(exact, part, ca, cb)
        total = term if total is None else total + term
    return total


def mm_right(v, exact, ca=1, cb=0, count=3):
    total = None
    for part in parts_of(v, count):
        term = mm(part, exact, ca, cb)
        total = term if total is None else total + term
    return total


def sigmoid(v):
    return 1.0 / (1.0 + jnp.exp(-v))


def softplus(v):
    return jnp.maximum(v, 0.0) + jnp.log1p(jnp.exp(-jnp.abs(v)))


def spread(scalars, shape, width):
    lane = lax.broadcasted_iota(jnp.int32, shape, 1) // width
    out = jnp.zeros(shape, F32)
    for h in range(scalars.shape[0]):
        out = jnp.where(lane == h, scalars[h], out)
    return out


def kernel(
    n_tm,
    n_head,
    series,
    w_in,
    w_dt,
    step_bias,
    log_rate,
    conv_w,
    conv_b,
    skip_gain,
    norm_gain,
    w_out,
    cot,
    layer_ref,
    rows_ref,
    w_in_ref,
    w_dt_ref,
    w_out_ref,
    rim_in,
    dec_send,
    dec_all,
    state_send,
    state_all,
    prefix_send,
    prefix_all,
    back_send,
    back_all,
    suffix_send,
    suffix_all,
    flat_state,
    own_keep,
    incoming,
    norm_send,
    norm_all,
    layer_send,
    layer_all,
    grow_send,
    grow_all,
    rim2_send,
    rim2_in,
    sum1_send,
    sum1_all,
    sum2_send,
    sum2_all,
    pre_buf,
    conv_buf,
    decays,
    inside_buf,
    gproj,
    send_sem,
    recv_sem,
):
    me = lax.axis_index("tm")
    mine = lax.axis_index("head")
    rows, inner = series.shape[0], w_out.shape[1]
    heads = step_bias.shape[0]
    size = inner // heads
    model = series.shape[1]
    per_owner = inner // n_tm
    owners_per_head = n_tm // heads
    quarter = rows // n_head

    barrier = pltpu.get_barrier_semaphore()

    def greet(d, c):
        pl.semaphore_signal(
            barrier, inc=1, device_id=(lax.rem(me + d, n_tm), mine), device_id_type=MESH
        )
        return c

    lax.fori_loop(1, n_tm, greet, 0)
    for d in range(1, n_head):
        pl.semaphore_signal(
            barrier, inc=1, device_id=(me, lax.rem(mine + d, n_head)), device_id_type=MESH
        )

    def push(src, dst, which, device):
        pltpu.make_async_remote_copy(
            src_ref=src,
            dst_ref=dst,
            send_sem=send_sem.at[which],
            recv_sem=recv_sem.at[which],
            device_id=device,
            device_id_type=MESH,
        ).start()

    def arrived(ref, which):
        pltpu.make_async_copy(ref, ref, recv_sem.at[which]).wait()

    def departed(ref, which):
        pltpu.make_async_copy(ref, ref, send_sem.at[which]).wait()

    def to_all(source_of, dst, which):
        def one(d, c):
            peer = lax.rem(me + d, n_tm)
            push(source_of(peer), dst.at[me], which, (peer, mine))
            return c

        lax.fori_loop(1, n_tm, one, 0)

    def to_heads(source_of, dst, which):
        for d in range(1, n_head):
            peer = lax.rem(mine + d, n_head)
            push(source_of(peer), dst.at[mine], which, (me, peer))

    expand = (
        lax.broadcasted_iota(jnp.int32, (heads, inner), 1) // size
        == lax.broadcasted_iota(jnp.int32, (heads, inner), 0)
    ).astype(BF16)
    narrow_eye = (
        lax.broadcasted_iota(jnp.int32, (heads, N), 1)
        == lax.broadcasted_iota(jnp.int32, (heads, N), 0)
    ).astype(BF16)
    w_dt_wide = bf(mm(w_dt[...], expand))
    w_dt_narrow = bf(mm(w_dt[...], narrow_eye))
    rate_wide = jnp.exp(spread(log_rate, (1, inner), size))
    skip_wide = spread(skip_gain, (1, inner), size)
    step = softplus(mm(series[...], w_dt_wide) + spread(step_bias, (1, inner), size))
    row_id = lax.broadcasted_iota(jnp.int32, (rows, rows), 0)
    col_id = lax.broadcasted_iota(jnp.int32, (rows, rows), 1)
    below = col_id <= row_id
    run = mm_left(below.astype(BF16), -step * rate_wide)
    last = run[rows - 1 : rows, :]
    for h in range(heads):
        dec_send[h] = jnp.broadcast_to(last[:, h * size : h * size + 1], (1, N))

    pl.semaphore_wait(barrier, n_tm - 1 + n_head - 1)
    nxt, prv = lax.rem(me + 1, n_tm), lax.rem(me + n_tm - 1, n_tm)
    push(series.at[pl.ds(rows - 16, 16)], rim_in, RIM, (nxt, mine))
    to_all(lambda peer: dec_send.at[peer // owners_per_head], dec_all, DEC)
    dec_all[me] = dec_send[me // owners_per_head]

    projected = bf(mm(series[...], w_in[...])).astype(F32)
    gate = projected[:, :inner]
    pre_buf[pl.ds(8, rows), :] = projected[:, inner:]
    gate_sig = sigmoid(gate)
    gate_act = gate * gate_sig
    gain_grad = norm_gain[...] * mm(cot[...], w_out[...])
    run_t = run.T
    step_t = step.T
    for h in range(heads):
        gap = run[:, h * size : h * size + 1] - run_t[h * size : h * size + 1, :]
        decays[h] = jnp.exp(jnp.where(below, gap, -1e30))
    grow = jnp.exp(run)
    remain = jnp.exp(last - run)

    arrived(rim_in, RIM)
    rim = bf(mm(rim_in[...], w_in[:, inner:])).astype(F32)[8:16]
    pre_buf[pl.ds(0, 8), :] = jnp.where(me > 0, rim, 0.0)

    def conv_row(k):
        return jnp.concatenate([conv_w[k, 0:1, :], conv_w[k, 1:2, :]], axis=1)

    conv = jnp.concatenate([conv_b[0:1, :], conv_b[1:2, :]], axis=1)
    for k in range(KW):
        conv = conv + conv_row(k) * pre_buf[pl.ds(8 - (KW - 1) + k, rows), :]
    conv_sig = sigmoid(conv)
    active = bf(conv * conv_sig)
    conv_buf[...] = conv_sig * (1.0 + conv * (1.0 - conv_sig))
    x = active[:, :inner]
    b = active[:, inner : inner + N]
    c = active[:, inner + N :]
    xw = x.astype(F32)

    def exchange(own, send, everything, out_send, out_all, which, back, reverse, during):
        flat_state[...] = own

        def pack(j, k):
            send[j] = flat_state[pl.ds(per_owner * j, per_owner), :]
            return k

        lax.fori_loop(0, n_tm, pack, 0, unroll=8)
        to_all(lambda peer: send.at[peer], everything, which)
        everything[me] = send[me]
        kept = during()
        arrived(everything.at[pl.ds(0, n_tm - 1)], which)

        def hop(k, before):
            at = n_tm - 1 - k if reverse else k
            out_send[at] = before

            @pl.when(at != me)
            def _():
                push(out_send.at[at], out_all.at[me], back, (at, mine))

            return before * jnp.exp(dec_all[at]) + everything[at]

        lax.fori_loop(0, n_tm, hop, jnp.zeros((per_owner, N), F32))
        out_all[me] = out_send[me]
        return kept

    def collect(out_all, back):
        arrived(out_all.at[pl.ds(0, n_tm - 1)], back)

        def unpack(j, k):
            flat_state[pl.ds(per_owner * j, per_owner), :] = out_all[j]
            return k

        lax.fori_loop(0, n_tm, unpack, 0, unroll=8)
        return flat_state[...]

    own = mm(remain * step * xw, b, 0, 0)
    own_keep[...] = own

    def intra_forward():
        scores = mm(c, b, 1, 1)
        for h in range(heads):
            at = slice(h * size, (h + 1) * size)
            mixing = scores * decays[h] * step_t[h * size : h * size + 1, :]
            inside_buf[:, at] = mm(mixing, x[:, at])
        return scores

    def first_wait():
        arrived(dec_all.at[pl.ds(0, n_tm - 1)], DEC)
        return intra_forward()

    scores = exchange(
        own, state_send, state_all, prefix_send, prefix_all, SCAN1, BACK1, False, first_wait
    )
    start = collect(prefix_all, BACK1)
    incoming[...] = start

    ssm = inside_buf[...] + grow * mm(c, start, 1, 1)
    y = ssm + skip_wide * xw
    gated = y * gate_act
    ones = jnp.ones((8, inner), BF16)
    power = mm_left(ones, gated * gated, 1, 1, 2)
    cross = mm_left(ones, gated * gain_grad, 1, 1, 2)
    first_row = lax.broadcasted_iota(jnp.int32, (8, rows), 0) == 0
    norm_send[...] = jnp.where(first_row, power, cross)
    to_heads(lambda peer: norm_send, norm_all, NORM)
    norm_all[mine] = norm_send[...]
    arrived(norm_all.at[pl.ds(0, n_head - 1)], NORM)
    totals = norm_all[0]
    for p in range(1, n_head):
        totals = totals + norm_all[p]
    inv_row = lax.rsqrt(totals[0:1] / E + EPS)
    coef_row = inv_row * inv_row * inv_row * totals[1:2] / E
    inv = jnp.broadcast_to(inv_row, (inner, rows)).T
    coef = jnp.broadcast_to(coef_row, (inner, rows)).T
    grad_gated = inv * gain_grad - gated * coef
    grad_y = grad_gated * gate_act
    gy = bf(grad_y)
    grown = bf(grow * grad_y)
    normed = bf(gated * inv * norm_gain[...])
    grad_gate = bf(grad_gated * y * (gate_sig * (1.0 + gate * (1.0 - gate_sig))))
    gproj[:, :inner] = grad_gate

    def intra_backward():
        group = jnp.zeros((rows, rows), F32)
        for h in range(heads):
            at = slice(h * size, (h + 1) * size)
            inside_buf[:, at] = mm(scores * decays[h], gy[:, at], 0, 0)
            group = group + decays[h] * mm(gy[:, at], x[:, at], 1, 1) * (
                step_t[h * size : h * size + 1, :]
            )
        grad_c = mm(group, b) + mm(grown, start)
        grad_b = mm(group, c, 0, 0)
        part = bf(mm(normed, w_out[...], 1, 1))
        for p in range(n_head):
            layer_send[p] = part[p * quarter : (p + 1) * quarter]
        to_heads(lambda peer: layer_send.at[peer], layer_all, LAYER)
        layer_all[mine] = layer_send[mine]
        chunk = (n_tm, model // n_tm, inner)
        sum1_send[...] = bf(
            jnp.concatenate(
                [
                    mm(cot[...], normed, 0, 0).reshape(chunk),
                    mm(series[...], grad_gate, 0, 0).reshape(chunk),
                ],
                axis=1,
            )
        )
        return grad_b, grad_c

    grad_b, grad_c = exchange(
        mm(grown, c, 0, 0),
        back_send,
        back_all,
        suffix_send,
        suffix_all,
        SCAN2,
        BACK2,
        True,
        intra_backward,
    )
    to_all(lambda peer: sum1_send.at[peer], sum1_all, WSUM1)
    sum1_all[me] = sum1_send[me]
    after = collect(suffix_all, BACK2)

    back_b = inside_buf[...] + remain * mm(b, after, 1, 1)
    grad_x = skip_wide * grad_y + step * back_b
    grad_b = grad_b + mm(step * remain * xw, after)
    gc = jnp.concatenate([grad_x, grad_b, grad_c], axis=1) * conv_buf[...]
    pre_buf[pl.ds(0, rows), :] = gc
    rim2_send[...] = gc[0:8]
    push(rim2_send, rim2_in, RIM2, (prv, mine))

    choose = (
        lax.broadcasted_iota(jnp.int32, (inner, N), 0) // size
        == lax.broadcasted_iota(jnp.int32, (inner, N), 1)
    )
    pick = choose.astype(BF16)
    shift_n = mm(series[...], w_dt_narrow) + spread(step_bias, (1, N), 1)
    x_back = mm_right(xw * back_b, pick)
    grad_cum = mm_right(grad_y * ssm, pick) - softplus(shift_n) * x_back
    final = jnp.exp(run_t[:, rows - 1 : rows]) * start + own_keep[...]
    carried = jnp.sum(
        jnp.where(choose, jnp.sum(after * final, axis=1, keepdims=True), 0.0),
        axis=0,
        keepdims=True,
    )
    grad_log = mm_left((col_id >= row_id).astype(BF16), grad_cum) + carried
    rate_n = jnp.exp(spread(log_rate, (1, N), 1))
    grad_raw = bf((x_back - rate_n * grad_log) * sigmoid(shift_n))

    arrived(rim2_in, RIM2)
    pre_buf[pl.ds(rows, 8), :] = jnp.where(me < n_tm - 1, rim2_in[...], 0.0)
    grad_pre = conv_row(0) * pre_buf[pl.ds(KW - 1, rows), :]
    for k in range(1, KW):
        grad_pre = grad_pre + conv_row(k) * pre_buf[pl.ds(KW - 1 - k, rows), :]
    grad_pre = bf(grad_pre)
    gproj[:, inner:] = grad_pre

    deep = mm(series[...], grad_pre, 0, 0)
    thin = mm(series[...], grad_raw, 0, 0)
    chunk = (n_tm, model // n_tm, inner)
    sum2_send[:, :, :inner] = bf(
        jnp.concatenate(
            [deep[:, :inner].reshape(chunk), deep[:, inner:].reshape(chunk)], axis=1
        )
    )
    thin = thin.reshape(n_tm, model // n_tm, N)
    sum2_send[:, :, inner:] = bf(jnp.concatenate([thin, jnp.zeros_like(thin)], axis=1))
    to_all(lambda peer: sum2_send.at[peer], sum2_all, WSUM2)
    sum2_all[me] = sum2_send[me]

    grad_rows = bf(mm(gproj[...], w_in[...], 1, 1) + mm(grad_raw, w_dt_narrow, 1, 1))
    for p in range(n_head):
        grow_send[p] = grad_rows[p * quarter : (p + 1) * quarter]
    to_heads(lambda peer: grow_send.at[peer], grow_all, ROWS)
    grow_all[mine] = grow_send[mine]

    def over_heads(everything):
        total = everything[0].astype(F32)
        for p in range(1, n_head):
            total = total + everything[p].astype(F32)
        return total

    arrived(layer_all.at[pl.ds(0, n_head - 1)], LAYER)
    layer_ref[...] = bf(over_heads(layer_all))
    arrived(sum1_all.at[pl.ds(0, n_tm - 1)], WSUM1)
    arrived(grow_all.at[pl.ds(0, n_head - 1)], ROWS)
    rows_ref[...] = over_heads(grow_all)

    def over_slabs(everything):
        def add(k, total):
            return total + everything[k].astype(F32)

        return lax.fori_loop(0, n_tm, add, jnp.zeros(everything.shape[1:], F32), unroll=4)

    few = model // n_tm
    total1 = over_slabs(sum1_all)
    w_out_ref[...] = total1[:few]
    w_in_ref[:, :inner] = total1[few:]
    arrived(sum2_all.at[pl.ds(0, n_tm - 1)], WSUM2)
    total2 = over_slabs(sum2_all)
    w_in_ref[:, inner : 2 * inner] = total2[:few, :inner]
    w_in_ref[:, 2 * inner :] = total2[few:, :inner]
    w_dt_ref[...] = total2[:few, inner:]

    departed(rim_in, RIM)
    departed(dec_all.at[pl.ds(0, n_tm - 1)], DEC)
    departed(state_all.at[pl.ds(0, n_tm - 1)], SCAN1)
    departed(prefix_all.at[pl.ds(0, n_tm - 1)], BACK1)
    departed(norm_all.at[pl.ds(0, n_head - 1)], NORM)
    departed(layer_all.at[pl.ds(0, n_head - 1)], LAYER)
    departed(back_all.at[pl.ds(0, n_tm - 1)], SCAN2)
    departed(suffix_all.at[pl.ds(0, n_tm - 1)], BACK2)
    departed(rim2_in, RIM2)
    departed(sum1_all.at[pl.ds(0, n_tm - 1)], WSUM1)
    departed(sum2_all.at[pl.ds(0, n_tm - 1)], WSUM2)
    departed(grow_all.at[pl.ds(0, n_head - 1)], ROWS)


def solution(mesh):
    n_tm, n_head = mesh.shape["tm"], mesh.shape["head"]

    def body(
        series,
        in_weight,
        step_weight,
        step_bias,
        log_rate,
        conv_weight,
        conv_bias,
        skip_gain,
        norm_gain,
        out_weight,
        cotangent,
    ):
        rows, model = series.shape
        inner = out_weight.shape[1]
        heads = step_bias.shape[0]
        few = model // n_tm
        quarter = rows // n_head
        vmem = pl.BlockSpec(memory_space=pltpu.VMEM)
        smem = pl.BlockSpec(memory_space=pltpu.SMEM)
        slab = pltpu.VMEM((n_tm, inner // n_tm, N), F32)
        peers = pltpu.VMEM((n_head, quarter, model), BF16)
        layer, rows_grad, w_in, w_dt, w_out = pl.pallas_call(
            functools.partial(kernel, n_tm, n_head),
            out_shape=(
                jax.ShapeDtypeStruct((quarter, model), BF16),
                jax.ShapeDtypeStruct((quarter, model), F32),
                jax.ShapeDtypeStruct((few, 3 * inner), F32),
                jax.ShapeDtypeStruct((few, N), F32),
                jax.ShapeDtypeStruct((few, inner), F32),
            ),
            in_specs=[vmem, vmem, vmem, smem, smem, vmem, vmem, smem, vmem, vmem, vmem],
            out_specs=(vmem,) * 5,
            scratch_shapes=[
                pltpu.VMEM((16, model), BF16),
                pltpu.VMEM((heads, 1, N), F32),
                pltpu.VMEM((n_tm, 1, N), F32),
                slab,
                slab,
                slab,
                slab,
                slab,
                slab,
                slab,
                slab,
                pltpu.VMEM((inner, N), F32),
                pltpu.VMEM((inner, N), F32),
                pltpu.VMEM((inner, N), F32),
                pltpu.VMEM((8, rows), F32),
                pltpu.VMEM((n_head, 8, rows), F32),
                peers,
                peers,
                peers,
                peers,
                pltpu.VMEM((8, 2 * inner), F32),
                pltpu.VMEM((8, 2 * inner), F32),
                pltpu.VMEM((n_tm, 2 * few, inner), BF16),
                pltpu.VMEM((n_tm, 2 * few, inner), BF16),
                pltpu.VMEM((n_tm, 2 * few, inner + N), BF16),
                pltpu.VMEM((n_tm, 2 * few, inner + N), BF16),
                pltpu.VMEM((rows + 8, 2 * inner), F32),
                pltpu.VMEM((rows, 2 * inner), F32),
                pltpu.VMEM((heads, rows, rows), F32),
                pltpu.VMEM((rows, inner), F32),
                pltpu.VMEM((rows, 3 * inner), BF16),
                pltpu.SemaphoreType.DMA((12,)),
                pltpu.SemaphoreType.DMA((12,)),
            ],
            compiler_params=pltpu.CompilerParams(collective_id=0, has_side_effects=True),
        )(
            series,
            in_weight.reshape(model, 3 * inner),
            step_weight,
            step_bias,
            log_rate,
            conv_weight,
            conv_bias,
            skip_gain,
            norm_gain.reshape(1, inner),
            out_weight,
            cotangent,
        )
        return (layer, rows_grad, w_in.reshape(few, 3, inner), w_dt[:, :heads], w_out)

    in_specs = (
        P("tm", None),
        P(None, None, "head"),
        P(None, "head"),
        P("head"),
        P("head"),
        P(None, None, "head"),
        P(None, "head"),
        P("head"),
        P("head"),
        P(None, "head"),
        P("tm", None),
    )
    out_specs = (
        P(("tm", "head"), None),
        P(("tm", "head"), None),
        P("tm", None, "head"),
        P("tm", "head"),
        P("tm", "head"),
    )
    return jax.shard_map(body, mesh=mesh, in_specs=in_specs, out_specs=out_specs, check_vma=False)
```

```python
import functools

import jax
import jax.numpy as jnp
from jax import lax
from jax.experimental import pallas as pl
from jax.experimental.pallas import tpu as pltpu
from jax.sharding import PartitionSpec as P

N = 128
KW = 4
E = 1024
EPS = 1e-05
MESH = pl.DeviceIdType.MESH
F32 = jnp.float32
BF16 = jnp.bfloat16

NZ = 8
RIM, DEC, SCAN1, BACK1, NORM, LAYER, SCAN2, BACK2, RIM2, ROWS = range(10)
CORE1, ALONG_Y1, ALONG_Z1, CORE2, ALONG_Y2, ALONG_Z2 = range(10, 16)
LOADS = 8


def bf(v):
    return v.astype(BF16)


def mm(a, b, ca=1, cb=0):
    return lax.dot_general(
        bf(a), bf(b), (((ca,), (cb,)), ((), ())), preferred_element_type=F32
    )


def parts_of(v, count):
    parts = []
    for _ in range(count):
        head = bf(v)
        parts.append(head)
        v = v - head.astype(F32)
    return parts


def mm_left(exact, v, ca=1, cb=0, count=3):
    total = None
    for part in parts_of(v, count):
        term = mm(exact, part, ca, cb)
        total = term if total is None else total + term
    return total


def mm_right(v, exact, ca=1, cb=0, count=3):
    total = None
    for part in parts_of(v, count):
        term = mm(part, exact, ca, cb)
        total = term if total is None else total + term
    return total


def sigmoid(v):
    return 1.0 / (1.0 + jnp.exp(-v))


def softplus(v):
    return jnp.maximum(v, 0.0) + jnp.log1p(jnp.exp(-jnp.abs(v)))


def spread(scalars, shape, width):
    lane = lax.broadcasted_iota(jnp.int32, shape, 1) // width
    out = jnp.zeros(shape, F32)
    for h in range(scalars.shape[0]):
        out = jnp.where(lane == h, scalars[h], out)
    return out


def kernel(
    n_tm,
    n_head,
    step_bias,
    log_rate,
    skip_gain,
    series_hbm,
    w_in_hbm,
    w_dt_hbm,
    conv_w_hbm,
    conv_b_hbm,
    norm_gain_hbm,
    w_out_hbm,
    cot_hbm,
    layer_ref,
    rows_ref,
    w_in_ref,
    w_dt_ref,
    w_out_ref,
    series,
    w_in,
    w_dt,
    conv_w,
    conv_b,
    norm_gain,
    w_out,
    cot,
    rim_in,
    dec_send,
    dec_all,
    state_send,
    state_all,
    prefix_send,
    prefix_all,
    back_send,
    back_all,
    suffix_send,
    suffix_all,
    flat_state,
    own_keep,
    norm_send,
    norm_all,
    layer_send,
    layer_all,
    grow_send,
    grow_all,
    rim2_send,
    rim2_in,
    core1_send,
    core1_in,
    y1_send,
    y1_all,
    z1_send,
    z1_all,
    core2_send,
    core2_in,
    y2_send,
    y2_all,
    z2_send,
    z2_all,
    pre_buf,
    conv_buf,
    act_buf,
    decays,
    inside_buf,
    load_sem,
    send_sem,
    recv_sem,
):
    me = lax.axis_index("tm")
    mine = lax.axis_index("head")
    core = lax.rem(me, 2)
    chip = me // 2
    at_z = lax.rem(chip, NZ)
    at_y = chip // NZ
    n_chip = n_tm // 2
    n_y = n_chip // NZ
    rows, model = series.shape
    inner = w_out.shape[1]
    heads = step_bias.shape[0]
    size = inner // heads
    per_owner = inner // n_tm
    owners_per_head = n_tm // heads
    quarter = rows // n_head
    few = model // n_tm

    barrier = pltpu.get_barrier_semaphore()

    def around(k):
        return lax.rem(me + 1 + lax.rem(k + 3 * n_tm // 8 - 1, n_tm - 1), n_tm)

    def greet(k, c):
        pl.semaphore_signal(barrier, inc=1, device_id=(around(k), mine), device_id_type=MESH)
        return c

    lax.fori_loop(0, n_tm - 1, greet, 0)
    for d in range(1, n_head):
        pl.semaphore_signal(
            barrier, inc=1, device_id=(me, lax.rem(mine + d, n_head)), device_id_type=MESH
        )
    loads = [
        pltpu.make_async_copy(src, dst, load_sem.at[k])
        for k, (src, dst) in enumerate(
            [
                (w_dt_hbm, w_dt),
                (series_hbm, series),
                (w_in_hbm, w_in),
                (conv_w_hbm, conv_w),
                (conv_b_hbm, conv_b),
                (cot_hbm, cot),
                (w_out_hbm, w_out),
                (norm_gain_hbm, norm_gain),
            ]
        )
    ]
    for load in loads:
        load.start()

    def push(src, dst, which, device):
        pltpu.make_async_remote_copy(
            src_ref=src,
            dst_ref=dst,
            send_sem=send_sem.at[which],
            recv_sem=recv_sem.at[which],
            device_id=device,
            device_id_type=MESH,
        ).start()

    def arrived(ref, which):
        pltpu.make_async_copy(ref, ref, recv_sem.at[which]).wait()

    def departed(ref, which):
        pltpu.make_async_copy(ref, ref, send_sem.at[which]).wait()

    def to_all(source_of, dst, which):
        def one(k, c):
            peer = around(k)
            push(source_of(peer), dst.at[me], which, (peer, mine))
            return c

        lax.fori_loop(0, n_tm - 1, one, 0)

    def to_heads(source_of, dst, which):
        for d in (2, 1, 3):
            peer = lax.rem(mine + d, n_head)
            push(source_of(peer), dst.at[mine], which, (me, peer))

    def chosen(width, per):
        return (
            lax.broadcasted_iota(jnp.int32, (width, heads), 0) // per
            == lax.broadcasted_iota(jnp.int32, (width, heads), 1)
        ).astype(BF16)

    rate_wide = jnp.exp(spread(log_rate, (1, inner), size))
    skip_wide = spread(skip_gain, (1, inner), size)
    row_id = lax.broadcasted_iota(jnp.int32, (rows, rows), 0)
    col_id = lax.broadcasted_iota(jnp.int32, (rows, rows), 1)
    below = col_id <= row_id
    loads[0].wait()
    w_dt_wide = bf(mm(chosen(inner, size), w_dt[...]))
    w_dt_rows = bf(mm(chosen(N, 1), w_dt[...]))
    loads[1].wait()
    step = softplus(mm(series[...], w_dt_wide, 1, 1) + spread(step_bias, (1, inner), size))
    shift_n = mm(series[...], w_dt_rows, 1, 1) + spread(step_bias, (1, N), 1)
    run = mm_left(below.astype(BF16), -step * rate_wide)
    last = run[rows - 1 : rows, :]
    for h in range(heads):
        dec_send[h] = jnp.broadcast_to(last[:, h * size : h * size + 1], (1, N))
    loads[2].wait()
    gate = bf(mm(series[...], w_in[0])).astype(F32)
    pre_buf[pl.ds(0, 8), :] = jnp.zeros((8, 2 * inner), F32)
    pre_buf[pl.ds(8, rows), :inner] = bf(mm(series[...], w_in[1])).astype(F32)
    pre_buf[pl.ds(8, rows), inner:] = bf(mm(series[...], w_in[2])).astype(F32)
    gate_sig = sigmoid(gate)
    gate_act = gate * gate_sig
    run_t = run.T
    step_t = step.T
    remain = jnp.exp(last - run)
    grow = jnp.exp(run)
    weight = remain * step

    def conv_row(k):
        return jnp.concatenate([conv_w[k, 0:1, :], conv_w[k, 1:2, :]], axis=1)

    loads[3].wait()
    loads[4].wait()

    def convolve(count):
        conv = jnp.concatenate([conv_b[0:1, :], conv_b[1:2, :]], axis=1)
        for k in range(KW):
            conv = conv + conv_row(k) * pre_buf[pl.ds(8 - (KW - 1) + k, count), :]
        conv_sig = sigmoid(conv)
        conv_buf[pl.ds(0, count), :] = conv_sig * (1.0 + conv * (1.0 - conv_sig))
        active = bf(conv * conv_sig).astype(F32)
        act_buf[pl.ds(0, count), :] = active
        return active

    active = convolve(rows)
    first = 16
    later = lax.broadcasted_iota(jnp.int32, (rows, inner), 0) >= first
    own = mm(jnp.where(later, weight * active[:, :inner], 0.0), active[:, inner : inner + N], 0, 0)
    loads[5].wait()
    loads[6].wait()
    loads[7].wait()
    gain_grad = norm_gain[...] * mm(cot[...], w_out[...])
    for h in range(heads):
        gap = run[:, h * size : h * size + 1] - run_t[h * size : h * size + 1, :]
        decays[h] = jnp.exp(jnp.where(below, gap, -1e30))

    pl.semaphore_wait(barrier, n_tm - 1 + n_head - 1)
    nxt, prv = lax.rem(me + 1, n_tm), lax.rem(me + n_tm - 1, n_tm)
    push(series.at[pl.ds(rows - 16, 16)], rim_in, RIM, (nxt, mine))
    to_all(lambda peer: dec_send.at[peer // owners_per_head], dec_all, DEC)
    dec_all[me] = dec_send[me // owners_per_head]

    arrived(rim_in, RIM)
    for s in (1, 2):
        rim = bf(mm(rim_in[...], w_in[s])).astype(F32)[8:16]
        pre_buf[pl.ds(0, 8), pl.ds((s - 1) * inner, inner)] = jnp.where(me > 0, rim, 0.0)
    active = convolve(first)
    own = own + mm(weight[:first] * active[:, :inner], active[:, inner : inner + N], 0, 0)

    def exchange(own, send, everything, out_send, out_all, which, back, reverse, during):
        flat_state[...] = own

        def pack(j, k):
            send[j] = flat_state[pl.ds(per_owner * j, per_owner), :]
            return k

        lax.fori_loop(0, n_tm, pack, 0, unroll=8)
        to_all(lambda peer: send.at[peer], everything, which)
        everything[me] = send[me]
        kept = during()
        arrived(everything.at[pl.ds(0, n_tm - 1)], which)

        def hop(k, before):
            at = n_tm - 1 - k if reverse else k
            out_send[at] = before

            @pl.when(at != me)
            def _():
                push(out_send.at[at], out_all.at[me], back, (at, mine))

            return before * jnp.exp(dec_all[at]) + everything[at]

        lax.fori_loop(0, n_tm, hop, jnp.zeros((per_owner, N), F32))
        out_all[me] = out_send[me]
        return kept

    def collect(out_all, back):
        arrived(out_all.at[pl.ds(0, n_tm - 1)], back)

        def unpack(j, k):
            flat_state[pl.ds(per_owner * j, per_owner), :] = out_all[j]
            return k

        lax.fori_loop(0, n_tm, unpack, 0, unroll=8)
        return flat_state[...]

    def by_chip(left, right, send, lanes):
        shape = (n_chip, 2, few, left.shape[1])
        left, right = left.reshape(shape), right.reshape(shape)
        for p in range(2):
            send[p, :, :, lanes] = bf(jnp.concatenate([left[:, p], right[:, p]], axis=1))

    def core_stage(send, into, which):
        push(send.at[1 - core], into, which, (me + 1 - 2 * core, mine))

    def y_stage(core_send, core_in, send, everything, which, core_which):
        arrived(core_in, core_which)
        send[...] = bf(core_send[core].astype(F32) + core_in[...].astype(F32)).reshape(send.shape)
        for d in (2, 1, 3):
            peer = lax.rem(at_y + d, n_y)
            push(
                send.at[peer],
                everything.at[at_y],
                which,
                ((peer * NZ + at_z) * 2 + core, mine),
            )

    def z_stage(y_send, y_all, send, everything, which, y_which):
        arrived(y_all.at[pl.ds(0, n_y - 1)], y_which)
        total = y_send[at_y].astype(F32)
        for d in range(1, n_y):
            total = total + y_all[lax.rem(at_y + d, n_y)].astype(F32)
        send[...] = bf(total)
        for d in (4, 3, 5, 2, 6, 1, 7):
            peer = lax.rem(at_z + d, NZ)
            push(
                send.at[peer],
                everything.at[at_z],
                which,
                ((at_y * NZ + peer) * 2 + core, mine),
            )

    def last_stage(z_send, z_all, which):
        arrived(z_all.at[pl.ds(0, NZ - 1)], which)
        total = z_send[at_z].astype(F32)
        for d in range(1, NZ):
            total = total + z_all[lax.rem(at_z + d, NZ)].astype(F32)
        return total

    own_keep[...] = own

    def intra_forward():
        x = bf(act_buf[:, :inner])
        b = bf(act_buf[:, inner : inner + N])
        c = bf(act_buf[:, inner + N :])
        scores = mm(c, b, 1, 1)
        for h in range(heads):
            at = slice(h * size, (h + 1) * size)
            mixing = scores * decays[h] * step_t[h * size : h * size + 1, :]
            inside_buf[:, at] = mm(mixing, x[:, at])
        arrived(dec_all.at[pl.ds(0, n_tm - 1)], DEC)
        return x, b, c, scores

    x, b, c, scores = exchange(
        own, state_send, state_all, prefix_send, prefix_all, SCAN1, BACK1, False, intra_forward
    )
    xw = x.astype(F32)
    start = collect(prefix_all, BACK1)

    ssm = inside_buf[...] + grow * mm(c, start, 1, 1)
    y = ssm + skip_wide * xw
    gated = y * gate_act
    ones = jnp.ones((8, inner), BF16)
    power = mm_left(ones, gated * gated, 1, 1, 2)
    cross = mm_left(ones, gated * gain_grad, 1, 1, 2)
    first_row = lax.broadcasted_iota(jnp.int32, (8, rows), 0) == 0
    norm_send[...] = jnp.where(first_row, power, cross)
    to_heads(lambda peer: norm_send, norm_all, NORM)
    norm_all[mine] = norm_send[...]
    arrived(norm_all.at[pl.ds(0, n_head - 1)], NORM)
    totals = norm_all[0]
    for p in range(1, n_head):
        totals = totals + norm_all[p]
    inv_row = lax.rsqrt(totals[0:1] / E + EPS)
    coef_row = inv_row * inv_row * inv_row * totals[1:2] / E
    inv = jnp.broadcast_to(inv_row, (inner, rows)).T
    coef = jnp.broadcast_to(coef_row, (inner, rows)).T
    grad_gated = inv * gain_grad - gated * coef
    grad_y = grad_gated * gate_act
    gy = bf(grad_y)
    grown = bf(grow * grad_y)

    def intra_backward():
        normed = bf(gated * inv * norm_gain[...])
        grad_gate = bf(grad_gated * y * (gate_sig * (1.0 + gate * (1.0 - gate_sig))))
        by_chip(
            mm(cot[...], normed, 0, 0),
            mm(series[...], grad_gate, 0, 0),
            core1_send,
            slice(None),
        )
        core_stage(core1_send, core1_in, CORE1)
        part = bf(mm(normed, w_out[...], 1, 1))
        for p in range(n_head):
            layer_send[p] = part[p * quarter : (p + 1) * quarter]
        to_heads(lambda peer: layer_send.at[peer], layer_all, LAYER)
        layer_all[mine] = layer_send[mine]
        group = jnp.zeros((rows, rows), F32)
        for h in range(heads):
            at = slice(h * size, (h + 1) * size)
            inside_buf[:, at] = mm(scores * decays[h], gy[:, at], 0, 0)
            group = group + decays[h] * mm(gy[:, at], x[:, at], 1, 1) * (
                step_t[h * size : h * size + 1, :]
            )
        grad_c = mm(group, b) + mm(grown, start)
        grad_b = mm(group, c, 0, 0)
        return grad_b, grad_c, grad_gate

    grad_b, grad_c, grad_gate = exchange(
        mm(grown, c, 0, 0),
        back_send,
        back_all,
        suffix_send,
        suffix_all,
        SCAN2,
        BACK2,
        True,
        intra_backward,
    )
    after = collect(suffix_all, BACK2)
    y_stage(core1_send, core1_in, y1_send, y1_all, ALONG_Y1, CORE1)

    back_b = inside_buf[...] + remain * mm(b, after, 1, 1)
    grad_x = skip_wide * grad_y + step * back_b
    grad_b = grad_b + mm(weight * xw, after)
    gc = jnp.concatenate([grad_x, grad_b, grad_c], axis=1) * conv_buf[...]
    pre_buf[pl.ds(0, rows), :] = gc
    rim2_send[...] = gc[0:8]
    push(rim2_send, rim2_in, RIM2, (prv, mine))

    choose = (
        lax.broadcasted_iota(jnp.int32, (inner, N), 0) // size
        == lax.broadcasted_iota(jnp.int32, (inner, N), 1)
    )
    pick = choose.astype(BF16)
    x_back = mm_right(xw * back_b, pick)
    grad_cum = mm_right(grad_y * ssm, pick) - softplus(shift_n) * x_back
    final = jnp.exp(run_t[:, rows - 1 : rows]) * start + own_keep[...]
    carried = jnp.sum(
        jnp.where(choose, jnp.sum(after * final, axis=1, keepdims=True), 0.0),
        axis=0,
        keepdims=True,
    )
    grad_log = mm_left((col_id >= row_id).astype(BF16), grad_cum) + carried
    rate_n = jnp.exp(spread(log_rate, (1, N), 1))
    grad_raw = bf((x_back - rate_n * grad_log) * sigmoid(shift_n))
    thin = mm(series[...], grad_raw, 0, 0)
    by_chip(thin, jnp.zeros_like(thin), core2_send, slice(inner, inner + N))

    arrived(rim2_in, RIM2)
    pre_buf[pl.ds(rows, 8), :] = jnp.where(me < n_tm - 1, rim2_in[...], 0.0)
    grad_pre = conv_row(0) * pre_buf[pl.ds(KW - 1, rows), :]
    for k in range(1, KW):
        grad_pre = grad_pre + conv_row(k) * pre_buf[pl.ds(KW - 1 - k, rows), :]
    grad_pre = bf(grad_pre)
    by_chip(
        mm(series[...], grad_pre[:, :inner], 0, 0),
        mm(series[...], grad_pre[:, inner:], 0, 0),
        core2_send,
        slice(0, inner),
    )
    core_stage(core2_send, core2_in, CORE2)

    grad_rows = bf(
        mm(grad_gate, w_in[0], 1, 1)
        + mm(grad_pre[:, :inner], w_in[1], 1, 1)
        + mm(grad_pre[:, inner:], w_in[2], 1, 1)
        + mm(grad_raw, w_dt_rows)
    )
    for p in range(n_head):
        grow_send[p] = grad_rows[p * quarter : (p + 1) * quarter]
    to_heads(lambda peer: grow_send.at[peer], grow_all, ROWS)
    grow_all[mine] = grow_send[mine]

    def over_heads(everything):
        total = everything[0].astype(F32)
        for p in range(1, n_head):
            total = total + everything[p].astype(F32)
        return total

    y_stage(core2_send, core2_in, y2_send, y2_all, ALONG_Y2, CORE2)
    z_stage(y1_send, y1_all, z1_send, z1_all, ALONG_Z1, ALONG_Y1)
    arrived(layer_all.at[pl.ds(0, n_head - 1)], LAYER)
    layer_ref[...] = bf(over_heads(layer_all))
    z_stage(y2_send, y2_all, z2_send, z2_all, ALONG_Z2, ALONG_Y2)
    total1 = last_stage(z1_send, z1_all, ALONG_Z1)
    w_out_ref[...] = total1[:few]
    w_in_ref[0] = total1[few:]
    arrived(grow_all.at[pl.ds(0, n_head - 1)], ROWS)
    rows_ref[...] = over_heads(grow_all)
    total2 = last_stage(z2_send, z2_all, ALONG_Z2)
    w_in_ref[1] = total2[:few, :inner]
    w_in_ref[2] = total2[few:, :inner]
    w_dt_ref[...] = total2[:few, inner:].T[:heads]

    departed(rim_in, RIM)
    departed(dec_all.at[pl.ds(0, n_tm - 1)], DEC)
    departed(state_all.at[pl.ds(0, n_tm - 1)], SCAN1)
    departed(prefix_all.at[pl.ds(0, n_tm - 1)], BACK1)
    departed(norm_all.at[pl.ds(0, n_head - 1)], NORM)
    departed(layer_all.at[pl.ds(0, n_head - 1)], LAYER)
    departed(back_all.at[pl.ds(0, n_tm - 1)], SCAN2)
    departed(suffix_all.at[pl.ds(0, n_tm - 1)], BACK2)
    departed(rim2_in, RIM2)
    departed(grow_all.at[pl.ds(0, n_head - 1)], ROWS)
    departed(core1_in, CORE1)
    departed(core2_in, CORE2)
    departed(y1_all.at[pl.ds(0, n_y - 1)], ALONG_Y1)
    departed(y2_all.at[pl.ds(0, n_y - 1)], ALONG_Y2)
    departed(z1_all.at[pl.ds(0, NZ - 1)], ALONG_Z1)
    departed(z2_all.at[pl.ds(0, NZ - 1)], ALONG_Z2)


def hand_over(*refs):
    half = len(refs) // 2
    for src, dst in zip(refs[:half], refs[half:]):
        dst[...] = src[...]


def solution(mesh):
    n_tm, n_head = mesh.shape["tm"], mesh.shape["head"]

    def body(
        series,
        in_weight,
        step_weight,
        step_bias,
        log_rate,
        conv_weight,
        conv_bias,
        skip_gain,
        norm_gain,
        out_weight,
        cotangent,
    ):
        rows, model = series.shape
        inner = out_weight.shape[1]
        heads = step_bias.shape[0]
        few = model // n_tm
        quarter = rows // n_head
        n_chip = n_tm // 2
        n_y = n_chip // NZ
        vmem = pl.BlockSpec(memory_space=pltpu.VMEM)
        smem = pl.BlockSpec(memory_space=pltpu.SMEM)
        left = pl.BlockSpec(memory_space=pl.ANY)
        arrays = (
            series,
            in_weight.transpose(1, 0, 2),
            step_weight.T,
            conv_weight,
            conv_bias,
            norm_gain.reshape(1, inner),
            out_weight,
            cotangent,
        )
        out_shape = (
            jax.ShapeDtypeStruct((quarter, model), BF16),
            jax.ShapeDtypeStruct((quarter, model), F32),
            jax.ShapeDtypeStruct((3, few, inner), F32),
            jax.ShapeDtypeStruct((heads, few), F32),
            jax.ShapeDtypeStruct((few, inner), F32),
        )

        def sums(width):
            return [
                pltpu.VMEM((2, n_chip, 2 * few, width), BF16),
                pltpu.VMEM((n_chip, 2 * few, width), BF16),
                pltpu.VMEM((n_y, NZ, 2 * few, width), BF16),
                pltpu.VMEM((n_y, NZ, 2 * few, width), BF16),
                pltpu.VMEM((NZ, 2 * few, width), BF16),
                pltpu.VMEM((NZ, 2 * few, width), BF16),
            ]

        slab = pltpu.VMEM((n_tm, inner // n_tm, N), F32)
        peers = pltpu.VMEM((n_head, quarter, model), BF16)
        results = pl.pallas_call(
            functools.partial(kernel, n_tm, n_head),
            out_shape=out_shape,
            in_specs=[smem] * 3 + [left] * len(arrays),
            out_specs=(vmem,) * 5,
            scratch_shapes=[pltpu.VMEM(a.shape, a.dtype) for a in arrays]
            + [
                pltpu.VMEM((16, model), BF16),
                pltpu.VMEM((heads, 1, N), F32),
                pltpu.VMEM((n_tm, 1, N), F32),
            ]
            + [slab] * 8
            + [
                pltpu.VMEM((inner, N), F32),
                pltpu.VMEM((inner, N), F32),
                pltpu.VMEM((8, rows), F32),
                pltpu.VMEM((n_head, 8, rows), F32),
                peers,
                peers,
                peers,
                peers,
                pltpu.VMEM((8, 2 * inner), F32),
                pltpu.VMEM((8, 2 * inner), F32),
            ]
            + sums(inner)
            + sums(inner + N)
            + [
                pltpu.VMEM((rows + 8, 2 * inner), F32),
                pltpu.VMEM((rows, 2 * inner), F32),
                pltpu.VMEM((rows, 2 * inner), F32),
                pltpu.VMEM((heads, rows, rows), F32),
                pltpu.VMEM((rows, inner), F32),
                pltpu.SemaphoreType.DMA((LOADS,)),
                pltpu.SemaphoreType.DMA((16,)),
                pltpu.SemaphoreType.DMA((16,)),
            ],
            compiler_params=pltpu.CompilerParams(collective_id=0, has_side_effects=True),
        )(step_bias, log_rate, skip_gain, *arrays)
        layer, rows_grad, w_in, w_dt, w_out = pl.pallas_call(
            hand_over,
            out_shape=out_shape,
            in_specs=[vmem] * 5,
            out_specs=(vmem,) * 5,
        )(*results)
        return (layer, rows_grad, w_in.transpose(1, 0, 2), w_dt.T, w_out)

    in_specs = (
        P("tm", None),
        P(None, None, "head"),
        P(None, "head"),
        P("head"),
        P("head"),
        P(None, None, "head"),
        P(None, "head"),
        P("head"),
        P("head"),
        P(None, "head"),
        P("tm", None),
    )
    out_specs = (
        P(("tm", "head"), None),
        P(("tm", "head"), None),
        P("tm", None, "head"),
        P("tm", "head"),
        P("tm", "head"),
    )
    return jax.shard_map(body, mesh=mesh, in_specs=in_specs, out_specs=out_specs, check_vma=False)
```

```python
import functools

import jax
import jax.numpy as jnp
from jax import lax
from jax.experimental import pallas as pl
from jax.experimental.pallas import tpu as pltpu
from jax.sharding import PartitionSpec as P

N = 128
KW = 4
E = 1024
EPS = 1e-05
MESH = pl.DeviceIdType.MESH
F32 = jnp.float32
BF16 = jnp.bfloat16

NZ = 8
ROW = 2 * NZ
RIM, DEC, SCAN1, TOTAL1, BACK1, NORM, LAYER, SCAN2, TOTAL2, BACK2 = range(10)
RIM2, RIM3, ROWS, CORE1, ALONG_Y1, ALONG_Z1, CORE2, ALONG_Y2, ALONG_Z2 = range(10, 19)
CORE3, ALONG_Y3, ALONG_Z3 = range(19, 22)
COPIES = 22
LOADS = 8


def bf(v):
    return v.astype(BF16)


def mm(a, b, ca=1, cb=0):
    return lax.dot_general(
        bf(a), bf(b), (((ca,), (cb,)), ((), ())), preferred_element_type=F32
    )


def parts_of(v, count):
    parts = []
    for _ in range(count):
        head = bf(v)
        parts.append(head)
        v = v - head.astype(F32)
    return parts


def mm_left(exact, v, ca=1, cb=0, count=3):
    total = None
    for part in parts_of(v, count):
        term = mm(exact, part, ca, cb)
        total = term if total is None else total + term
    return total


def mm_right(v, exact, ca=1, cb=0, count=3):
    total = None
    for part in parts_of(v, count):
        term = mm(part, exact, ca, cb)
        total = term if total is None else total + term
    return total


def sigmoid(v):
    return 1.0 / (1.0 + jnp.exp(-v))


def softplus(v):
    return jnp.maximum(v, 0.0) + jnp.log1p(jnp.exp(-jnp.abs(v)))


def spread(scalars, shape, width):
    lane = lax.broadcasted_iota(jnp.int32, shape, 1) // width
    out = jnp.zeros(shape, F32)
    for h in range(scalars.shape[0]):
        out = jnp.where(lane == h, scalars[h], out)
    return out


def kernel(
    n_tm,
    n_head,
    step_bias,
    log_rate,
    skip_gain,
    series_hbm,
    w_in_hbm,
    w_dt_hbm,
    conv_w_hbm,
    conv_b_hbm,
    norm_gain_hbm,
    w_out_hbm,
    cot_hbm,
    layer_ref,
    rows_ref,
    w_in_ref,
    w_dt_ref,
    w_out_ref,
    series,
    w_in,
    w_dt,
    conv_w,
    conv_b,
    norm_gain,
    w_out,
    cot,
    rim_in,
    dec_send,
    dec_all,
    state_send,
    state_all,
    total_send,
    total_all,
    prefix_send,
    prefix_all,
    back_send,
    back_all,
    rest_send,
    rest_all,
    suffix_send,
    suffix_all,
    within,
    own_keep,
    norm_send,
    norm_all,
    layer_send,
    layer_all,
    grow_send,
    grow_all,
    rim2_send,
    rim2_in,
    rim3_send,
    rim3_in,
    core1_send,
    core1_in,
    y1_send,
    y1_all,
    z1_send,
    z1_all,
    core2_send,
    core2_in,
    y2_send,
    y2_all,
    z2_send,
    z2_all,
    core3_send,
    core3_in,
    y3_send,
    y3_all,
    z3_send,
    z3_all,
    pre_buf,
    conv_buf,
    act_buf,
    decays,
    inside_buf,
    load_sem,
    send_sem,
    recv_sem,
):
    me = lax.axis_index("tm")
    mine = lax.axis_index("head")
    core = lax.rem(me, 2)
    place = lax.rem(me, ROW)
    at_z = place // 2
    at_y = me // ROW
    n_y = n_tm // ROW
    n_chip = n_tm // 2
    rows, model = series.shape
    inner = w_out.shape[1]
    heads = step_bias.shape[0]
    size = inner // heads
    per_owner = inner // ROW
    owners_per_head = ROW // heads
    quarter = rows // n_head
    few = model // n_tm
    nxt, prv = lax.rem(me + 1, n_tm), lax.rem(me + n_tm - 1, n_tm)

    barrier = pltpu.get_barrier_semaphore()
    far_first = sorted(range(1, ROW), key=lambda d: -min(d, ROW - d))
    across = (2, 1, 3)
    z_first = (4, 3, 5, 2, 6, 1, 7)
    row_peers = [at_y * ROW + lax.rem(place + d, ROW) for d in far_first]
    y_peers = [lax.rem(at_y + d, n_y) for d in across]
    z_peers = [lax.rem(at_z + d, NZ) for d in z_first]
    head_peers = [lax.rem(mine + d, n_head) for d in across]

    def greet(device):
        pl.semaphore_signal(barrier, inc=1, device_id=device, device_id_type=MESH)

    for peer in row_peers:
        greet((peer, mine))
    for peer in y_peers:
        greet((peer * ROW + place, mine))
    for peer in head_peers:
        greet((me, peer))
    greet((nxt, mine))
    greet((prv, mine))
    greeted = len(row_peers) + len(y_peers) + len(head_peers) + 2
    loads = [
        pltpu.make_async_copy(src, dst, load_sem.at[k])
        for k, (src, dst) in enumerate(
            [
                (w_dt_hbm, w_dt),
                (series_hbm, series),
                (w_in_hbm, w_in),
                (conv_w_hbm, conv_w),
                (conv_b_hbm, conv_b),
                (cot_hbm, cot),
                (w_out_hbm, w_out),
                (norm_gain_hbm, norm_gain),
            ]
        )
    ]
    for load in loads:
        load.start()

    def push(src, dst, which, device):
        pltpu.make_async_remote_copy(
            src_ref=src,
            dst_ref=dst,
            send_sem=send_sem.at[which],
            recv_sem=recv_sem.at[which],
            device_id=device,
            device_id_type=MESH,
        ).start()

    def arrived(ref, which):
        pltpu.make_async_copy(ref, ref, recv_sem.at[which]).wait()

    def departed(ref, which):
        pltpu.make_async_copy(ref, ref, send_sem.at[which]).wait()

    def to_row(source_of, dst, which):
        for peer in row_peers:
            at = lax.rem(peer, ROW)
            push(source_of(at), dst.at[place], which, (peer, mine))

    def to_heads(source_of, dst, which):
        for peer in head_peers:
            push(source_of(peer), dst.at[mine], which, (me, peer))

    def to_y(source_of, dst, which):
        for peer in y_peers:
            push(source_of(peer), dst.at[at_y], which, (peer * ROW + place, mine))

    def to_z(source_of, dst, which):
        for peer in z_peers:
            to = at_y * ROW + peer * 2 + core
            push(source_of(peer), dst.at[at_z], which, (to, mine))

    def over(first, everything, at, count):
        total = first
        for d in range(1, count):
            total = total + everything[lax.rem(at + d, count)].astype(F32)
        return total

    def chosen(width, per):
        return (
            lax.broadcasted_iota(jnp.int32, (width, heads), 0) // per
            == lax.broadcasted_iota(jnp.int32, (width, heads), 1)
        ).astype(BF16)

    rate_wide = jnp.exp(spread(log_rate, (1, inner), size))
    skip_wide = spread(skip_gain, (1, inner), size)
    row_id = lax.broadcasted_iota(jnp.int32, (rows, rows), 0)
    col_id = lax.broadcasted_iota(jnp.int32, (rows, rows), 1)
    below = col_id <= row_id
    loads[0].wait()
    w_dt_wide = bf(mm(chosen(inner, size), w_dt[...]))
    w_dt_rows = bf(mm(chosen(N, 1), w_dt[...]))
    loads[1].wait()
    step = softplus(mm(series[...], w_dt_wide, 1, 1) + spread(step_bias, (1, inner), size))
    shift_n = mm(series[...], w_dt_rows, 1, 1) + spread(step_bias, (1, N), 1)
    run = mm_left(below.astype(BF16), -step * rate_wide)
    last = run[rows - 1 : rows, :]
    for h in range(heads):
        dec_send[h] = jnp.broadcast_to(last[:, h * size : h * size + 1], (1, N))
    loads[2].wait()
    pre_buf[pl.ds(0, 8), :] = jnp.zeros((8, 2 * inner), F32)
    pre_buf[pl.ds(8, rows), :inner] = bf(mm(series[...], w_in[1])).astype(F32)
    pre_buf[pl.ds(8, rows), inner:] = bf(mm(series[...], w_in[2])).astype(F32)
    remain = jnp.exp(last - run)
    weight = remain * step

    def conv_row(k):
        return jnp.concatenate([conv_w[k, 0:1, :], conv_w[k, 1:2, :]], axis=1)

    loads[3].wait()
    loads[4].wait()

    def convolve(count):
        conv = jnp.concatenate([conv_b[0:1, :], conv_b[1:2, :]], axis=1)
        for k in range(KW):
            conv = conv + conv_row(k) * pre_buf[pl.ds(8 - (KW - 1) + k, count), :]
        conv_sig = sigmoid(conv)
        conv_buf[pl.ds(0, count), :] = conv_sig * (1.0 + conv * (1.0 - conv_sig))
        active = bf(conv * conv_sig).astype(F32)
        act_buf[pl.ds(0, count), :] = active
        return active

    active = convolve(rows)
    first = 16
    later = lax.broadcasted_iota(jnp.int32, (rows, inner), 0) >= first
    own = mm(jnp.where(later, weight * active[:, :inner], 0.0), active[:, inner : inner + N], 0, 0)

    pl.semaphore_wait(barrier, greeted)
    push(series.at[pl.ds(rows - 16, 16)], rim_in, RIM, (nxt, mine))
    to_row(lambda at: dec_send.at[at // owners_per_head], dec_all, DEC)
    dec_all[place] = dec_send[place // owners_per_head]

    arrived(rim_in, RIM)
    for s in (1, 2):
        rim = bf(mm(rim_in[...], w_in[s])).astype(F32)[8:16]
        pre_buf[pl.ds(0, 8), pl.ds((s - 1) * inner, inner)] = jnp.where(me > 0, rim, 0.0)
    active = convolve(first)
    own = own + mm(weight[:first] * active[:, :inner], active[:, inner : inner + N], 0, 0)

    def exchange(own, send, everything, totals, all_totals, out_send, out_all, which, during):
        scan, total, back = which
        reverse = scan == SCAN2
        slabs = (ROW, per_owner, N)
        send[...] = bf(own).reshape(slabs)
        to_row(lambda at: send.at[at], everything, scan)
        everything[place] = send[place]
        kept = during()
        arrived(everything.at[pl.ds(0, ROW - 1)], scan)
        order = range(ROW - 1, -1, -1) if reverse else range(ROW)
        state = jnp.zeros((per_owner, N), F32)
        log = jnp.zeros((1, N), F32)
        logs = {}
        for k in order:
            within[k] = state
            logs[k] = log
            state = state * jnp.exp(dec_all[k]) + everything[k].astype(F32)
            log = log + dec_all[k]
        totals[pl.ds(0, per_owner), :] = state
        totals[pl.ds(per_owner, 8), :] = jnp.broadcast_to(log, (8, N))
        to_y(lambda peer: totals, all_totals, total)
        all_totals[at_y] = totals[...]
        arrived(all_totals.at[pl.ds(0, n_y - 1)], total)
        outer = jnp.zeros((per_owner, N), F32)
        for k in range(n_y - 1, -1, -1) if reverse else range(n_y):
            new = outer * jnp.exp(all_totals[k, per_owner : per_owner + 1, :])
            new = new + all_totals[k, :per_owner, :]
            outer = jnp.where(k > at_y if reverse else k < at_y, new, outer)
        for k in range(ROW):
            out_send[k] = bf(within[k] + jnp.exp(logs[k]) * outer)
        to_row(lambda at: out_send.at[at], out_all, back)
        out_all[place] = out_send[place]
        return kept

    def collect(out_all, back):
        arrived(out_all.at[pl.ds(0, ROW - 1)], back)
        return out_all[...].reshape(inner, N)

    def by_chip(v, send, lanes):
        v = bf(v).reshape(n_chip, 2, few, v.shape[1])
        for p in range(2):
            send[p, :, :, lanes] = v[:, p]

    def core_stage(send, into, which):
        push(send.at[1 - core], into, which, (me + 1 - 2 * core, mine))

    def y_stage(core_send, core_in, send, everything, which, core_which):
        arrived(core_in, core_which)
        total = core_send[core].astype(F32) + core_in[...].astype(F32)
        send[...] = total.astype(send.dtype).reshape(send.shape)
        to_y(lambda peer: send.at[peer], everything, which)

    def z_stage(y_send, y_all, send, everything, which, y_which):
        arrived(y_all.at[pl.ds(0, n_y - 1)], y_which)
        send[...] = over(y_send[at_y].astype(F32), y_all, at_y, n_y).astype(send.dtype)
        to_z(lambda peer: send.at[peer], everything, which)

    def last_stage(z_send, z_all, which):
        arrived(z_all.at[pl.ds(0, NZ - 1)], which)
        return over(z_send[at_z].astype(F32), z_all, at_z, NZ)

    own_keep[...] = own

    def intra_forward():
        x = bf(act_buf[:, :inner])
        b = bf(act_buf[:, inner : inner + N])
        c = bf(act_buf[:, inner + N :])
        run_t = run.T
        step_t = step.T
        scores = mm(c, b, 1, 1)
        for h in range(heads):
            at = slice(h * size, (h + 1) * size)
            gap = run[:, h * size : h * size + 1] - run_t[h * size : h * size + 1, :]
            decay = jnp.exp(jnp.where(below, gap, -1e30))
            decays[h] = decay
            mixing = scores * decay * step_t[h * size : h * size + 1, :]
            inside_buf[:, at] = mm(mixing, x[:, at])
        gate = bf(mm(series[...], w_in[0])).astype(F32)
        gate_sig = sigmoid(gate)
        for k in (5, 6, 7):
            loads[k].wait()
        gain_grad = norm_gain[...] * mm(cot[...], w_out[...])
        arrived(dec_all.at[pl.ds(0, ROW - 1)], DEC)
        return x, b, c, scores, run_t, step_t, jnp.exp(run), gate, gate_sig, gain_grad

    x, b, c, scores, run_t, step_t, grow, gate, gate_sig, gain_grad = exchange(
        own,
        state_send,
        state_all,
        total_send,
        total_all,
        prefix_send,
        prefix_all,
        (SCAN1, TOTAL1, BACK1),
        intra_forward,
    )
    xw = x.astype(F32)
    gate_act = gate * gate_sig
    start = collect(prefix_all, BACK1)

    ssm = inside_buf[...] + grow * mm(c, start, 1, 1)
    y = ssm + skip_wide * xw
    gated = y * gate_act
    ones = jnp.ones((8, inner), BF16)
    power = mm_left(ones, gated * gated, 1, 1, 2)
    cross = mm_left(ones, gated * gain_grad, 1, 1, 2)
    first_row = lax.broadcasted_iota(jnp.int32, (8, rows), 0) == 0
    norm_send[...] = jnp.where(first_row, power, cross)
    to_heads(lambda peer: norm_send, norm_all, NORM)
    norm_all[mine] = norm_send[...]
    arrived(norm_all.at[pl.ds(0, n_head - 1)], NORM)
    totals = norm_all[0]
    for p in range(1, n_head):
        totals = totals + norm_all[p]
    inv_row = lax.rsqrt(totals[0:1] / E + EPS)
    coef_row = inv_row * inv_row * inv_row * totals[1:2] / E
    inv = jnp.broadcast_to(inv_row, (inner, rows)).T
    coef = jnp.broadcast_to(coef_row, (inner, rows)).T
    grad_gated = inv * gain_grad - gated * coef
    grad_y = grad_gated * gate_act
    gy = bf(grad_y)
    grown = bf(grow * grad_y)

    def unfold(lanes):
        def tap(k):
            return conv_row(k)[:, lanes] * pre_buf[pl.ds(KW - 1 - k, rows), lanes]

        total = tap(0)
        for k in range(1, KW):
            total = total + tap(k)
        return bf(total)

    c_lanes = slice(inner + N, 2 * inner)
    xb_lanes = slice(0, inner + N)
    is_last = me == n_tm - 1

    def intra_backward():
        group = jnp.zeros((rows, rows), F32)
        for h in range(heads):
            at = slice(h * size, (h + 1) * size)
            inside_buf[:, at] = mm(scores * decays[h], gy[:, at], 0, 0)
            group = group + decays[h] * mm(gy[:, at], x[:, at], 1, 1) * (
                step_t[h * size : h * size + 1, :]
            )
        grad_conv = (mm(group, b) + mm(grown, start)) * conv_buf[:, c_lanes]
        pre_buf[pl.ds(0, rows), c_lanes] = grad_conv
        rim3_send[...] = grad_conv[0:8]
        push(rim3_send, rim3_in, RIM3, (prv, mine))
        grad_b = mm(group, c, 0, 0)
        normed = bf(gated * inv * norm_gain[...])
        grad_gate = bf(grad_gated * y * (gate_sig * (1.0 + gate * (1.0 - gate_sig))))
        by_chip(mm(cot[...], normed, 0, 0), core1_send, slice(0, inner))
        by_chip(mm(series[...], grad_gate, 0, 0), core1_send, slice(inner, 2 * inner))
        part = bf(mm(normed, w_out[...], 1, 1))
        for p in range(n_head):
            layer_send[p] = part[p * quarter : (p + 1) * quarter]
        to_heads(lambda peer: layer_send.at[peer], layer_all, LAYER)
        layer_all[mine] = layer_send[mine]
        arrived(rim3_in, RIM3)
        pre_buf[pl.ds(rows, 8), c_lanes] = jnp.where(is_last, 0.0, rim3_in[...])
        grad_pre_c = unfold(c_lanes)
        by_chip(mm(series[...], grad_pre_c, 0, 0), core1_send, slice(2 * inner, 2 * inner + N))
        core_stage(core1_send, core1_in, CORE1)
        return grad_b, grad_gate, grad_pre_c

    grad_b, grad_gate, grad_pre_c = exchange(
        mm(grown, c, 0, 0),
        back_send,
        back_all,
        rest_send,
        rest_all,
        suffix_send,
        suffix_all,
        (SCAN2, TOTAL2, BACK2),
        intra_backward,
    )
    y_stage(core1_send, core1_in, y1_send, y1_all, ALONG_Y1, CORE1)
    after = collect(suffix_all, BACK2)

    back_b = inside_buf[...] + remain * mm(b, after, 1, 1)
    grad_x = skip_wide * grad_y + step * back_b
    grad_b = grad_b + mm(weight * xw, after)
    gc = jnp.concatenate([grad_x, grad_b], axis=1) * conv_buf[:, xb_lanes]
    pre_buf[pl.ds(0, rows), xb_lanes] = gc
    rim2_send[...] = gc[0:8]
    push(rim2_send, rim2_in, RIM2, (prv, mine))

    choose = (
        lax.broadcasted_iota(jnp.int32, (inner, N), 0) // size
        == lax.broadcasted_iota(jnp.int32, (inner, N), 1)
    )
    pick = choose.astype(BF16)
    x_back = mm_right(xw * back_b, pick)
    grad_cum = mm_right(grad_y * ssm, pick) - softplus(shift_n) * x_back
    final = jnp.exp(run_t[:, rows - 1 : rows]) * start.astype(F32) + own_keep[...]
    carried = jnp.sum(
        jnp.where(choose, jnp.sum(after.astype(F32) * final, axis=1, keepdims=True), 0.0),
        axis=0,
        keepdims=True,
    )
    grad_log = mm_left((col_id >= row_id).astype(BF16), grad_cum) + carried
    rate_n = jnp.exp(spread(log_rate, (1, N), 1))
    grad_raw = bf((x_back - rate_n * grad_log) * sigmoid(shift_n))
    thin = mm(series[...], grad_raw, 0, 0).reshape(n_y, NZ, 2, few, N)
    packed = thin[:, 0]
    for z in range(1, NZ):
        packed = packed + pltpu.roll(thin[:, z].reshape(n_y * 2 * few, N), z * ROW, 1).reshape(
            n_y, 2, few, N
        )
    for p in range(2):
        core3_send[p] = packed[:, p]
    core_stage(core3_send, core3_in, CORE3)

    arrived(rim2_in, RIM2)
    pre_buf[pl.ds(rows, 8), xb_lanes] = jnp.where(is_last, 0.0, rim2_in[...])
    grad_pre = unfold(xb_lanes)
    by_chip(mm(series[...], grad_pre, 0, 0), core2_send, slice(None))
    core_stage(core2_send, core2_in, CORE2)
    z_stage(y1_send, y1_all, z1_send, z1_all, ALONG_Z1, ALONG_Y1)

    grad_bc = jnp.concatenate([grad_pre[:, inner:], grad_pre_c], axis=1)
    grad_rows = bf(
        mm(grad_gate, w_in[0], 1, 1)
        + mm(grad_pre[:, :inner], w_in[1], 1, 1)
        + mm(grad_bc, w_in[2], 1, 1)
        + mm(grad_raw, w_dt_rows)
    )
    y_stage(core2_send, core2_in, y2_send, y2_all, ALONG_Y2, CORE2)
    y_stage(core3_send, core3_in, y3_send, y3_all, ALONG_Y3, CORE3)
    for p in range(n_head):
        grow_send[p] = grad_rows[p * quarter : (p + 1) * quarter]
    to_heads(lambda peer: grow_send.at[peer], grow_all, ROWS)
    grow_all[mine] = grow_send[mine]

    def over_heads(everything):
        total = everything[0].astype(F32)
        for p in range(1, n_head):
            total = total + everything[p].astype(F32)
        return total

    arrived(layer_all.at[pl.ds(0, n_head - 1)], LAYER)
    layer_ref[...] = bf(over_heads(layer_all))
    total1 = last_stage(z1_send, z1_all, ALONG_Z1)
    w_out_ref[...] = total1[:, :inner]
    w_in_ref[0] = total1[:, inner : 2 * inner]
    w_in_ref[2, :, N:] = total1[:, 2 * inner :]
    z_stage(y2_send, y2_all, z2_send, z2_all, ALONG_Z2, ALONG_Y2)
    arrived(y3_all.at[pl.ds(0, n_y - 1)], ALONG_Y3)
    z3_send[...] = over(y3_send[at_y], y3_all, at_y, n_y)
    to_z(lambda peer: z3_send, z3_all, ALONG_Z3)
    arrived(grow_all.at[pl.ds(0, n_head - 1)], ROWS)
    rows_ref[...] = over_heads(grow_all)
    total2 = last_stage(z2_send, z2_all, ALONG_Z2)
    w_in_ref[1] = total2[:, :inner]
    w_in_ref[2, :, :N] = total2[:, inner:]
    arrived(z3_all.at[pl.ds(0, NZ - 1)], ALONG_Z3)
    total3 = over(z3_send[...], z3_all, at_z, NZ)
    thin = total3
    for z in range(1, NZ):
        thin = jnp.where(at_z == z, pltpu.roll(total3, N - z * ROW, 1), thin)
    w_dt_ref[...] = thin.T[:heads]

    departed(rim_in, RIM)
    departed(rim2_in, RIM2)
    departed(rim3_in, RIM3)
    for ref, which in (
        (dec_all, DEC),
        (state_all, SCAN1),
        (prefix_all, BACK1),
        (back_all, SCAN2),
        (suffix_all, BACK2),
    ):
        departed(ref.at[pl.ds(0, ROW - 1)], which)
    for ref, which in ((norm_all, NORM), (layer_all, LAYER), (grow_all, ROWS)):
        departed(ref.at[pl.ds(0, n_head - 1)], which)
    for ref, which in (
        (total_all, TOTAL1),
        (rest_all, TOTAL2),
        (y1_all, ALONG_Y1),
        (y2_all, ALONG_Y2),
        (y3_all, ALONG_Y3),
    ):
        departed(ref.at[pl.ds(0, n_y - 1)], which)
    for ref, which in ((z1_all, ALONG_Z1), (z2_all, ALONG_Z2), (z3_all, ALONG_Z3)):
        departed(ref.at[pl.ds(0, NZ - 1)], which)
    departed(core1_in, CORE1)
    departed(core2_in, CORE2)
    departed(core3_in, CORE3)


def hand_over(*refs):
    half = len(refs) // 2
    for src, dst in zip(refs[:half], refs[half:]):
        dst[...] = src[...]


def solution(mesh):
    n_tm, n_head = mesh.shape["tm"], mesh.shape["head"]

    def body(
        series,
        in_weight,
        step_weight,
        step_bias,
        log_rate,
        conv_weight,
        conv_bias,
        skip_gain,
        norm_gain,
        out_weight,
        cotangent,
    ):
        rows, model = series.shape
        inner = out_weight.shape[1]
        heads = step_bias.shape[0]
        few = model // n_tm
        quarter = rows // n_head
        n_chip = n_tm // 2
        n_y = n_tm // ROW
        vmem = pl.BlockSpec(memory_space=pltpu.VMEM)
        smem = pl.BlockSpec(memory_space=pltpu.SMEM)
        left = pl.BlockSpec(memory_space=pl.ANY)
        arrays = (
            series,
            in_weight.transpose(1, 0, 2),
            step_weight.T,
            conv_weight,
            conv_bias,
            norm_gain.reshape(1, inner),
            out_weight,
            cotangent,
        )
        out_shape = (
            jax.ShapeDtypeStruct((quarter, model), BF16),
            jax.ShapeDtypeStruct((quarter, model), F32),
            jax.ShapeDtypeStruct((3, few, inner), F32),
            jax.ShapeDtypeStruct((heads, few), F32),
            jax.ShapeDtypeStruct((few, inner), F32),
        )

        def sums(width):
            return [
                pltpu.VMEM((2, n_chip, few, width), BF16),
                pltpu.VMEM((n_chip, few, width), BF16),
                pltpu.VMEM((n_y, NZ, few, width), BF16),
                pltpu.VMEM((n_y, NZ, few, width), BF16),
                pltpu.VMEM((NZ, few, width), BF16),
                pltpu.VMEM((NZ, few, width), BF16),
            ]

        per_owner = inner // ROW
        slab = pltpu.VMEM((ROW, per_owner, N), BF16)
        scan = [
            slab,
            slab,
            pltpu.VMEM((per_owner + 8, N), F32),
            pltpu.VMEM((n_y, per_owner + 8, N), F32),
            slab,
            slab,
        ]
        peers = pltpu.VMEM((n_head, quarter, model), BF16)
        results = pl.pallas_call(
            functools.partial(kernel, n_tm, n_head),
            out_shape=out_shape,
            in_specs=[smem] * 3 + [left] * len(arrays),
            out_specs=(vmem,) * 5,
            scratch_shapes=[pltpu.VMEM(a.shape, a.dtype) for a in arrays]
            + [
                pltpu.VMEM((16, model), BF16),
                pltpu.VMEM((heads, 1, N), F32),
                pltpu.VMEM((ROW, 1, N), F32),
            ]
            + scan
            + scan
            + [
                pltpu.VMEM((ROW, per_owner, N), F32),
                pltpu.VMEM((inner, N), F32),
                pltpu.VMEM((8, rows), F32),
                pltpu.VMEM((n_head, 8, rows), F32),
                peers,
                peers,
                peers,
                peers,
                pltpu.VMEM((8, inner + N), F32),
                pltpu.VMEM((8, inner + N), F32),
                pltpu.VMEM((8, N), F32),
                pltpu.VMEM((8, N), F32),
            ]
            + sums(2 * inner + N)
            + sums(inner + N)
            + [
                pltpu.VMEM((2, n_y, few, N), F32),
                pltpu.VMEM((n_y, few, N), F32),
                pltpu.VMEM((n_y, few, N), F32),
                pltpu.VMEM((n_y, few, N), F32),
                pltpu.VMEM((few, N), F32),
                pltpu.VMEM((NZ, few, N), F32),
                pltpu.VMEM((rows + 8, 2 * inner), F32),
                pltpu.VMEM((rows, 2 * inner), F32),
                pltpu.VMEM((rows, 2 * inner), F32),
                pltpu.VMEM((heads, rows, rows), F32),
                pltpu.VMEM((rows, inner), F32),
                pltpu.SemaphoreType.DMA((LOADS,)),
                pltpu.SemaphoreType.DMA((COPIES,)),
                pltpu.SemaphoreType.DMA((COPIES,)),
            ],
            compiler_params=pltpu.CompilerParams(collective_id=0, has_side_effects=True),
        )(step_bias, log_rate, skip_gain, *arrays)
        layer, rows_grad, w_in, w_dt, w_out = pl.pallas_call(
            hand_over,
            out_shape=out_shape,
            in_specs=[vmem] * 5,
            out_specs=(vmem,) * 5,
        )(*results)
        return (layer, rows_grad, w_in.transpose(1, 0, 2), w_dt.T, w_out)

    in_specs = (
        P("tm", None),
        P(None, None, "head"),
        P(None, "head"),
        P("head"),
        P("head"),
        P(None, None, "head"),
        P(None, "head"),
        P("head"),
        P("head"),
        P(None, "head"),
        P("tm", None),
    )
    out_specs = (
        P(("tm", "head"), None),
        P(("tm", "head"), None),
        P("tm", None, "head"),
        P("tm", "head"),
        P("tm", "head"),
    )
    return jax.shard_map(body, mesh=mesh, in_specs=in_specs, out_specs=out_specs, check_vma=False)
```

```python
import functools

import jax
import jax.numpy as jnp
from jax import lax
from jax.experimental import pallas as pl
from jax.experimental.pallas import tpu as pltpu
from jax.sharding import PartitionSpec as P

N = 128
KW = 4
E = 1024
EPS = 1e-05
MESH = pl.DeviceIdType.MESH
F32 = jnp.float32
BF16 = jnp.bfloat16

NZ = 8
ROW = 2 * NZ
RIM, DEC, SCAN1, TOTAL1, BACK1, NORM, LAYER, SCAN2, TOTAL2, BACK2 = range(10)
RIM2, RIM3, ROWS, CORE1, ALONG_Y1, ALONG_Z1, CORE2, ALONG_Y2, ALONG_Z2 = range(10, 19)
CORE3, ALONG_Y3, ALONG_Z3, FIRST_Z, THEN_Y = range(19, 24)
COPIES = 24
LOADS = 11


def bf(v):
    return v.astype(BF16)


def mm(a, b, ca=1, cb=0):
    return lax.dot_general(
        bf(a), bf(b), (((ca,), (cb,)), ((), ())), preferred_element_type=F32
    )


def parts_of(v, count):
    parts = []
    for _ in range(count):
        head = bf(v)
        parts.append(head)
        v = v - head.astype(F32)
    return parts


def mm_left(exact, v, ca=1, cb=0, count=3):
    total = None
    for part in parts_of(v, count):
        term = mm(exact, part, ca, cb)
        total = term if total is None else total + term
    return total


def mm_right(v, exact, ca=1, cb=0, count=3):
    total = None
    for part in parts_of(v, count):
        term = mm(part, exact, ca, cb)
        total = term if total is None else total + term
    return total


def sigmoid(v):
    return 1.0 / (1.0 + jnp.exp(-v))


def softplus(v):
    return jnp.maximum(v, 0.0) + jnp.log1p(jnp.exp(-jnp.abs(v)))


def spread(scalars, shape, width):
    lane = lax.broadcasted_iota(jnp.int32, shape, 1) // width
    out = jnp.zeros(shape, F32)
    for h in range(scalars.shape[0]):
        out = jnp.where(lane == h, scalars[h], out)
    return out


def kernel(
    n_tm,
    n_head,
    step_bias_hbm,
    log_rate_hbm,
    skip_gain_hbm,
    series_hbm,
    w_in_hbm,
    w_dt_hbm,
    conv_w_hbm,
    conv_b_hbm,
    norm_gain_hbm,
    w_out_hbm,
    cot_hbm,
    layer_ref,
    rows_ref,
    w_in_ref,
    w_dt_ref,
    w_out_ref,
    step_bias,
    log_rate,
    skip_gain,
    series,
    w_in,
    w_dt,
    conv_w,
    conv_b,
    norm_gain,
    w_out,
    cot,
    rim_in,
    dec_send,
    dec_all,
    state_send,
    state_all,
    total_send,
    total_all,
    prefix_send,
    prefix_all,
    back_send,
    back_all,
    rest_send,
    rest_all,
    suffix_send,
    suffix_all,
    within,
    own_keep,
    norm_send,
    norm_all,
    layer_send,
    layer_all,
    grow_send,
    grow_all,
    rim2_send,
    rim2_in,
    rim3_send,
    rim3_in,
    core1_send,
    core1_in,
    y1_send,
    y1_all,
    z1_send,
    z1_all,
    core2_send,
    core2_in,
    y2_send,
    y2_all,
    z2_send,
    z2_all,
    core3_send,
    core3_in,
    y3_send,
    y3_all,
    z3_send,
    z3_all,
    zb_send,
    zb_all,
    yb_send,
    yb_all,
    factors,
    pre_buf,
    conv_buf,
    act_buf,
    decays,
    inside_buf,
    load_sem,
    send_sem,
    recv_sem,
):
    me = lax.axis_index("tm")
    mine = lax.axis_index("head")
    core = lax.rem(me, 2)
    place = lax.rem(me, ROW)
    at_z = place // 2
    at_y = me // ROW
    n_y = n_tm // ROW
    n_chip = n_tm // 2
    rows, model = series.shape
    inner = w_out.shape[1]
    heads = step_bias.shape[0]
    size = inner // heads
    per_owner = inner // ROW
    owners_per_head = ROW // heads
    quarter = rows // n_head
    few = model // n_tm
    nxt, prv = lax.rem(me + 1, n_tm), lax.rem(me + n_tm - 1, n_tm)

    loads = [
        pltpu.make_async_copy(src, dst, load_sem.at[k])
        for k, (src, dst) in enumerate(
            [
                (w_dt_hbm, w_dt),
                (series_hbm, series),
                (w_in_hbm, w_in),
                (conv_w_hbm, conv_w),
                (conv_b_hbm, conv_b),
                (step_bias_hbm, step_bias),
                (log_rate_hbm, log_rate),
                (skip_gain_hbm, skip_gain),
                (cot_hbm, cot),
                (w_out_hbm, w_out),
                (norm_gain_hbm, norm_gain),
            ]
        )
    ]
    for load in loads:
        load.start()

    barrier = pltpu.get_barrier_semaphore()
    far_first = sorted(range(1, ROW), key=lambda d: -min(d, ROW - d))
    across = (2, 1, 3)
    z_first = (4, 3, 5, 2, 6, 1, 7)
    row_peers = [at_y * ROW + lax.rem(place + d, ROW) for d in far_first]
    y_peers = [lax.rem(at_y + d, n_y) for d in across]
    z_peers = [lax.rem(at_z + d, NZ) for d in z_first]
    head_peers = [lax.rem(mine + d, n_head) for d in across]

    def greet(device):
        pl.semaphore_signal(barrier, inc=1, device_id=device, device_id_type=MESH)

    for peer in row_peers:
        greet((peer, mine))
    for peer in y_peers:
        greet((peer * ROW + place, mine))
    for peer in head_peers:
        greet((me, peer))
    greet((nxt, mine))
    greet((prv, mine))
    greeted = len(row_peers) + len(y_peers) + len(head_peers) + 2
    def push(src, dst, which, device):
        pltpu.make_async_remote_copy(
            src_ref=src,
            dst_ref=dst,
            send_sem=send_sem.at[which],
            recv_sem=recv_sem.at[which],
            device_id=device,
            device_id_type=MESH,
        ).start()

    def arrived(ref, which):
        pltpu.make_async_copy(ref, ref, recv_sem.at[which]).wait()

    def departed(ref, which):
        pltpu.make_async_copy(ref, ref, send_sem.at[which]).wait()

    def to_row(source_of, dst, which):
        for peer in row_peers:
            at = lax.rem(peer, ROW)
            push(source_of(at), dst.at[place], which, (peer, mine))

    def to_heads(source_of, dst, which):
        for peer in head_peers:
            push(source_of(peer), dst.at[mine], which, (me, peer))

    def to_y(source_of, dst, which):
        for peer in y_peers:
            push(source_of(peer), dst.at[at_y], which, (peer * ROW + place, mine))

    def to_z(source_of, dst, which):
        for peer in z_peers:
            to = at_y * ROW + peer * 2 + core
            push(source_of(peer), dst.at[at_z], which, (to, mine))

    def over(first, everything, at, count):
        total = first
        for d in range(1, count):
            total = total + everything[lax.rem(at + d, count)].astype(F32)
        return total

    def chosen(width, per):
        return (
            lax.broadcasted_iota(jnp.int32, (width, heads), 0) // per
            == lax.broadcasted_iota(jnp.int32, (width, heads), 1)
        ).astype(BF16)

    for k in (5, 6, 7, 0):
        loads[k].wait()
    rate_wide = jnp.exp(spread(log_rate, (1, inner), size))
    skip_wide = spread(skip_gain, (1, inner), size)
    row_id = lax.broadcasted_iota(jnp.int32, (rows, rows), 0)
    col_id = lax.broadcasted_iota(jnp.int32, (rows, rows), 1)
    below = col_id <= row_id
    w_dt_wide = bf(mm(chosen(inner, size), w_dt[...]))
    w_dt_rows = bf(mm(chosen(N, 1), w_dt[...]))
    loads[1].wait()
    step = softplus(mm(series[...], w_dt_wide, 1, 1) + spread(step_bias, (1, inner), size))
    shift_n = mm(series[...], w_dt_rows, 1, 1) + spread(step_bias, (1, N), 1)
    run = mm_left(below.astype(BF16), -step * rate_wide)
    last = run[rows - 1 : rows, :]
    for h in range(heads):
        dec_send[h] = jnp.broadcast_to(last[:, h * size : h * size + 1], (1, N))
    loads[2].wait()
    pre_buf[pl.ds(0, 8), :] = jnp.zeros((8, 2 * inner), F32)
    pre_buf[pl.ds(8, rows), :inner] = bf(mm(series[...], w_in[1])).astype(F32)
    pre_buf[pl.ds(8, rows), inner:] = bf(mm(series[...], w_in[2])).astype(F32)
    pl.semaphore_wait(barrier, greeted)
    push(series.at[pl.ds(rows - 16, 16)], rim_in, RIM, (nxt, mine))
    to_row(lambda at: dec_send.at[at // owners_per_head], dec_all, DEC)
    dec_all[place] = dec_send[place // owners_per_head]

    remain = jnp.exp(last - run)
    weight = remain * step

    def conv_row(k):
        return jnp.concatenate([conv_w[k, 0:1, :], conv_w[k, 1:2, :]], axis=1)

    loads[3].wait()
    loads[4].wait()

    def convolve(count):
        conv = jnp.concatenate([conv_b[0:1, :], conv_b[1:2, :]], axis=1)
        for k in range(KW):
            conv = conv + conv_row(k) * pre_buf[pl.ds(8 - (KW - 1) + k, count), :]
        conv_sig = sigmoid(conv)
        conv_buf[pl.ds(0, count), :] = conv_sig * (1.0 + conv * (1.0 - conv_sig))
        active = bf(conv * conv_sig).astype(F32)
        act_buf[pl.ds(0, count), :] = active
        return active

    active = convolve(rows)
    first = 16
    later = lax.broadcasted_iota(jnp.int32, (rows, inner), 0) >= first
    own = mm(jnp.where(later, weight * active[:, :inner], 0.0), active[:, inner : inner + N], 0, 0)
    arrived(rim_in, RIM)
    for s in (1, 2):
        rim = bf(mm(rim_in[...], w_in[s])).astype(F32)[8:16]
        pre_buf[pl.ds(0, 8), pl.ds((s - 1) * inner, inner)] = jnp.where(me > 0, rim, 0.0)
    active = convolve(first)
    own = own + mm(weight[:first] * active[:, :inner], active[:, inner : inner + N], 0, 0)

    def exchange(own, send, everything, totals, all_totals, out_send, out_all, which, during):
        scan, total, back = which
        reverse = scan == SCAN2
        slabs = (ROW, per_owner, N)
        send[...] = bf(own).reshape(slabs)
        to_row(lambda at: send.at[at], everything, scan)
        everything[place] = send[place]
        kept = during()
        arrived(everything.at[pl.ds(0, ROW - 1)], scan)
        order = range(ROW - 1, -1, -1) if reverse else range(ROW)
        state = jnp.zeros((per_owner, N), F32)
        for k in order:
            within[k] = state
            state = state * factors[0, k] + everything[k].astype(F32)
        totals[pl.ds(0, per_owner), :] = state
        totals[pl.ds(per_owner, 8), :] = jnp.broadcast_to(factors[0, ROW], (8, N))
        to_y(lambda peer: totals, all_totals, total)
        all_totals[at_y] = totals[...]
        arrived(all_totals.at[pl.ds(0, n_y - 1)], total)
        outer = jnp.zeros((per_owner, N), F32)
        for k in range(n_y - 1, -1, -1) if reverse else range(n_y):
            new = outer * all_totals[k, per_owner : per_owner + 1, :]
            new = new + all_totals[k, :per_owner, :]
            outer = jnp.where(k > at_y if reverse else k < at_y, new, outer)
        for k in range(ROW):
            out_send[k] = bf(within[k] + factors[2 if reverse else 1, k] * outer)
        to_row(lambda at: out_send.at[at], out_all, back)
        out_all[place] = out_send[place]
        return kept

    def collect(out_all, back):
        arrived(out_all.at[pl.ds(0, ROW - 1)], back)
        return out_all[...].reshape(inner, N)

    def by_chip(v, send, lanes):
        v = bf(v).reshape(n_chip, 2, few, v.shape[1])
        for p in range(2):
            send[p, :, :, lanes] = v[:, p]

    def core_stage(send, into, which):
        push(send.at[1 - core], into, which, (me + 1 - 2 * core, mine))

    def y_stage(core_send, core_in, send, everything, which, core_which):
        arrived(core_in, core_which)
        total = core_send[core].astype(F32) + core_in[...].astype(F32)
        send[...] = total.astype(send.dtype).reshape(send.shape)
        to_y(lambda peer: send.at[peer], everything, which)

    def z_stage(y_send, y_all, send, everything, which, y_which):
        arrived(y_all.at[pl.ds(0, n_y - 1)], y_which)
        send[...] = over(y_send[at_y].astype(F32), y_all, at_y, n_y).astype(send.dtype)
        to_z(lambda peer: send.at[peer], everything, which)

    def last_stage(z_send, z_all, which):
        arrived(z_all.at[pl.ds(0, NZ - 1)], which)
        return over(z_send[at_z].astype(F32), z_all, at_z, NZ)

    own_keep[...] = own

    def intra_forward():
        x = bf(act_buf[:, :inner])
        b = bf(act_buf[:, inner : inner + N])
        c = bf(act_buf[:, inner + N :])
        run_t = run.T
        step_t = step.T
        scores = mm(c, b, 1, 1)
        for h in range(heads):
            at = slice(h * size, (h + 1) * size)
            gap = run[:, h * size : h * size + 1] - run_t[h * size : h * size + 1, :]
            decay = jnp.exp(jnp.where(below, gap, -1e30))
            decays[h] = decay
            mixing = scores * decay * step_t[h * size : h * size + 1, :]
            inside_buf[:, at] = mm(mixing, x[:, at])
        gate = bf(mm(series[...], w_in[0])).astype(F32)
        gate_sig = sigmoid(gate)
        for k in (8, 9, 10):
            loads[k].wait()
        gain_grad = norm_gain[...] * mm(cot[...], w_out[...])
        arrived(dec_all.at[pl.ds(0, ROW - 1)], DEC)
        for row, order in ((1, range(ROW)), (2, range(ROW - 1, -1, -1))):
            log = jnp.zeros((1, N), F32)
            for k in order:
                factors[row, k] = jnp.exp(log)
                log = log + dec_all[k]
        factors[0, ROW] = jnp.exp(log)
        for k in range(ROW):
            factors[0, k] = jnp.exp(dec_all[k])
        return x, b, c, scores, run_t, step_t, jnp.exp(run), gate, gate_sig, gain_grad

    x, b, c, scores, run_t, step_t, grow, gate, gate_sig, gain_grad = exchange(
        own,
        state_send,
        state_all,
        total_send,
        total_all,
        prefix_send,
        prefix_all,
        (SCAN1, TOTAL1, BACK1),
        intra_forward,
    )
    xw = x.astype(F32)
    gate_act = gate * gate_sig
    start = collect(prefix_all, BACK1)

    ssm = inside_buf[...] + grow * mm(c, start, 1, 1)
    y = ssm + skip_wide * xw
    gated = y * gate_act
    ones = jnp.ones((8, inner), BF16)
    power = mm_left(ones, gated * gated, 1, 1, 2)
    cross = mm_left(ones, gated * gain_grad, 1, 1, 2)
    first_row = lax.broadcasted_iota(jnp.int32, (8, rows), 0) == 0
    norm_send[...] = jnp.where(first_row, power, cross)
    to_heads(lambda peer: norm_send, norm_all, NORM)
    norm_all[mine] = norm_send[...]
    arrived(norm_all.at[pl.ds(0, n_head - 1)], NORM)
    totals = norm_all[0]
    for p in range(1, n_head):
        totals = totals + norm_all[p]
    inv_row = lax.rsqrt(totals[0:1] / E + EPS)
    coef_row = inv_row * inv_row * inv_row * totals[1:2] / E
    inv = jnp.broadcast_to(inv_row, (inner, rows)).T
    coef = jnp.broadcast_to(coef_row, (inner, rows)).T
    grad_gated = inv * gain_grad - gated * coef
    grad_y = grad_gated * gate_act
    gy = bf(grad_y)
    grown = bf(grow * grad_y)

    def unfold(lanes, at, count):
        def tap(k):
            return conv_row(k)[:, lanes] * pre_buf[pl.ds(at + KW - 1 - k, count), lanes]

        total = tap(0)
        for k in range(1, KW):
            total = total + tap(k)
        return bf(total)

    c_lanes = slice(inner + N, 2 * inner)
    xb_lanes = slice(0, inner + N)
    is_last = me == n_tm - 1

    def intra_backward():
        group = jnp.zeros((rows, rows), F32)
        for h in range(heads):
            at = slice(h * size, (h + 1) * size)
            inside_buf[:, at] = mm(scores * decays[h], gy[:, at], 0, 0)
            group = group + decays[h] * mm(gy[:, at], x[:, at], 1, 1) * (
                step_t[h * size : h * size + 1, :]
            )
        grad_conv = (mm(group, b) + mm(grown, start)) * conv_buf[:, c_lanes]
        pre_buf[pl.ds(0, rows), c_lanes] = grad_conv
        rim3_send[...] = grad_conv[0:8]
        push(rim3_send, rim3_in, RIM3, (prv, mine))
        grad_b = mm(group, c, 0, 0)
        normed = bf(gated * inv * norm_gain[...])
        grad_gate = bf(grad_gated * y * (gate_sig * (1.0 + gate * (1.0 - gate_sig))))
        by_chip(mm(cot[...], normed, 0, 0), core1_send, slice(0, inner))
        by_chip(mm(series[...], grad_gate, 0, 0), core1_send, slice(inner, 2 * inner))
        part = bf(mm(normed, w_out[...], 1, 1))
        for p in range(n_head):
            layer_send[p] = part[p * quarter : (p + 1) * quarter]
        to_heads(lambda peer: layer_send.at[peer], layer_all, LAYER)
        layer_all[mine] = layer_send[mine]
        arrived(rim3_in, RIM3)
        pre_buf[pl.ds(rows, 8), c_lanes] = jnp.where(is_last, 0.0, rim3_in[...])
        grad_pre_c = unfold(c_lanes, 0, rows)
        by_chip(mm(series[...], grad_pre_c, 0, 0), core1_send, slice(2 * inner, 2 * inner + N))
        core_stage(core1_send, core1_in, CORE1)
        return grad_b, grad_gate, grad_pre_c

    grad_b, grad_gate, grad_pre_c = exchange(
        mm(grown, c, 0, 0),
        back_send,
        back_all,
        rest_send,
        rest_all,
        suffix_send,
        suffix_all,
        (SCAN2, TOTAL2, BACK2),
        intra_backward,
    )
    y_stage(core1_send, core1_in, y1_send, y1_all, ALONG_Y1, CORE1)
    after = collect(suffix_all, BACK2)

    back_b = inside_buf[...] + remain * mm(b, after, 1, 1)
    grad_x = skip_wide * grad_y + step * back_b
    grad_b = grad_b + mm(weight * xw, after)
    gc = jnp.concatenate([grad_x, grad_b], axis=1) * conv_buf[:, xb_lanes]
    pre_buf[pl.ds(0, rows), xb_lanes] = gc
    rim2_send[...] = gc[0:8]
    push(rim2_send, rim2_in, RIM2, (prv, mine))
    main = rows - 16
    pre_main = unfold(xb_lanes, 0, main)
    deep = mm(series[:main], pre_main, 0, 0)

    choose = (
        lax.broadcasted_iota(jnp.int32, (inner, N), 0) // size
        == lax.broadcasted_iota(jnp.int32, (inner, N), 1)
    )
    pick = choose.astype(BF16)
    x_back = mm_right(xw * back_b, pick)
    grad_cum = mm_right(grad_y * ssm, pick) - softplus(shift_n) * x_back
    final = jnp.exp(run_t[:, rows - 1 : rows]) * start.astype(F32) + own_keep[...]
    carried = jnp.sum(
        jnp.where(choose, jnp.sum(after.astype(F32) * final, axis=1, keepdims=True), 0.0),
        axis=0,
        keepdims=True,
    )
    grad_log = mm_left((col_id >= row_id).astype(BF16), grad_cum) + carried
    rate_n = jnp.exp(spread(log_rate, (1, N), 1))
    grad_raw = bf((x_back - rate_n * grad_log) * sigmoid(shift_n))
    thin = mm(series[...], grad_raw, 0, 0).reshape(n_y, NZ, 2, few, N)
    packed = thin[:, 0]
    for z in range(1, NZ):
        packed = packed + pltpu.roll(thin[:, z].reshape(n_y * 2 * few, N), z * ROW, 1).reshape(
            n_y, 2, few, N
        )
    for p in range(2):
        core3_send[p] = packed[:, p]
    core_stage(core3_send, core3_in, CORE3)

    arrived(rim2_in, RIM2)
    pre_buf[pl.ds(rows, 8), xb_lanes] = jnp.where(is_last, 0.0, rim2_in[...])
    pre_rest = unfold(xb_lanes, main, 16)
    by_chip(deep + mm(series[main:], pre_rest, 0, 0), core2_send, slice(None))
    core_stage(core2_send, core2_in, CORE2)
    y_stage(core3_send, core3_in, y3_send, y3_all, ALONG_Y3, CORE3)
    z_stage(y1_send, y1_all, z1_send, z1_all, ALONG_Z1, ALONG_Y1)
    grad_pre = jnp.concatenate([pre_main, pre_rest], axis=0)

    grad_bc = jnp.concatenate([grad_pre[:, inner:], grad_pre_c], axis=1)
    grad_rows = bf(
        mm(grad_gate, w_in[0], 1, 1)
        + mm(grad_pre[:, :inner], w_in[1], 1, 1)
        + mm(grad_bc, w_in[2], 1, 1)
        + mm(grad_raw, w_dt_rows)
    )
    for p in range(n_head):
        grow_send[p] = grad_rows[p * quarter : (p + 1) * quarter]
    to_heads(lambda peer: grow_send.at[peer], grow_all, ROWS)
    grow_all[mine] = grow_send[mine]

    def over_heads(everything):
        total = everything[0].astype(F32)
        for p in range(1, n_head):
            total = total + everything[p].astype(F32)
        return total

    arrived(core2_in, CORE2)
    pair = core2_send[core].astype(F32) + core2_in[...].astype(F32)
    y2_send[...] = bf(pair[:, :, :inner]).reshape(y2_send.shape)
    to_y(lambda peer: y2_send.at[peer], y2_all, ALONG_Y2)
    thick = bf(pair[:, :, inner:]).reshape(n_y, NZ, few, N)
    for z in range(NZ):
        zb_send[z] = thick[:, z]
    to_z(lambda peer: zb_send.at[peer], zb_all, FIRST_Z)
    arrived(layer_all.at[pl.ds(0, n_head - 1)], LAYER)
    layer_ref[...] = bf(over_heads(layer_all))
    arrived(y3_all.at[pl.ds(0, n_y - 1)], ALONG_Y3)
    z3_send[...] = over(y3_send[at_y], y3_all, at_y, n_y)
    to_z(lambda peer: z3_send, z3_all, ALONG_Z3)
    z_stage(y2_send, y2_all, z2_send, z2_all, ALONG_Z2, ALONG_Y2)
    arrived(zb_all.at[pl.ds(0, NZ - 1)], FIRST_Z)
    yb_send[...] = bf(over(zb_send[at_z].astype(F32), zb_all, at_z, NZ))
    to_y(lambda peer: yb_send.at[peer], yb_all, THEN_Y)
    total1 = last_stage(z1_send, z1_all, ALONG_Z1)
    w_out_ref[...] = total1[:, :inner]
    w_in_ref[0] = total1[:, inner : 2 * inner]
    w_in_ref[2, :, N:] = total1[:, 2 * inner :]
    arrived(grow_all.at[pl.ds(0, n_head - 1)], ROWS)
    rows_ref[...] = over_heads(grow_all)
    arrived(yb_all.at[pl.ds(0, n_y - 1)], THEN_Y)
    w_in_ref[2, :, :N] = over(yb_send[at_y].astype(F32), yb_all, at_y, n_y)
    w_in_ref[1] = last_stage(z2_send, z2_all, ALONG_Z2)
    arrived(z3_all.at[pl.ds(0, NZ - 1)], ALONG_Z3)
    total3 = over(z3_send[...], z3_all, at_z, NZ)
    thin = total3
    for z in range(1, NZ):
        thin = jnp.where(at_z == z, pltpu.roll(total3, N - z * ROW, 1), thin)
    w_dt_ref[...] = thin.T[:heads]

    departed(rim_in, RIM)
    departed(rim2_in, RIM2)
    departed(rim3_in, RIM3)
    for ref, which in (
        (dec_all, DEC),
        (state_all, SCAN1),
        (prefix_all, BACK1),
        (back_all, SCAN2),
        (suffix_all, BACK2),
    ):
        departed(ref.at[pl.ds(0, ROW - 1)], which)
    for ref, which in ((norm_all, NORM), (layer_all, LAYER), (grow_all, ROWS)):
        departed(ref.at[pl.ds(0, n_head - 1)], which)
    for ref, which in (
        (total_all, TOTAL1),
        (rest_all, TOTAL2),
        (y1_all, ALONG_Y1),
        (y2_all, ALONG_Y2),
        (y3_all, ALONG_Y3),
        (yb_all, THEN_Y),
    ):
        departed(ref.at[pl.ds(0, n_y - 1)], which)
    for ref, which in (
        (z1_all, ALONG_Z1),
        (z2_all, ALONG_Z2),
        (z3_all, ALONG_Z3),
        (zb_all, FIRST_Z),
    ):
        departed(ref.at[pl.ds(0, NZ - 1)], which)
    departed(core1_in, CORE1)
    departed(core2_in, CORE2)
    departed(core3_in, CORE3)


def hand_over(*refs):
    half = len(refs) // 2
    for src, dst in zip(refs[:half], refs[half:]):
        dst[...] = src[...]


def solution(mesh):
    n_tm, n_head = mesh.shape["tm"], mesh.shape["head"]

    def body(
        series,
        in_weight,
        step_weight,
        step_bias,
        log_rate,
        conv_weight,
        conv_bias,
        skip_gain,
        norm_gain,
        out_weight,
        cotangent,
    ):
        rows, model = series.shape
        inner = out_weight.shape[1]
        heads = step_bias.shape[0]
        few = model // n_tm
        quarter = rows // n_head
        n_chip = n_tm // 2
        n_y = n_tm // ROW
        vmem = pl.BlockSpec(memory_space=pltpu.VMEM)
        left = pl.BlockSpec(memory_space=pl.ANY)
        arrays = (
            series,
            in_weight.transpose(1, 0, 2),
            step_weight.T,
            conv_weight,
            conv_bias,
            norm_gain.reshape(1, inner),
            out_weight,
            cotangent,
        )
        out_shape = (
            jax.ShapeDtypeStruct((quarter, model), BF16),
            jax.ShapeDtypeStruct((quarter, model), F32),
            jax.ShapeDtypeStruct((3, few, inner), F32),
            jax.ShapeDtypeStruct((heads, few), F32),
            jax.ShapeDtypeStruct((few, inner), F32),
        )

        def sums(width, first):
            return [
                pltpu.VMEM((2, n_chip, few, width), BF16),
                pltpu.VMEM((n_chip, few, width), BF16),
                pltpu.VMEM((n_y, NZ, few, first), BF16),
                pltpu.VMEM((n_y, NZ, few, first), BF16),
                pltpu.VMEM((NZ, few, first), BF16),
                pltpu.VMEM((NZ, few, first), BF16),
            ]

        per_owner = inner // ROW
        slab = pltpu.VMEM((ROW, per_owner, N), BF16)
        scan = [
            slab,
            slab,
            pltpu.VMEM((per_owner + 8, N), F32),
            pltpu.VMEM((n_y, per_owner + 8, N), F32),
            slab,
            slab,
        ]
        peers = pltpu.VMEM((n_head, quarter, model), BF16)
        results = pl.pallas_call(
            functools.partial(kernel, n_tm, n_head),
            out_shape=out_shape,
            in_specs=[left] * (3 + len(arrays)),
            out_specs=(vmem,) * 5,
            scratch_shapes=[pltpu.SMEM((heads,), F32)] * 3
            + [pltpu.VMEM(a.shape, a.dtype) for a in arrays]
            + [
                pltpu.VMEM((16, model), BF16),
                pltpu.VMEM((heads, 1, N), F32),
                pltpu.VMEM((ROW, 1, N), F32),
            ]
            + scan
            + scan
            + [
                pltpu.VMEM((ROW, per_owner, N), F32),
                pltpu.VMEM((inner, N), F32),
                pltpu.VMEM((8, rows), F32),
                pltpu.VMEM((n_head, 8, rows), F32),
                peers,
                peers,
                peers,
                peers,
                pltpu.VMEM((8, inner + N), F32),
                pltpu.VMEM((8, inner + N), F32),
                pltpu.VMEM((8, N), F32),
                pltpu.VMEM((8, N), F32),
            ]
            + sums(2 * inner + N, 2 * inner + N)
            + sums(inner + N, inner)
            + [
                pltpu.VMEM((2, n_y, few, N), F32),
                pltpu.VMEM((n_y, few, N), F32),
                pltpu.VMEM((n_y, few, N), F32),
                pltpu.VMEM((n_y, few, N), F32),
                pltpu.VMEM((few, N), F32),
                pltpu.VMEM((NZ, few, N), F32),
                pltpu.VMEM((NZ, n_y, few, N), BF16),
                pltpu.VMEM((NZ, n_y, few, N), BF16),
                pltpu.VMEM((n_y, few, N), BF16),
                pltpu.VMEM((n_y, few, N), BF16),
                pltpu.VMEM((3, ROW + 1, 1, N), F32),
                pltpu.VMEM((rows + 8, 2 * inner), F32),
                pltpu.VMEM((rows, 2 * inner), F32),
                pltpu.VMEM((rows, 2 * inner), F32),
                pltpu.VMEM((heads, rows, rows), F32),
                pltpu.VMEM((rows, inner), F32),
                pltpu.SemaphoreType.DMA((LOADS,)),
                pltpu.SemaphoreType.DMA((COPIES,)),
                pltpu.SemaphoreType.DMA((COPIES,)),
            ],
            compiler_params=pltpu.CompilerParams(collective_id=0, has_side_effects=True),
        )(step_bias, log_rate, skip_gain, *arrays)
        layer, rows_grad, w_in, w_dt, w_out = pl.pallas_call(
            hand_over,
            out_shape=out_shape,
            in_specs=[vmem] * 5,
            out_specs=(vmem,) * 5,
        )(*results)
        return (layer, rows_grad, w_in.transpose(1, 0, 2), w_dt.T, w_out)

    in_specs = (
        P("tm", None),
        P(None, None, "head"),
        P(None, "head"),
        P("head"),
        P("head"),
        P(None, None, "head"),
        P(None, "head"),
        P("head"),
        P("head"),
        P(None, "head"),
        P("tm", None),
    )
    out_specs = (
        P(("tm", "head"), None),
        P(("tm", "head"), None),
        P("tm", None, "head"),
        P("tm", "head"),
        P("tm", "head"),
    )
    return jax.shard_map(body, mesh=mesh, in_specs=in_specs, out_specs=out_specs, check_vma=False)
```

```python
import functools

import jax
import jax.numpy as jnp
from jax import lax
from jax.experimental import pallas as pl
from jax.experimental.pallas import tpu as pltpu
from jax.sharding import PartitionSpec as P

N = 128
KW = 4
E = 1024
EPS = 1e-05
MESH = pl.DeviceIdType.MESH
F32 = jnp.float32
BF16 = jnp.bfloat16

NZ = 8
ROW = 2 * NZ
RIM, DEC, SCAN1, TOTAL1, BACK1, NORM, LAYER, SCAN2, TOTAL2, BACK2 = range(10)
RIM2, RIM3, ROWS, CORE1, ALONG_Y1, ALONG_Z1, CORE2, ALONG_Y2, ALONG_Z2 = range(10, 19)
CORE3, ALONG_Y3, ALONG_Z3, FIRST_Z, THEN_Y, FACTOR, RIM_ROWS = range(19, 26)
COPIES = 26
LOADS = 11
STORES = 7


def bf(v):
    return v.astype(BF16)


def mm(a, b, ca=1, cb=0):
    return lax.dot_general(
        bf(a), bf(b), (((ca,), (cb,)), ((), ())), preferred_element_type=F32
    )


def parts_of(v, count):
    parts = []
    for _ in range(count):
        head = bf(v)
        parts.append(head)
        v = v - head.astype(F32)
    return parts


def mm_left(exact, v, ca=1, cb=0, count=3):
    total = None
    for part in parts_of(v, count):
        term = mm(exact, part, ca, cb)
        total = term if total is None else total + term
    return total


def mm_right(v, exact, ca=1, cb=0, count=3):
    total = None
    for part in parts_of(v, count):
        term = mm(part, exact, ca, cb)
        total = term if total is None else total + term
    return total


def sigmoid(v):
    return 1.0 / (1.0 + jnp.exp(-v))


def softplus(v):
    return jnp.maximum(v, 0.0) + jnp.log1p(jnp.exp(-jnp.abs(v)))


def spread(scalars, shape, width):
    lane = lax.broadcasted_iota(jnp.int32, shape, 1) // width
    out = jnp.zeros(shape, F32)
    for h in range(scalars.shape[0]):
        out = jnp.where(lane == h, scalars[h], out)
    return out


def kernel(
    n_tm,
    n_head,
    step_bias_hbm,
    log_rate_hbm,
    skip_gain_hbm,
    series_hbm,
    w_in_hbm,
    w_dt_hbm,
    conv_w_hbm,
    conv_b_hbm,
    norm_gain_hbm,
    w_out_hbm,
    cot_hbm,
    layer_out,
    rows_out,
    w_in_out,
    w_dt_out,
    w_out_out,
    layer_ref,
    rows_ref,
    w_in_ref,
    w_dt_ref,
    w_out_ref,
    step_bias,
    log_rate,
    skip_gain,
    series,
    w_in,
    w_dt,
    conv_w,
    conv_b,
    norm_gain,
    w_out,
    cot,
    rim_in,
    rim_send,
    rim_pre,
    dec_send,
    dec_all,
    state_send,
    state_all,
    total_send,
    total_all,
    prefix_send,
    prefix_all,
    back_send,
    back_all,
    rest_send,
    rest_all,
    suffix_send,
    suffix_all,
    within,
    own_keep,
    norm_send,
    norm_all,
    layer_send,
    layer_all,
    grow_send,
    grow_all,
    rim2_send,
    rim2_in,
    rim3_send,
    rim3_in,
    core1_send,
    core1_in,
    y1_send,
    y1_all,
    z1_send,
    z1_all,
    core2_send,
    core2_in,
    y2_send,
    y2_all,
    z2_send,
    z2_all,
    core3_send,
    core3_in,
    y3_send,
    y3_all,
    z3_send,
    z3_all,
    zb_send,
    zb_all,
    yb_send,
    yb_all,
    factors,
    row_factor_send,
    row_factor,
    pre_buf,
    conv_buf,
    act_buf,
    decays,
    inside_buf,
    gc_buf,
    load_sem,
    store_sem,
    send_sem,
    recv_sem,
):
    me = lax.axis_index("tm")
    mine = lax.axis_index("head")
    core = lax.rem(me, 2)
    place = lax.rem(me, ROW)
    at_z = place // 2
    at_y = me // ROW
    n_y = n_tm // ROW
    n_chip = n_tm // 2
    rows, model = series.shape
    inner = w_out.shape[1]
    heads = step_bias.shape[0]
    size = inner // heads
    per_owner = inner // ROW
    owners_per_head = ROW // heads
    quarter = rows // n_head
    few = model // n_tm
    nxt, prv = lax.rem(me + 1, n_tm), lax.rem(me + n_tm - 1, n_tm)

    loads = [
        pltpu.make_async_copy(src, dst, load_sem.at[k])
        for k, (src, dst) in enumerate(
            [
                (w_dt_hbm, w_dt),
                (series_hbm, series),
                (w_in_hbm, w_in),
                (conv_w_hbm, conv_w),
                (conv_b_hbm, conv_b),
                (step_bias_hbm, step_bias),
                (log_rate_hbm, log_rate),
                (skip_gain_hbm, skip_gain),
                (cot_hbm, cot),
                (w_out_hbm, w_out),
                (norm_gain_hbm, norm_gain),
            ]
        )
    ]
    for load in loads:
        load.start()

    barrier = pltpu.get_barrier_semaphore()
    far_first = sorted(range(1, ROW), key=lambda d: -min(d, ROW - d))
    across = (2, 1, 3)
    z_first = (4, 3, 5, 2, 6, 1, 7)
    row_peers = [at_y * ROW + lax.rem(place + d, ROW) for d in far_first]
    y_peers = [lax.rem(at_y + d, n_y) for d in across]
    z_peers = [lax.rem(at_z + d, NZ) for d in z_first]
    head_peers = [lax.rem(mine + d, n_head) for d in across]

    def greet(device):
        pl.semaphore_signal(barrier, inc=1, device_id=device, device_id_type=MESH)

    for peer in row_peers:
        greet((peer, mine))
    for peer in y_peers:
        greet((peer * ROW + place, mine))
    for peer in head_peers:
        greet((me, peer))
    greet((nxt, mine))
    greet((prv, mine))
    greeted = len(row_peers) + len(y_peers) + len(head_peers) + 2
    def push(src, dst, which, device):
        pltpu.make_async_remote_copy(
            src_ref=src,
            dst_ref=dst,
            send_sem=send_sem.at[which],
            recv_sem=recv_sem.at[which],
            device_id=device,
            device_id_type=MESH,
        ).start()

    def arrived(ref, which):
        pltpu.make_async_copy(ref, ref, recv_sem.at[which]).wait()

    def departed(ref, which):
        pltpu.make_async_copy(ref, ref, send_sem.at[which]).wait()

    def to_row(source_of, dst, which):
        for peer in row_peers:
            at = lax.rem(peer, ROW)
            push(source_of(at), dst.at[place], which, (peer, mine))

    def to_heads(source_of, dst, which):
        for peer in head_peers:
            push(source_of(peer), dst.at[mine], which, (me, peer))

    def to_y(source_of, dst, which):
        for peer in y_peers:
            push(source_of(peer), dst.at[at_y], which, (peer * ROW + place, mine))

    def to_z(source_of, dst, which):
        for peer in z_peers:
            to = at_y * ROW + peer * 2 + core
            push(source_of(peer), dst.at[at_z], which, (to, mine))

    def over(first, everything, at, count):
        total = first
        for d in range(1, count):
            total = total + everything[lax.rem(at + d, count)].astype(F32)
        return total

    def chosen(width, per):
        return (
            lax.broadcasted_iota(jnp.int32, (width, heads), 0) // per
            == lax.broadcasted_iota(jnp.int32, (width, heads), 1)
        ).astype(BF16)

    for k in (5, 6, 7, 0):
        loads[k].wait()
    rate_wide = jnp.exp(spread(log_rate, (1, inner), size))
    skip_wide = spread(skip_gain, (1, inner), size)
    row_id = lax.broadcasted_iota(jnp.int32, (rows, rows), 0)
    col_id = lax.broadcasted_iota(jnp.int32, (rows, rows), 1)
    below = col_id <= row_id
    w_dt_wide = bf(mm(chosen(inner, size), w_dt[...]))
    w_dt_rows = bf(mm(chosen(N, 1), w_dt[...]))
    loads[1].wait()
    step = softplus(mm(series[...], w_dt_wide, 1, 1) + spread(step_bias, (1, inner), size))
    shift_n = mm(series[...], w_dt_rows, 1, 1) + spread(step_bias, (1, N), 1)
    run = mm_left(below.astype(BF16), -step * rate_wide)
    last = run[rows - 1 : rows, :]
    for h in range(heads):
        dec_send[h] = jnp.broadcast_to(last[:, h * size : h * size + 1], (1, N))
    loads[2].wait()
    pre_buf[pl.ds(0, 8), :] = jnp.zeros((8, 2 * inner), F32)
    pre_buf[pl.ds(8, rows), :inner] = bf(mm(series[...], w_in[1])).astype(F32)
    pre_buf[pl.ds(8, rows), inner:] = bf(mm(series[...], w_in[2])).astype(F32)
    rim_send[...] = bf(pre_buf[pl.ds(rows, 8), :])

    pl.semaphore_wait(barrier, greeted)
    push(rim_send, rim_pre, RIM, (nxt, mine))
    push(series.at[pl.ds(rows - 16, 16)], rim_in, RIM_ROWS, (nxt, mine))
    to_row(lambda at: dec_send.at[at // owners_per_head], dec_all, DEC)
    dec_all[place] = dec_send[place // owners_per_head]

    remain = jnp.exp(last - run)
    weight = remain * step

    def conv_row(k):
        return jnp.concatenate([conv_w[k, 0:1, :], conv_w[k, 1:2, :]], axis=1)

    loads[3].wait()
    loads[4].wait()

    def convolve(count):
        conv = jnp.concatenate([conv_b[0:1, :], conv_b[1:2, :]], axis=1)
        for k in range(KW):
            conv = conv + conv_row(k) * pre_buf[pl.ds(8 - (KW - 1) + k, count), :]
        conv_sig = sigmoid(conv)
        conv_buf[pl.ds(0, count), :] = conv_sig * (1.0 + conv * (1.0 - conv_sig))
        active = bf(conv * conv_sig).astype(F32)
        act_buf[pl.ds(0, count), :] = active
        return active

    active = convolve(rows)
    first = 16
    later = lax.broadcasted_iota(jnp.int32, (rows, inner), 0) >= first
    own = mm(jnp.where(later, weight * active[:, :inner], 0.0), active[:, inner : inner + N], 0, 0)
    arrived(rim_pre, RIM)
    pre_buf[pl.ds(0, 8), :] = jnp.where(me > 0, rim_pre[...].astype(F32), 0.0)
    active = convolve(first)
    own = own + mm(weight[:first] * active[:, :inner], active[:, inner : inner + N], 0, 0)

    def exchange(own, send, everything, totals, all_totals, out_send, out_all, which, during):
        scan, total, back = which
        reverse = scan == SCAN2
        slabs = (ROW, per_owner, N)
        send[...] = bf(own).reshape(slabs)
        to_row(lambda at: send.at[at], everything, scan)
        everything[place] = send[place]
        kept = during()
        arrived(everything.at[pl.ds(0, ROW - 1)], scan)
        order = range(ROW - 1, -1, -1) if reverse else range(ROW)
        state = jnp.zeros((per_owner, N), F32)
        for k in order:
            within[k] = state
            state = state * factors[0, k] + everything[k].astype(F32)
        totals[...] = bf(state)
        to_y(lambda peer: totals, all_totals, total)
        all_totals[at_y] = totals[...]
        if not reverse:
            arrived(row_factor.at[pl.ds(0, n_y - 1)], FACTOR)
        arrived(all_totals.at[pl.ds(0, n_y - 1)], total)
        outer = jnp.zeros((per_owner, N), F32)
        for k in range(n_y - 1, -1, -1) if reverse else range(n_y):
            new = outer * row_factor[k] + all_totals[k].astype(F32)
            outer = jnp.where(k > at_y if reverse else k < at_y, new, outer)
        for k in range(ROW):
            out_send[k] = bf(within[k] + factors[2 if reverse else 1, k] * outer)
        to_row(lambda at: out_send.at[at], out_all, back)
        out_all[place] = out_send[place]
        return kept

    def collect(out_all, back):
        arrived(out_all.at[pl.ds(0, ROW - 1)], back)
        return out_all[...].reshape(inner, N)

    def by_chip(v, send, lanes):
        v = bf(v).reshape(n_chip, 2, few, v.shape[1])
        for p in range(2):
            send[p, :, :, lanes] = v[:, p]

    def core_stage(send, into, which):
        push(send.at[1 - core], into, which, (me + 1 - 2 * core, mine))

    def y_stage(core_send, core_in, send, everything, which, core_which):
        arrived(core_in, core_which)
        total = core_send[core].astype(F32) + core_in[...].astype(F32)
        send[...] = total.astype(send.dtype).reshape(send.shape)
        to_y(lambda peer: send.at[peer], everything, which)

    def z_stage(y_send, y_all, send, everything, which, y_which):
        arrived(y_all.at[pl.ds(0, n_y - 1)], y_which)
        send[...] = over(y_send[at_y].astype(F32), y_all, at_y, n_y).astype(send.dtype)
        to_z(lambda peer: send.at[peer], everything, which)

    def last_stage(z_send, z_all, which):
        arrived(z_all.at[pl.ds(0, NZ - 1)], which)
        return over(z_send[at_z].astype(F32), z_all, at_z, NZ)

    own_keep[...] = own

    def intra_forward():
        x = bf(act_buf[:, :inner])
        b = bf(act_buf[:, inner : inner + N])
        c = bf(act_buf[:, inner + N :])
        run_t = run.T
        step_t = step.T
        scores = mm(c, b, 1, 1)
        for h in range(heads):
            at = slice(h * size, (h + 1) * size)
            gap = run[:, h * size : h * size + 1] - run_t[h * size : h * size + 1, :]
            decay = jnp.exp(jnp.where(below, gap, -1e30))
            decays[h] = decay
            mixing = scores * decay * step_t[h * size : h * size + 1, :]
            inside_buf[:, at] = mm(mixing, x[:, at])
        gate = bf(mm(series[...], w_in[0])).astype(F32)
        gate_sig = sigmoid(gate)
        for k in (8, 9, 10):
            loads[k].wait()
        gain_grad = norm_gain[...] * mm(cot[...], w_out[...])
        arrived(rim_in, RIM_ROWS)
        arrived(dec_all.at[pl.ds(0, ROW - 1)], DEC)
        for row, order in ((1, range(ROW)), (2, range(ROW - 1, -1, -1))):
            log = jnp.zeros((1, N), F32)
            for k in order:
                factors[row, k] = jnp.exp(log)
                log = log + dec_all[k]
        row_factor_send[...] = jnp.exp(log)
        to_y(lambda peer: row_factor_send, row_factor, FACTOR)
        row_factor[at_y] = row_factor_send[...]
        for k in range(ROW):
            factors[0, k] = jnp.exp(dec_all[k])
        return x, b, c, scores, run_t, step_t, jnp.exp(run), gate, gate_sig, gain_grad

    x, b, c, scores, run_t, step_t, grow, gate, gate_sig, gain_grad = exchange(
        own,
        state_send,
        state_all,
        total_send,
        total_all,
        prefix_send,
        prefix_all,
        (SCAN1, TOTAL1, BACK1),
        intra_forward,
    )
    xw = x.astype(F32)
    gate_act = gate * gate_sig
    start = collect(prefix_all, BACK1)

    ssm = inside_buf[...] + grow * mm(c, start, 1, 1)
    y = ssm + skip_wide * xw
    gated = y * gate_act
    ones = jnp.ones((8, inner), BF16)
    power = mm(ones, gated * gated, 1, 1)
    cross = mm(ones, gated * gain_grad, 1, 1)
    norm_send[0:1, :] = power[0:1]
    norm_send[1:2, :] = cross[0:1]
    to_heads(lambda peer: norm_send, norm_all, NORM)
    norm_all[mine] = norm_send[...]
    arrived(norm_all.at[pl.ds(0, n_head - 1)], NORM)
    totals = norm_all[0]
    for p in range(1, n_head):
        totals = totals + norm_all[p]
    inv_row = lax.rsqrt(totals[0:1] / E + EPS)
    coef_row = inv_row * inv_row * inv_row * totals[1:2] / E
    inv = jnp.broadcast_to(inv_row, (inner, rows)).T
    coef = jnp.broadcast_to(coef_row, (inner, rows)).T
    grad_gated = inv * gain_grad - gated * coef
    grad_y = grad_gated * gate_act
    gy = bf(grad_y)
    grown = bf(grow * grad_y)

    def unfold(lanes, at, count):
        def tap(k):
            return conv_row(k)[:, lanes] * pre_buf[pl.ds(at + KW - 1 - k, count), lanes]

        total = tap(0)
        for k in range(1, KW):
            total = total + tap(k)
        return bf(total)

    c_lanes = slice(inner + N, 2 * inner)
    xb_lanes = slice(0, inner + N)
    is_last = me == n_tm - 1

    choose = (
        lax.broadcasted_iota(jnp.int32, (inner, N), 0) // size
        == lax.broadcasted_iota(jnp.int32, (inner, N), 1)
    )
    pick = choose.astype(BF16)
    rate_n = jnp.exp(spread(log_rate, (1, N), 1))

    def intra_backward():
        group = jnp.zeros((rows, rows), F32)
        for h in range(heads):
            at = slice(h * size, (h + 1) * size)
            inside_buf[:, at] = mm(scores * decays[h], gy[:, at], 0, 0)
            group = group + decays[h] * mm(gy[:, at], x[:, at], 1, 1) * (
                step_t[h * size : h * size + 1, :]
            )
        grad_conv = (mm(group, b) + mm(grown, start)) * conv_buf[:, c_lanes]
        pre_buf[pl.ds(0, rows), c_lanes] = grad_conv
        rim3_send[...] = grad_conv[0:8]
        push(rim3_send, rim3_in, RIM3, (prv, mine))
        grad_b = mm(group, c, 0, 0)
        normed = bf(gated * inv * norm_gain[...])
        grad_gate = bf(grad_gated * y * (gate_sig * (1.0 + gate * (1.0 - gate_sig))))
        by_chip(mm(cot[...], normed, 0, 0), core1_send, slice(0, inner))
        by_chip(mm(series[...], grad_gate, 0, 0), core1_send, slice(inner, 2 * inner))
        part = bf(mm(normed, w_out[...], 1, 1))
        for p in range(n_head):
            layer_send[p] = part[p * quarter : (p + 1) * quarter]
        to_heads(lambda peer: layer_send.at[peer], layer_all, LAYER)
        layer_all[mine] = layer_send[mine]
        arrived(rim3_in, RIM3)
        pre_buf[pl.ds(rows, 8), c_lanes] = jnp.where(is_last, 0.0, rim3_in[...])
        grad_pre_c = unfold(c_lanes, 0, rows)
        by_chip(mm(series[...], grad_pre_c, 0, 0), core1_send, slice(2 * inner, 2 * inner + N))
        core_stage(core1_send, core1_in, CORE1)
        along_y = mm_right(grad_y * ssm, pick, 1, 0, 2)
        final = jnp.exp(run_t[:, rows - 1 : rows]) * start.astype(F32) + own_keep[...]
        return grad_b, grad_gate, grad_pre_c, along_y, softplus(shift_n), sigmoid(shift_n), final

    grad_b, grad_gate, grad_pre_c, along_y, step_n, slope_n, final = exchange(
        mm(grown, c, 0, 0),
        back_send,
        back_all,
        rest_send,
        rest_all,
        suffix_send,
        suffix_all,
        (SCAN2, TOTAL2, BACK2),
        intra_backward,
    )
    y_stage(core1_send, core1_in, y1_send, y1_all, ALONG_Y1, CORE1)
    after = collect(suffix_all, BACK2)

    back_b = inside_buf[...] + remain * mm(b, after, 1, 1)
    grad_x = skip_wide * grad_y + step * back_b
    grad_b = grad_b + mm(weight * xw, after)
    gc = jnp.concatenate([grad_x, grad_b], axis=1) * conv_buf[:, xb_lanes]
    rim2_send[...] = gc[0:8]
    push(rim2_send, rim2_in, RIM2, (prv, mine))
    gc_buf[pl.ds(0, 16), :] = jnp.zeros((16, inner + N), F32)
    gc_buf[pl.ds(16, rows), :] = gc
    gc_buf[pl.ds(16 + rows, 8), :] = jnp.zeros((8, inner + N), F32)

    def unfold_own(at, count):
        total = conv_row(0)[:, xb_lanes] * gc_buf[pl.ds(at + KW - 1, count), :]
        for k in range(1, KW):
            tap = conv_row(k)[:, xb_lanes] * gc_buf[pl.ds(at + KW - 1 - k, count), :]
            total = total + tap
        return bf(total)

    before = unfold_own(0, 16)
    before = jnp.where(me > 0, before, jnp.zeros_like(before))
    pre_own = unfold_own(16, rows)
    by_chip(mm(series[...], pre_own, 0, 0) + mm(rim_in[...], before, 0, 0), core2_send, slice(None))
    core_stage(core2_send, core2_in, CORE2)

    x_back = mm_right(xw * back_b, pick, 1, 0, 2)
    grad_cum = along_y - step_n * x_back
    carried = jnp.sum(
        jnp.where(choose, jnp.sum(after.astype(F32) * final, axis=1, keepdims=True), 0.0),
        axis=0,
        keepdims=True,
    )
    grad_log = mm_left((col_id >= row_id).astype(BF16), grad_cum, 1, 0, 2) + carried
    grad_raw = bf((x_back - rate_n * grad_log) * slope_n)
    thin = mm(series[...], grad_raw, 0, 0).reshape(n_y, NZ, 2, few, N)
    packed = thin[:, 0]
    for z in range(1, NZ):
        packed = packed + pltpu.roll(thin[:, z].reshape(n_y * 2 * few, N), z * ROW, 1).reshape(
            n_y, 2, few, N
        )
    for p in range(2):
        core3_send[p] = packed[:, p]
    core_stage(core3_send, core3_in, CORE3)

    arrived(core2_in, CORE2)
    pair = core2_send[core].astype(F32) + core2_in[...].astype(F32)
    y2_send[...] = bf(pair[:, :, :inner]).reshape(y2_send.shape)
    to_y(lambda peer: y2_send.at[peer], y2_all, ALONG_Y2)
    thick = bf(pair[:, :, inner:]).reshape(n_y, NZ, few, N)
    for z in range(NZ):
        zb_send[z] = thick[:, z]
    to_z(lambda peer: zb_send.at[peer], zb_all, FIRST_Z)
    z_stage(y1_send, y1_all, z1_send, z1_all, ALONG_Z1, ALONG_Y1)
    y_stage(core3_send, core3_in, y3_send, y3_all, ALONG_Y3, CORE3)

    arrived(rim2_in, RIM2)
    gc_buf[pl.ds(16 + rows, 8), :] = jnp.where(is_last, 0.0, rim2_in[...])
    main = rows - 16
    grad_pre = jnp.concatenate([pre_own[:main], unfold_own(rows, 16)], axis=0)
    grad_bc = jnp.concatenate([grad_pre[:, inner:], grad_pre_c], axis=1)
    grad_rows = bf(
        mm(grad_gate, w_in[0], 1, 1)
        + mm(grad_pre[:, :inner], w_in[1], 1, 1)
        + mm(grad_bc, w_in[2], 1, 1)
        + mm(grad_raw, w_dt_rows)
    )
    for p in range(n_head):
        grow_send[p] = grad_rows[p * quarter : (p + 1) * quarter]
    to_heads(lambda peer: grow_send.at[peer], grow_all, ROWS)
    grow_all[mine] = grow_send[mine]

    stores = []

    def store(src, dst):
        copy = pltpu.make_async_copy(src, dst, store_sem.at[len(stores)])
        copy.start()
        stores.append(copy)

    def over_heads(everything):
        total = everything[0].astype(F32)
        for p in range(1, n_head):
            total = total + everything[p].astype(F32)
        return total

    z_stage(y2_send, y2_all, z2_send, z2_all, ALONG_Z2, ALONG_Y2)
    arrived(y3_all.at[pl.ds(0, n_y - 1)], ALONG_Y3)
    z3_send[...] = over(y3_send[at_y], y3_all, at_y, n_y)
    to_z(lambda peer: z3_send, z3_all, ALONG_Z3)
    arrived(zb_all.at[pl.ds(0, NZ - 1)], FIRST_Z)
    yb_send[...] = bf(over(zb_send[at_z].astype(F32), zb_all, at_z, NZ))
    to_y(lambda peer: yb_send.at[peer], yb_all, THEN_Y)
    arrived(layer_all.at[pl.ds(0, n_head - 1)], LAYER)
    layer_ref[...] = bf(over_heads(layer_all))
    store(layer_ref, layer_out)
    total1 = last_stage(z1_send, z1_all, ALONG_Z1)
    w_out_ref[...] = total1[:, :inner]
    w_in_ref[0] = total1[:, inner : 2 * inner]
    store(w_out_ref, w_out_out)
    store(w_in_ref.at[0], w_in_out.at[0])
    w_in_ref[2, :, N:] = total1[:, 2 * inner :]
    arrived(grow_all.at[pl.ds(0, n_head - 1)], ROWS)
    rows_ref[...] = over_heads(grow_all)
    store(rows_ref, rows_out)
    w_in_ref[1] = last_stage(z2_send, z2_all, ALONG_Z2)
    store(w_in_ref.at[1], w_in_out.at[1])
    arrived(z3_all.at[pl.ds(0, NZ - 1)], ALONG_Z3)
    total3 = over(z3_send[...], z3_all, at_z, NZ)
    thin = total3
    for z in range(1, NZ):
        thin = jnp.where(at_z == z, pltpu.roll(total3, N - z * ROW, 1), thin)
    w_dt_ref[...] = thin.T[:heads]
    store(w_dt_ref, w_dt_out)
    arrived(yb_all.at[pl.ds(0, n_y - 1)], THEN_Y)
    w_in_ref[2, :, :N] = over(yb_send[at_y].astype(F32), yb_all, at_y, n_y)
    store(w_in_ref.at[2], w_in_out.at[2])

    departed(rim_pre, RIM)
    departed(rim_in, RIM_ROWS)
    departed(rim2_in, RIM2)
    departed(rim3_in, RIM3)
    for ref, which in (
        (dec_all, DEC),
        (state_all, SCAN1),
        (prefix_all, BACK1),
        (back_all, SCAN2),
        (suffix_all, BACK2),
    ):
        departed(ref.at[pl.ds(0, ROW - 1)], which)
    for ref, which in ((norm_all, NORM), (layer_all, LAYER), (grow_all, ROWS)):
        departed(ref.at[pl.ds(0, n_head - 1)], which)
    for ref, which in (
        (total_all, TOTAL1),
        (rest_all, TOTAL2),
        (y1_all, ALONG_Y1),
        (y2_all, ALONG_Y2),
        (y3_all, ALONG_Y3),
        (yb_all, THEN_Y),
        (row_factor, FACTOR),
    ):
        departed(ref.at[pl.ds(0, n_y - 1)], which)
    for ref, which in (
        (z1_all, ALONG_Z1),
        (z2_all, ALONG_Z2),
        (z3_all, ALONG_Z3),
        (zb_all, FIRST_Z),
    ):
        departed(ref.at[pl.ds(0, NZ - 1)], which)
    departed(core1_in, CORE1)
    departed(core2_in, CORE2)
    departed(core3_in, CORE3)
    for copy in stores:
        copy.wait()


def hand_over(*refs):
    given, results, held, sems = refs[:5], refs[5:10], refs[10:15], refs[15]
    loads = [pltpu.make_async_copy(given[k], held[k], sems.at[0, k]) for k in range(5)]
    stores = [pltpu.make_async_copy(held[k], results[k], sems.at[1, k]) for k in range(5)]
    for load in loads:
        load.start()
    for load, store in zip(loads, stores):
        load.wait()
        store.start()
    for store in stores:
        store.wait()


def solution(mesh):
    n_tm, n_head = mesh.shape["tm"], mesh.shape["head"]

    def body(
        series,
        in_weight,
        step_weight,
        step_bias,
        log_rate,
        conv_weight,
        conv_bias,
        skip_gain,
        norm_gain,
        out_weight,
        cotangent,
    ):
        rows, model = series.shape
        inner = out_weight.shape[1]
        heads = step_bias.shape[0]
        few = model // n_tm
        quarter = rows // n_head
        n_chip = n_tm // 2
        n_y = n_tm // ROW
        left = pl.BlockSpec(memory_space=pl.ANY)
        arrays = (
            series,
            in_weight.transpose(1, 0, 2),
            step_weight.T,
            conv_weight,
            conv_bias,
            norm_gain.reshape(1, inner),
            out_weight,
            cotangent,
        )
        out_shape = (
            jax.ShapeDtypeStruct((quarter, model), BF16),
            jax.ShapeDtypeStruct((quarter, model), F32),
            jax.ShapeDtypeStruct((3, few, inner), F32),
            jax.ShapeDtypeStruct((heads, few), F32),
            jax.ShapeDtypeStruct((few, inner), F32),
        )

        def sums(width, first):
            return [
                pltpu.VMEM((2, n_chip, few, width), BF16),
                pltpu.VMEM((n_chip, few, width), BF16),
                pltpu.VMEM((n_y, NZ, few, first), BF16),
                pltpu.VMEM((n_y, NZ, few, first), BF16),
                pltpu.VMEM((NZ, few, first), BF16),
                pltpu.VMEM((NZ, few, first), BF16),
            ]

        per_owner = inner // ROW
        slab = pltpu.VMEM((ROW, per_owner, N), BF16)
        scan = [
            slab,
            slab,
            pltpu.VMEM((per_owner, N), BF16),
            pltpu.VMEM((n_y, per_owner, N), BF16),
            slab,
            slab,
        ]
        peers = pltpu.VMEM((n_head, quarter, model), BF16)
        results = pl.pallas_call(
            functools.partial(kernel, n_tm, n_head),
            out_shape=out_shape,
            in_specs=[left] * (3 + len(arrays)),
            out_specs=(left,) * 5,
            scratch_shapes=[pltpu.VMEM(o.shape, o.dtype) for o in out_shape]
            + [pltpu.SMEM((heads,), F32)] * 3
            + [pltpu.VMEM(a.shape, a.dtype) for a in arrays]
            + [
                pltpu.VMEM((16, model), BF16),
                pltpu.VMEM((8, 2 * inner), BF16),
                pltpu.VMEM((8, 2 * inner), BF16),
                pltpu.VMEM((heads, 1, N), F32),
                pltpu.VMEM((ROW, 1, N), F32),
            ]
            + scan
            + scan
            + [
                pltpu.VMEM((ROW, per_owner, N), F32),
                pltpu.VMEM((inner, N), F32),
                pltpu.VMEM((2, rows), F32),
                pltpu.VMEM((n_head, 2, rows), F32),
                peers,
                peers,
                peers,
                peers,
                pltpu.VMEM((8, inner + N), F32),
                pltpu.VMEM((8, inner + N), F32),
                pltpu.VMEM((8, N), F32),
                pltpu.VMEM((8, N), F32),
            ]
            + sums(2 * inner + N, 2 * inner + N)
            + sums(inner + N, inner)
            + [
                pltpu.VMEM((2, n_y, few, N), F32),
                pltpu.VMEM((n_y, few, N), F32),
                pltpu.VMEM((n_y, few, N), F32),
                pltpu.VMEM((n_y, few, N), F32),
                pltpu.VMEM((few, N), F32),
                pltpu.VMEM((NZ, few, N), F32),
                pltpu.VMEM((NZ, n_y, few, N), BF16),
                pltpu.VMEM((NZ, n_y, few, N), BF16),
                pltpu.VMEM((n_y, few, N), BF16),
                pltpu.VMEM((n_y, few, N), BF16),
                pltpu.VMEM((3, ROW, 1, N), F32),
                pltpu.VMEM((1, N), F32),
                pltpu.VMEM((n_y, 1, N), F32),
                pltpu.VMEM((rows + 8, 2 * inner), F32),
                pltpu.VMEM((rows, 2 * inner), F32),
                pltpu.VMEM((rows, 2 * inner), F32),
                pltpu.VMEM((heads, rows, rows), F32),
                pltpu.VMEM((rows, inner), F32),
                pltpu.VMEM((rows + 24, inner + N), F32),
                pltpu.SemaphoreType.DMA((LOADS,)),
                pltpu.SemaphoreType.DMA((STORES,)),
                pltpu.SemaphoreType.DMA((COPIES,)),
                pltpu.SemaphoreType.DMA((COPIES,)),
            ],
            compiler_params=pltpu.CompilerParams(collective_id=0, has_side_effects=True),
        )(step_bias, log_rate, skip_gain, *arrays)
        layer, rows_grad, w_in, w_dt, w_out = pl.pallas_call(
            hand_over,
            out_shape=out_shape,
            in_specs=[left] * 5,
            out_specs=(left,) * 5,
            scratch_shapes=[pltpu.VMEM(o.shape, o.dtype) for o in out_shape]
            + [pltpu.SemaphoreType.DMA((2, 5))],
        )(*results)
        return (layer, rows_grad, w_in.transpose(1, 0, 2), w_dt.T, w_out)

    in_specs = (
        P("tm", None),
        P(None, None, "head"),
        P(None, "head"),
        P("head"),
        P("head"),
        P(None, None, "head"),
        P(None, "head"),
        P("head"),
        P("head"),
        P(None, "head"),
        P("tm", None),
    )
    out_specs = (
        P(("tm", "head"), None),
        P(("tm", "head"), None),
        P("tm", None, "head"),
        P("tm", "head"),
        P("tm", "head"),
    )
    return jax.shard_map(body, mesh=mesh, in_specs=in_specs, out_specs=out_specs, check_vma=False)
```

```python
import functools

import jax
import jax.numpy as jnp
from jax import lax
from jax.experimental import pallas as pl
from jax.experimental.pallas import tpu as pltpu
from jax.sharding import PartitionSpec as P

N = 128
KW = 4
E = 1024
EPS = 1e-05
MESH = pl.DeviceIdType.MESH
F32 = jnp.float32
BF16 = jnp.bfloat16

NZ = 8
ROW = 2 * NZ
RIM, DEC, SCAN1, TOTAL1, BACK1, NORM, LAYER, SCAN2, TOTAL2, BACK2 = range(10)
RIM2, RIM3, ROWS, CORE1, ALONG_Y1, ALONG_Z1, CORE2, ALONG_Y2, ALONG_Z2 = range(10, 19)
CORE3, ALONG_Y3, ALONG_Z3, FIRST_Z, THEN_Y, FACTOR, RIM_ROWS, ALONG_Y4, ALONG_Z4 = range(19, 28)
COPIES = 28
LOADS = 6
BIAS, RATE, SKIP, GAIN, CONV_B = range(5)
W_DT = CONV_B + 2
GRANT = 56200000


def bf(v):
    return v.astype(BF16)


def mm(a, b, ca=1, cb=0):
    return lax.dot_general(
        bf(a), bf(b), (((ca,), (cb,)), ((), ())), preferred_element_type=F32
    )


def parts_of(v, count):
    parts = []
    for _ in range(count):
        head = bf(v)
        parts.append(head)
        v = v - head.astype(F32)
    return parts


def mm_left(exact, v, ca=1, cb=0, count=3):
    total = None
    for part in parts_of(v, count):
        term = mm(exact, part, ca, cb)
        total = term if total is None else total + term
    return total


def mm_right(v, exact, ca=1, cb=0, count=3):
    total = None
    for part in parts_of(v, count):
        term = mm(part, exact, ca, cb)
        total = term if total is None else total + term
    return total


def sigmoid(v):
    return 1.0 / (1.0 + jnp.exp(-v))


def softplus(v):
    return jnp.maximum(v, 0.0) + jnp.log1p(jnp.exp(-jnp.abs(v)))


def spread(row, heads, shape, width):
    lane = lax.broadcasted_iota(jnp.int32, shape, 1) // width
    out = jnp.zeros(shape, F32)
    for h in range(heads):
        out = jnp.where(lane == h, row[:, h : h + 1], out)
    return out


def kernel(
    n_tm,
    n_head,
    small_hbm,
    series_hbm,
    w_in_hbm,
    conv_w_hbm,
    w_out_hbm,
    cot_hbm,
    layer_ref,
    rows_ref,
    w_in_ref,
    w_dt_ref,
    w_out_ref,
    small,
    series,
    w_in,
    conv_w,
    w_out,
    cot,
    rim_in,
    rim_send,
    rim_pre,
    dec_send,
    dec_all,
    state_send,
    state_all,
    total_send,
    total_all,
    prefix_send,
    prefix_all,
    back_send,
    back_all,
    rest_send,
    rest_all,
    suffix_send,
    suffix_all,
    within,
    own_keep,
    norm_send,
    norm_all,
    layer_send,
    layer_all,
    grow_send,
    grow_all,
    rim2_send,
    rim2_in,
    rim3_send,
    rim3_in,
    core1_send,
    core1_in,
    y1_send,
    y1_all,
    z1_send,
    z1_all,
    core2_send,
    core2_in,
    y2_send,
    y2_all,
    z2_send,
    z2_all,
    y4_send,
    y4_all,
    z4_send,
    z4_all,
    core3_send,
    core3_in,
    y3_send,
    y3_all,
    z3_send,
    z3_all,
    zb_send,
    zb_all,
    yb_send,
    yb_all,
    factors,
    row_factor_send,
    row_factor,
    pre_buf,
    conv_buf,
    act_buf,
    decays,
    inside_buf,
    gc_buf,
    load_sem,
    send_sem,
    recv_sem,
):
    me = lax.axis_index("tm")
    mine = lax.axis_index("head")
    core = lax.rem(me, 2)
    place = lax.rem(me, ROW)
    at_z = place // 2
    at_y = me // ROW
    n_y = n_tm // ROW
    n_chip = n_tm // 2
    rows, model = series.shape
    inner = w_out.shape[1]
    heads = w_dt_ref.shape[0]
    size = inner // heads
    per_owner = inner // ROW
    owners_per_head = ROW // heads
    quarter = rows // n_head
    few = model // n_tm
    nxt, prv = lax.rem(me + 1, n_tm), lax.rem(me + n_tm - 1, n_tm)

    loads = [
        pltpu.make_async_copy(src, dst, load_sem.at[k])
        for k, (src, dst) in enumerate(
            [
                (small_hbm, small),
                (series_hbm, series),
                (w_in_hbm, w_in),
                (conv_w_hbm, conv_w),
                (cot_hbm, cot),
                (w_out_hbm, w_out),
            ]
        )
    ]
    for load in loads:
        load.start()

    barrier = pltpu.get_barrier_semaphore()
    far_first = sorted(range(1, ROW), key=lambda d: -min(d, ROW - d))
    across = (2, 1, 3)
    z_first = (4, 3, 5, 2, 6, 1, 7)
    row_peers = [at_y * ROW + lax.rem(place + d, ROW) for d in far_first]
    y_peers = [lax.rem(at_y + d, n_y) for d in across]
    z_peers = [lax.rem(at_z + d, NZ) for d in z_first]
    head_peers = [lax.rem(mine + d, n_head) for d in across]

    def greet(device):
        pl.semaphore_signal(barrier, inc=1, device_id=device, device_id_type=MESH)

    for peer in row_peers:
        greet((peer, mine))
    for peer in y_peers:
        greet((peer * ROW + place, mine))
    for peer in head_peers:
        greet((me, peer))
    greet((nxt, mine))
    greet((prv, mine))
    greeted = len(row_peers) + len(y_peers) + len(head_peers) + 2
    def push(src, dst, which, device):
        pltpu.make_async_remote_copy(
            src_ref=src,
            dst_ref=dst,
            send_sem=send_sem.at[which],
            recv_sem=recv_sem.at[which],
            device_id=device,
            device_id_type=MESH,
        ).start()

    def arrived(ref, which):
        pltpu.make_async_copy(ref, ref, recv_sem.at[which]).wait()

    def departed(ref, which):
        pltpu.make_async_copy(ref, ref, send_sem.at[which]).wait()

    def to_row(source_of, dst, which):
        for peer in row_peers:
            at = lax.rem(peer, ROW)
            push(source_of(at), dst.at[place], which, (peer, mine))

    def to_heads(source_of, dst, which):
        for peer in head_peers:
            push(source_of(peer), dst.at[mine], which, (me, peer))

    def to_y(source_of, dst, which):
        for peer in y_peers:
            push(source_of(peer), dst.at[at_y], which, (peer * ROW + place, mine))

    def to_z(source_of, dst, which):
        for peer in z_peers:
            to = at_y * ROW + peer * 2 + core
            push(source_of(peer), dst.at[at_z], which, (to, mine))

    def over(first, everything, at, count):
        total = first
        for d in range(1, count):
            total = total + everything[lax.rem(at + d, count)].astype(F32)
        return total

    def chosen(width, per):
        return (
            lax.broadcasted_iota(jnp.int32, (width, heads), 0) // per
            == lax.broadcasted_iota(jnp.int32, (width, heads), 1)
        ).astype(BF16)

    for k in (0, 3):
        loads[k].wait()
    rate_wide = jnp.exp(spread(small[RATE : RATE + 1, :N], heads, (1, inner), size))
    skip_wide = spread(small[SKIP : SKIP + 1, :N], heads, (1, inner), size)
    row_id = lax.broadcasted_iota(jnp.int32, (rows, rows), 0)
    col_id = lax.broadcasted_iota(jnp.int32, (rows, rows), 1)
    below = col_id <= row_id
    w_dt = small[W_DT : W_DT + heads, :]
    w_dt_wide = bf(mm(chosen(inner, size), w_dt))
    w_dt_rows = bf(mm(chosen(N, 1), w_dt))
    loads[1].wait()
    step = softplus(mm(series[...], w_dt_wide, 1, 1) + spread(small[BIAS : BIAS + 1, :N], heads, (1, inner), size))
    shift_n = mm(series[...], w_dt_rows, 1, 1) + spread(small[BIAS : BIAS + 1, :N], heads, (1, N), 1)
    run = mm_left(below.astype(BF16), -step * rate_wide)
    last = run[rows - 1 : rows, :]
    for h in range(heads):
        dec_send[h] = jnp.broadcast_to(last[:, h * size : h * size + 1], (1, N))
    loads[2].wait()
    pre_buf[pl.ds(0, 8), :] = jnp.zeros((8, 2 * inner), F32)
    pre_buf[pl.ds(8, rows), :inner] = bf(mm(series[...], w_in[1])).astype(F32)
    pre_buf[pl.ds(8, rows), inner:] = bf(mm(series[...], w_in[2])).astype(F32)
    rim_send[...] = bf(pre_buf[pl.ds(rows, 8), :])

    pl.semaphore_wait(barrier, greeted)
    push(rim_send, rim_pre, RIM, (nxt, mine))
    push(series.at[pl.ds(rows - 16, 16)], rim_in, RIM_ROWS, (nxt, mine))
    to_row(lambda at: dec_send.at[at // owners_per_head], dec_all, DEC)
    dec_all[place] = dec_send[place // owners_per_head]

    remain = jnp.exp(last - run)
    weight = remain * step

    def conv_row(k):
        return jnp.concatenate([conv_w[0, k, 0:1, :], conv_w[0, k, 1:2, :]], axis=1)


    def convolve(count):
        conv = jnp.concatenate([small[CONV_B : CONV_B + 1, :inner], small[CONV_B + 1 : CONV_B + 2, :inner]], axis=1)
        for k in range(KW):
            conv = conv + conv_row(k) * pre_buf[pl.ds(8 - (KW - 1) + k, count), :]
        conv_sig = sigmoid(conv)
        conv_buf[pl.ds(0, count), :] = conv_sig * (1.0 + conv * (1.0 - conv_sig))
        active = bf(conv * conv_sig).astype(F32)
        act_buf[pl.ds(0, count), :] = active
        return active

    active = convolve(rows)
    first = 16
    later = lax.broadcasted_iota(jnp.int32, (rows, inner), 0) >= first
    own = mm(jnp.where(later, weight * active[:, :inner], 0.0), active[:, inner : inner + N], 0, 0)
    arrived(rim_pre, RIM)
    pre_buf[pl.ds(0, 8), :] = jnp.where(me > 0, rim_pre[...].astype(F32), 0.0)
    active = convolve(first)
    own = own + mm(weight[:first] * active[:, :inner], active[:, inner : inner + N], 0, 0)

    def exchange(own, send, everything, totals, all_totals, out_send, out_all, which, during):
        scan, total, back = which
        reverse = scan == SCAN2
        slabs = (ROW, per_owner, N)
        send[...] = bf(own).reshape(slabs)
        to_row(lambda at: send.at[at], everything, scan)
        everything[place] = send[place]
        kept = during()
        arrived(everything.at[pl.ds(0, ROW - 1)], scan)
        terms = [
            factors[1 if reverse else 2, k] * everything[k].astype(F32) for k in range(ROW)
        ]
        while len(terms) > 1:
            terms = [terms[k] + terms[k + 1] for k in range(0, len(terms), 2)]
        totals[...] = bf(terms[0])
        to_y(lambda peer: totals, all_totals, total)
        all_totals[at_y] = totals[...]
        state = jnp.zeros((per_owner, N), F32)
        for k in range(ROW - 1, -1, -1) if reverse else range(ROW):
            within[k] = state
            state = state * factors[0, k] + everything[k].astype(F32)
        if not reverse:
            arrived(row_factor.at[pl.ds(0, n_y - 1)], FACTOR)
        arrived(all_totals.at[pl.ds(0, n_y - 1)], total)
        outer = jnp.zeros((per_owner, N), F32)
        for k in range(n_y - 1, -1, -1) if reverse else range(n_y):
            new = outer * row_factor[k] + all_totals[k].astype(F32)
            outer = jnp.where(k > at_y if reverse else k < at_y, new, outer)
        def finished(at):
            return bf(within[at] + factors[2 if reverse else 1, at] * outer)

        for peer in row_peers:
            at = lax.rem(peer, ROW)
            out_send[at] = finished(at)
            push(out_send.at[at], out_all.at[place], back, (peer, mine))
        out_all[place] = finished(place)
        return kept

    def collect(out_all, back):
        arrived(out_all.at[pl.ds(0, ROW - 1)], back)
        return out_all[...].reshape(inner, N)

    def by_chip(v, send, lanes):
        v = bf(v).reshape(n_chip, 2, few, v.shape[1])
        for p in range(2):
            send[p, :, :, lanes] = v[:, p]

    def core_stage(send, into, which):
        push(send.at[1 - core], into, which, (me + 1 - 2 * core, mine))

    def y_stage(core_send, core_in, send, everything, which, core_which):
        arrived(core_in, core_which)
        total = core_send[core].astype(F32) + core_in[...].astype(F32)
        send[...] = total.astype(send.dtype).reshape(send.shape)
        to_y(lambda peer: send.at[peer], everything, which)

    def z_stage(y_send, y_all, send, everything, which, y_which):
        arrived(y_all.at[pl.ds(0, n_y - 1)], y_which)
        send[...] = over(y_send[at_y].astype(F32), y_all, at_y, n_y).astype(send.dtype)
        to_z(lambda peer: send.at[peer], everything, which)

    def last_stage(z_send, z_all, which):
        arrived(z_all.at[pl.ds(0, NZ - 1)], which)
        return over(z_send[at_z].astype(F32), z_all, at_z, NZ)

    own_keep[...] = own

    def intra_forward():
        x = bf(act_buf[:, :inner])
        b = bf(act_buf[:, inner : inner + N])
        c = bf(act_buf[:, inner + N :])
        run_t = run.T
        step_t = step.T
        scores = mm(c, b, 1, 1)
        for h in range(heads):
            at = slice(h * size, (h + 1) * size)
            gap = run[:, h * size : h * size + 1] - run_t[h * size : h * size + 1, :]
            decay = jnp.exp(jnp.where(below, gap, -1e30))
            decays[h] = decay
            mixing = scores * decay * step_t[h * size : h * size + 1, :]
            inside_buf[:, at] = mm(mixing, x[:, at])
        gate = bf(mm(series[...], w_in[0])).astype(F32)
        gate_sig = sigmoid(gate)
        for k in (4, 5):
            loads[k].wait()
        gain_grad = small[GAIN : GAIN + 1, :inner] * mm(cot[...], w_out[...])
        arrived(rim_in, RIM_ROWS)
        arrived(dec_all.at[pl.ds(0, ROW - 1)], DEC)
        for row, order in ((1, range(ROW)), (2, range(ROW - 1, -1, -1))):
            log = jnp.zeros((1, N), F32)
            for k in order:
                factors[row, k] = jnp.exp(log)
                log = log + dec_all[k]
        row_factor_send[...] = jnp.exp(log)
        to_y(lambda peer: row_factor_send, row_factor, FACTOR)
        row_factor[at_y] = row_factor_send[...]
        for k in range(ROW):
            factors[0, k] = jnp.exp(dec_all[k])
        return x, b, c, scores, run_t, step_t, jnp.exp(run), gate, gate_sig, gain_grad

    x, b, c, scores, run_t, step_t, grow, gate, gate_sig, gain_grad = exchange(
        own,
        state_send,
        state_all,
        total_send,
        total_all,
        prefix_send,
        prefix_all,
        (SCAN1, TOTAL1, BACK1),
        intra_forward,
    )
    xw = x.astype(F32)
    gate_act = gate * gate_sig
    start = collect(prefix_all, BACK1)

    ssm = inside_buf[...] + grow * mm(c, start, 1, 1)
    y = ssm + skip_wide * xw
    gated = y * gate_act
    ones = jnp.ones((8, inner), BF16)
    power = mm(ones, gated * gated, 1, 1)
    cross = mm(ones, gated * gain_grad, 1, 1)
    norm_send[0:1, :] = power[0:1]
    norm_send[1:2, :] = cross[0:1]
    to_heads(lambda peer: norm_send, norm_all, NORM)
    norm_all[mine] = norm_send[...]
    arrived(norm_all.at[pl.ds(0, n_head - 1)], NORM)
    totals = norm_all[0]
    for p in range(1, n_head):
        totals = totals + norm_all[p]
    inv_row = lax.rsqrt(totals[0:1] / E + EPS)
    coef_row = inv_row * inv_row * inv_row * totals[1:2] / E
    inv = jnp.broadcast_to(inv_row, (inner, rows)).T
    coef = jnp.broadcast_to(coef_row, (inner, rows)).T
    grad_gated = inv * gain_grad - gated * coef
    grad_y = grad_gated * gate_act
    gy = bf(grad_y)
    grown = bf(grow * grad_y)

    def unfold(lanes, at, count):
        def tap(k):
            return conv_row(k)[:, lanes] * pre_buf[pl.ds(at + KW - 1 - k, count), lanes]

        total = tap(0)
        for k in range(1, KW):
            total = total + tap(k)
        return bf(total)

    c_lanes = slice(inner + N, 2 * inner)
    xb_lanes = slice(0, inner + N)
    is_last = me == n_tm - 1

    choose = (
        lax.broadcasted_iota(jnp.int32, (inner, N), 0) // size
        == lax.broadcasted_iota(jnp.int32, (inner, N), 1)
    )
    pick = choose.astype(BF16)
    rate_n = jnp.exp(spread(small[RATE : RATE + 1, :N], heads, (1, N), 1))

    def intra_backward():
        group = jnp.zeros((rows, rows), F32)
        for h in range(heads):
            at = slice(h * size, (h + 1) * size)
            inside_buf[:, at] = mm(scores * decays[h], gy[:, at], 0, 0)
            group = group + decays[h] * mm(gy[:, at], x[:, at], 1, 1) * (
                step_t[h * size : h * size + 1, :]
            )
        grad_conv = (mm(group, b) + mm(grown, start)) * conv_buf[:, c_lanes]
        pre_buf[pl.ds(0, rows), c_lanes] = grad_conv
        rim3_send[...] = grad_conv[0:8]
        push(rim3_send, rim3_in, RIM3, (prv, mine))
        grad_b = mm(group, c, 0, 0)
        normed = bf(gated * inv * small[GAIN : GAIN + 1, :inner])
        grad_gate = bf(grad_gated * y * (gate_sig * (1.0 + gate * (1.0 - gate_sig))))
        by_chip(mm(cot[...], normed, 0, 0), core1_send, slice(0, inner))
        by_chip(mm(series[...], grad_gate, 0, 0), core1_send, slice(inner, 2 * inner))
        part = bf(mm(normed, w_out[...], 1, 1))
        for p in range(n_head):
            layer_send[p] = part[p * quarter : (p + 1) * quarter]
        to_heads(lambda peer: layer_send.at[peer], layer_all, LAYER)
        layer_all[mine] = layer_send[mine]
        arrived(rim3_in, RIM3)
        pre_buf[pl.ds(rows, 8), c_lanes] = jnp.where(is_last, 0.0, rim3_in[...])
        grad_pre_c = unfold(c_lanes, 0, rows)
        by_chip(mm(series[...], grad_pre_c, 0, 0), core1_send, slice(2 * inner, 2 * inner + N))
        core_stage(core1_send, core1_in, CORE1)
        along_y = mm_right(grad_y * ssm, pick, 1, 0, 2)
        final = jnp.exp(run_t[:, rows - 1 : rows]) * start.astype(F32) + own_keep[...]
        return grad_b, grad_gate, grad_pre_c, along_y, softplus(shift_n), sigmoid(shift_n), final

    grad_b, grad_gate, grad_pre_c, along_y, step_n, slope_n, final = exchange(
        mm(grown, c, 0, 0),
        back_send,
        back_all,
        rest_send,
        rest_all,
        suffix_send,
        suffix_all,
        (SCAN2, TOTAL2, BACK2),
        intra_backward,
    )
    y_stage(core1_send, core1_in, y1_send, y1_all, ALONG_Y1, CORE1)
    after = collect(suffix_all, BACK2)

    back_b = inside_buf[...] + remain * mm(b, after, 1, 1)
    grad_x = skip_wide * grad_y + step * back_b
    grad_b = grad_b + mm(weight * xw, after)
    gc = jnp.concatenate([grad_x, grad_b], axis=1) * conv_buf[:, xb_lanes]
    rim2_send[...] = gc[0:8]
    push(rim2_send, rim2_in, RIM2, (prv, mine))
    gc_buf[pl.ds(0, 16), :] = jnp.zeros((16, inner + N), F32)
    gc_buf[pl.ds(16, rows), :] = gc
    gc_buf[pl.ds(16 + rows, 8), :] = jnp.zeros((8, inner + N), F32)

    def unfold_own(at, count):
        total = conv_row(0)[:, xb_lanes] * gc_buf[pl.ds(at + KW - 1, count), :]
        for k in range(1, KW):
            tap = conv_row(k)[:, xb_lanes] * gc_buf[pl.ds(at + KW - 1 - k, count), :]
            total = total + tap
        return bf(total)

    before = unfold_own(0, 16)
    before = jnp.where(me > 0, before, jnp.zeros_like(before))
    pre_own = unfold_own(16, rows)
    by_chip(mm(series[...], pre_own, 0, 0) + mm(rim_in[...], before, 0, 0), core2_send, slice(None))
    core_stage(core2_send, core2_in, CORE2)

    x_back = mm_right(xw * back_b, pick, 1, 0, 2)
    grad_cum = along_y - step_n * x_back
    carried = jnp.sum(
        jnp.where(choose, jnp.sum(after.astype(F32) * final, axis=1, keepdims=True), 0.0),
        axis=0,
        keepdims=True,
    )
    grad_log = mm_left((col_id >= row_id).astype(BF16), grad_cum, 1, 0, 2) + carried
    grad_raw = bf((x_back - rate_n * grad_log) * slope_n)
    thin = mm(series[...], grad_raw, 0, 0).reshape(n_y, NZ, 2, few, N)
    packed = thin[:, 0]
    for z in range(1, NZ):
        packed = packed + pltpu.roll(thin[:, z].reshape(n_y * 2 * few, N), z * ROW, 1).reshape(
            n_y, 2, few, N
        )
    for p in range(2):
        core3_send[p] = packed[:, p]
    core_stage(core3_send, core3_in, CORE3)

    arrived(core2_in, CORE2)
    pair = core2_send[core].astype(F32) + core2_in[...].astype(F32)
    half = inner // 2
    y2_send[...] = bf(pair[:, :, :half]).reshape(y2_send.shape)
    to_y(lambda peer: y2_send.at[peer], y2_all, ALONG_Y2)
    y4_send[...] = bf(pair[:, :, half:inner]).reshape(y4_send.shape)
    to_y(lambda peer: y4_send.at[peer], y4_all, ALONG_Y4)
    thick = bf(pair[:, :, inner:]).reshape(n_y, NZ, few, N)
    for z in range(NZ):
        zb_send[z] = thick[:, z]
    to_z(lambda peer: zb_send.at[peer], zb_all, FIRST_Z)
    z_stage(y1_send, y1_all, z1_send, z1_all, ALONG_Z1, ALONG_Y1)
    y_stage(core3_send, core3_in, y3_send, y3_all, ALONG_Y3, CORE3)

    arrived(rim2_in, RIM2)
    gc_buf[pl.ds(16 + rows, 8), :] = jnp.where(is_last, 0.0, rim2_in[...])
    main = rows - 16
    grad_pre = jnp.concatenate([pre_own[:main], unfold_own(rows, 16)], axis=0)
    grad_bc = jnp.concatenate([grad_pre[:, inner:], grad_pre_c], axis=1)
    grad_rows = bf(
        mm(grad_gate, w_in[0], 1, 1)
        + mm(grad_pre[:, :inner], w_in[1], 1, 1)
        + mm(grad_bc, w_in[2], 1, 1)
        + mm(grad_raw, w_dt_rows)
    )
    for p in range(n_head):
        grow_send[p] = grad_rows[p * quarter : (p + 1) * quarter]
    to_heads(lambda peer: grow_send.at[peer], grow_all, ROWS)
    grow_all[mine] = grow_send[mine]

    def over_heads(everything):
        total = everything[0].astype(F32)
        for p in range(1, n_head):
            total = total + everything[p].astype(F32)
        return total

    z_stage(y2_send, y2_all, z2_send, z2_all, ALONG_Z2, ALONG_Y2)
    z_stage(y4_send, y4_all, z4_send, z4_all, ALONG_Z4, ALONG_Y4)
    arrived(y3_all.at[pl.ds(0, n_y - 1)], ALONG_Y3)
    z3_send[...] = over(y3_send[at_y], y3_all, at_y, n_y)
    to_z(lambda peer: z3_send, z3_all, ALONG_Z3)
    arrived(zb_all.at[pl.ds(0, NZ - 1)], FIRST_Z)
    yb_send[...] = bf(over(zb_send[at_z].astype(F32), zb_all, at_z, NZ))
    to_y(lambda peer: yb_send.at[peer], yb_all, THEN_Y)
    arrived(layer_all.at[pl.ds(0, n_head - 1)], LAYER)
    layer_ref[...] = bf(over_heads(layer_all))
    total1 = last_stage(z1_send, z1_all, ALONG_Z1)
    w_out_ref[...] = total1[:, :inner]
    w_in_ref[0] = total1[:, inner : 2 * inner]
    w_in_ref[2, :, N:] = total1[:, 2 * inner :]
    arrived(grow_all.at[pl.ds(0, n_head - 1)], ROWS)
    rows_ref[...] = over_heads(grow_all)
    w_in_ref[1, :, :half] = last_stage(z2_send, z2_all, ALONG_Z2)
    w_in_ref[1, :, half:] = last_stage(z4_send, z4_all, ALONG_Z4)
    arrived(z3_all.at[pl.ds(0, NZ - 1)], ALONG_Z3)
    total3 = over(z3_send[...], z3_all, at_z, NZ)
    thin = total3
    for z in range(1, NZ):
        thin = jnp.where(at_z == z, pltpu.roll(total3, N - z * ROW, 1), thin)
    w_dt_ref[...] = thin.T[:heads]
    arrived(yb_all.at[pl.ds(0, n_y - 1)], THEN_Y)
    w_in_ref[2, :, :N] = over(yb_send[at_y].astype(F32), yb_all, at_y, n_y)

    departed(rim_pre, RIM)
    departed(rim_in, RIM_ROWS)
    departed(rim2_in, RIM2)
    departed(rim3_in, RIM3)
    for ref, which in (
        (dec_all, DEC),
        (state_all, SCAN1),
        (prefix_all, BACK1),
        (back_all, SCAN2),
        (suffix_all, BACK2),
    ):
        departed(ref.at[pl.ds(0, ROW - 1)], which)
    for ref, which in ((norm_all, NORM), (layer_all, LAYER), (grow_all, ROWS)):
        departed(ref.at[pl.ds(0, n_head - 1)], which)
    for ref, which in (
        (total_all, TOTAL1),
        (rest_all, TOTAL2),
        (y1_all, ALONG_Y1),
        (y2_all, ALONG_Y2),
        (y3_all, ALONG_Y3),
        (y4_all, ALONG_Y4),
        (yb_all, THEN_Y),
        (row_factor, FACTOR),
    ):
        departed(ref.at[pl.ds(0, n_y - 1)], which)
    for ref, which in (
        (z1_all, ALONG_Z1),
        (z2_all, ALONG_Z2),
        (z3_all, ALONG_Z3),
        (z4_all, ALONG_Z4),
        (zb_all, FIRST_Z),
    ):
        departed(ref.at[pl.ds(0, NZ - 1)], which)
    departed(core1_in, CORE1)
    departed(core2_in, CORE2)
    departed(core3_in, CORE3)


def hand_over(*refs):
    given, results, sems = refs[:5], refs[5:10], refs[10]
    stores = [pltpu.make_async_copy(given[k], results[k], sems.at[k]) for k in range(5)]
    for store in stores:
        store.start()
    for store in stores:
        store.wait()


def solution(mesh):
    n_tm, n_head = mesh.shape["tm"], mesh.shape["head"]

    def body(
        series,
        in_weight,
        step_weight,
        step_bias,
        log_rate,
        conv_weight,
        conv_bias,
        skip_gain,
        norm_gain,
        out_weight,
        cotangent,
    ):
        rows, model = series.shape
        inner = out_weight.shape[1]
        heads = step_bias.shape[0]
        few = model // n_tm
        quarter = rows // n_head
        n_chip = n_tm // 2
        n_y = n_tm // ROW
        vmem = pl.BlockSpec(memory_space=pltpu.VMEM)
        left = pl.BlockSpec(memory_space=pl.ANY)
        pieces = [v[None] for v in (step_bias, log_rate, skip_gain, norm_gain)] + [conv_bias]
        pieces.append(step_weight.T.astype(F32))
        height, at = sum(p.shape[0] for p in pieces), 0
        few_rows = jnp.zeros((height, model), F32)
        for p in pieces:
            below = height - at - p.shape[0]
            few_rows = few_rows + jnp.pad(p, ((at, below), (0, model - p.shape[1])))
            at += p.shape[0]
        arrays = (
            series,
            in_weight.transpose(1, 0, 2),
            conv_weight[None],
            out_weight,
            cotangent,
        )
        out_shape = (
            jax.ShapeDtypeStruct((quarter, model), BF16),
            jax.ShapeDtypeStruct((quarter, model), F32),
            jax.ShapeDtypeStruct((3, few, inner), F32),
            jax.ShapeDtypeStruct((heads, few), F32),
            jax.ShapeDtypeStruct((few, inner), F32),
        )

        def sums(width, first):
            return [
                pltpu.VMEM((2, n_chip, few, width), BF16),
                pltpu.VMEM((n_chip, few, width), BF16),
                pltpu.VMEM((n_y, NZ, few, first), BF16),
                pltpu.VMEM((n_y, NZ, few, first), BF16),
                pltpu.VMEM((NZ, few, first), BF16),
                pltpu.VMEM((NZ, few, first), BF16),
            ]

        per_owner = inner // ROW
        slab = pltpu.VMEM((ROW, per_owner, N), BF16)
        scan = [
            slab,
            slab,
            pltpu.VMEM((per_owner, N), BF16),
            pltpu.VMEM((n_y, per_owner, N), BF16),
            slab,
            slab,
        ]
        peers = pltpu.VMEM((n_head, quarter, model), BF16)
        results = pl.pallas_call(
            functools.partial(kernel, n_tm, n_head),
            out_shape=out_shape,
            in_specs=[left] * (1 + len(arrays)),
            out_specs=(vmem,) * 5,
            scratch_shapes=[pltpu.VMEM(few_rows.shape, F32)]
            + [pltpu.VMEM(a.shape, a.dtype) for a in arrays]
            + [
                pltpu.VMEM((16, model), BF16),
                pltpu.VMEM((8, 2 * inner), BF16),
                pltpu.VMEM((8, 2 * inner), BF16),
                pltpu.VMEM((heads, 1, N), F32),
                pltpu.VMEM((ROW, 1, N), F32),
            ]
            + scan
            + scan
            + [
                pltpu.VMEM((ROW, per_owner, N), F32),
                pltpu.VMEM((inner, N), F32),
                pltpu.VMEM((2, rows), F32),
                pltpu.VMEM((n_head, 2, rows), F32),
                peers,
                peers,
                peers,
                peers,
                pltpu.VMEM((8, inner + N), F32),
                pltpu.VMEM((8, inner + N), F32),
                pltpu.VMEM((8, N), F32),
                pltpu.VMEM((8, N), F32),
            ]
            + sums(2 * inner + N, 2 * inner + N)
            + sums(inner + N, inner // 2)
            + sums(inner + N, inner // 2)[2:]
            + [
                pltpu.VMEM((2, n_y, few, N), F32),
                pltpu.VMEM((n_y, few, N), F32),
                pltpu.VMEM((n_y, few, N), F32),
                pltpu.VMEM((n_y, few, N), F32),
                pltpu.VMEM((few, N), F32),
                pltpu.VMEM((NZ, few, N), F32),
                pltpu.VMEM((NZ, n_y, few, N), BF16),
                pltpu.VMEM((NZ, n_y, few, N), BF16),
                pltpu.VMEM((n_y, few, N), BF16),
                pltpu.VMEM((n_y, few, N), BF16),
                pltpu.VMEM((3, ROW, 1, N), F32),
                pltpu.VMEM((1, N), F32),
                pltpu.VMEM((n_y, 1, N), F32),
                pltpu.VMEM((rows + 8, 2 * inner), F32),
                pltpu.VMEM((rows, 2 * inner), F32),
                pltpu.VMEM((rows, 2 * inner), F32),
                pltpu.VMEM((heads, rows, rows), F32),
                pltpu.VMEM((rows, inner), F32),
                pltpu.VMEM((rows + 24, inner + N), F32),
                pltpu.SemaphoreType.DMA((LOADS,)),
                pltpu.SemaphoreType.DMA((COPIES,)),
                pltpu.SemaphoreType.DMA((COPIES,)),
            ],
            compiler_params=pltpu.CompilerParams(collective_id=0, has_side_effects=True, vmem_limit_bytes=GRANT),
        )(few_rows, *arrays)
        layer, rows_grad, w_in, w_dt, w_out = pl.pallas_call(
            hand_over,
            out_shape=out_shape,
            in_specs=[vmem] * 5,
            out_specs=(left,) * 5,
            scratch_shapes=[pltpu.SemaphoreType.DMA((5,))],
            compiler_params=pltpu.CompilerParams(vmem_limit_bytes=1024 * 1024),
        )(*results)
        return (layer, rows_grad, w_in.transpose(1, 0, 2), w_dt.T, w_out)

    in_specs = (
        P("tm", None),
        P(None, None, "head"),
        P(None, "head"),
        P("head"),
        P("head"),
        P(None, None, "head"),
        P(None, "head"),
        P("head"),
        P("head"),
        P(None, "head"),
        P("tm", None),
    )
    out_specs = (
        P(("tm", "head"), None),
        P(("tm", "head"), None),
        P("tm", None, "head"),
        P("tm", "head"),
        P("tm", "head"),
    )
    return jax.shard_map(body, mesh=mesh, in_specs=in_specs, out_specs=out_specs, check_vma=False)
```

```python
import functools

import jax
import jax.numpy as jnp
from jax import lax
from jax.experimental import pallas as pl
from jax.experimental.pallas import tpu as pltpu
from jax.sharding import PartitionSpec as P

N = 128
KW = 4
E = 1024
EPS = 1e-05
MESH = pl.DeviceIdType.MESH
F32 = jnp.float32
BF16 = jnp.bfloat16

NZ = 8
ROW = 2 * NZ
RIM, DEC, SCAN1, TOTAL1, BACK1, NORM, LAYER, SCAN2, TOTAL2, BACK2 = range(10)
RIM2, RIM3, ROWS, CORE1, ALONG_Y1, ALONG_Z1, CORE2, ALONG_Y2, ALONG_Z2 = range(10, 19)
CORE3, ALONG_Y3, ALONG_Z3, FIRST_Z, THEN_Y, FACTOR, RIM_ROWS, ALONG_Y4, ALONG_Z4 = range(19, 28)
COPIES = 28
LOADS = 6
BIAS, RATE, SKIP, GAIN, CONV_B = range(5)
W_DT = CONV_B + 2
GRANT = 56200000


def bf(v):
    return v.astype(BF16)


def mm(a, b, ca=1, cb=0):
    return lax.dot_general(
        bf(a), bf(b), (((ca,), (cb,)), ((), ())), preferred_element_type=F32
    )


def parts_of(v, count):
    parts = []
    for _ in range(count):
        head = bf(v)
        parts.append(head)
        v = v - head.astype(F32)
    return parts


def mm_left(exact, v, ca=1, cb=0, count=3):
    total = None
    for part in parts_of(v, count):
        term = mm(exact, part, ca, cb)
        total = term if total is None else total + term
    return total


def mm_right(v, exact, ca=1, cb=0, count=3):
    total = None
    for part in parts_of(v, count):
        term = mm(part, exact, ca, cb)
        total = term if total is None else total + term
    return total


def sigmoid(v):
    return 1.0 / (1.0 + jnp.exp(-v))


def softplus(v):
    return jnp.maximum(v, 0.0) + jnp.log1p(jnp.exp(-jnp.abs(v)))


def spread(row, heads, shape, width):
    lane = lax.broadcasted_iota(jnp.int32, shape, 1) // width
    out = jnp.zeros(shape, F32)
    for h in range(heads):
        out = jnp.where(lane == h, row[:, h : h + 1], out)
    return out


def kernel(
    n_tm,
    n_head,
    small_hbm,
    series_hbm,
    w_in_hbm,
    conv_w_hbm,
    w_out_hbm,
    cot_hbm,
    layer_ref,
    rows_ref,
    w_in_ref,
    w_dt_ref,
    w_out_ref,
    small,
    series,
    w_in,
    conv_w,
    w_out,
    cot,
    rim_in,
    rim_send,
    rim_pre,
    dec_send,
    dec_all,
    state_send,
    state_all,
    total_send,
    total_all,
    prefix_send,
    prefix_all,
    back_send,
    back_all,
    rest_send,
    rest_all,
    suffix_send,
    suffix_all,
    within,
    own_keep,
    norm_send,
    norm_all,
    layer_send,
    layer_all,
    grow_send,
    grow_all,
    rim2_send,
    rim2_in,
    rim3_send,
    rim3_in,
    core1_send,
    core1_in,
    y1_send,
    y1_all,
    z1_send,
    z1_all,
    core2_send,
    core2_in,
    y2_send,
    y2_all,
    z2_send,
    z2_all,
    y4_send,
    y4_all,
    z4_send,
    z4_all,
    core3_send,
    core3_in,
    y3_send,
    y3_all,
    z3_send,
    z3_all,
    zb_send,
    zb_all,
    yb_send,
    yb_all,
    factors,
    row_factor_send,
    row_factor,
    pre_buf,
    conv_buf,
    act_buf,
    decays,
    inside_buf,
    gc_buf,
    load_sem,
    send_sem,
    recv_sem,
):
    me = lax.axis_index("tm")
    mine = lax.axis_index("head")
    core = lax.rem(me, 2)
    place = lax.rem(me, ROW)
    at_z = place // 2
    at_y = me // ROW
    n_y = n_tm // ROW
    n_chip = n_tm // 2
    rows, model = series.shape
    inner = w_out.shape[1]
    heads = w_dt_ref.shape[0]
    size = inner // heads
    per_owner = inner // ROW
    owners_per_head = ROW // heads
    quarter = rows // n_head
    few = model // n_tm
    nxt, prv = lax.rem(me + 1, n_tm), lax.rem(me + n_tm - 1, n_tm)

    loads = [
        pltpu.make_async_copy(src, dst, load_sem.at[k])
        for k, (src, dst) in enumerate(
            [
                (small_hbm, small),
                (series_hbm, series),
                (w_in_hbm, w_in),
                (conv_w_hbm, conv_w),
                (cot_hbm, cot),
                (w_out_hbm, w_out),
            ]
        )
    ]
    for load in loads:
        load.start()

    barrier = pltpu.get_barrier_semaphore()
    far_first = sorted(range(1, ROW), key=lambda d: -min(d, ROW - d))
    across = (2, 1, 3)
    z_first = (4, 3, 5, 2, 6, 1, 7)
    row_peers = [at_y * ROW + lax.rem(place + d, ROW) for d in far_first]
    y_peers = [lax.rem(at_y + d, n_y) for d in across]
    z_peers = [lax.rem(at_z + d, NZ) for d in z_first]
    head_peers = [lax.rem(mine + d, n_head) for d in across]

    def greet(device):
        pl.semaphore_signal(barrier, inc=1, device_id=device, device_id_type=MESH)

    for peer in row_peers:
        greet((peer, mine))
    for peer in y_peers:
        greet((peer * ROW + place, mine))
    for peer in head_peers:
        greet((me, peer))
    greet((nxt, mine))
    greet((prv, mine))
    greeted = len(row_peers) + len(y_peers) + len(head_peers) + 2
    def push(src, dst, which, device):
        pltpu.make_async_remote_copy(
            src_ref=src,
            dst_ref=dst,
            send_sem=send_sem.at[which],
            recv_sem=recv_sem.at[which],
            device_id=device,
            device_id_type=MESH,
        ).start()

    def arrived(ref, which):
        pltpu.make_async_copy(ref, ref, recv_sem.at[which]).wait()

    def departed(ref, which):
        pltpu.make_async_copy(ref, ref, send_sem.at[which]).wait()

    def to_row(source_of, dst, which):
        for peer in row_peers:
            at = lax.rem(peer, ROW)
            push(source_of(at), dst.at[place], which, (peer, mine))

    def to_heads(source_of, dst, which):
        for peer in head_peers:
            push(source_of(peer), dst.at[mine], which, (me, peer))

    def to_y(source_of, dst, which):
        for peer in y_peers:
            push(source_of(peer), dst.at[at_y], which, (peer * ROW + place, mine))

    def to_z(source_of, dst, which):
        for peer in z_peers:
            to = at_y * ROW + peer * 2 + core
            push(source_of(peer), dst.at[at_z], which, (to, mine))

    def over(first, everything, at, count):
        total = first
        for d in range(1, count):
            total = total + everything[lax.rem(at + d, count)].astype(F32)
        return total

    def chosen(width, per):
        return (
            lax.broadcasted_iota(jnp.int32, (width, heads), 0) // per
            == lax.broadcasted_iota(jnp.int32, (width, heads), 1)
        ).astype(BF16)

    for k in (0, 3):
        loads[k].wait()
    rate_wide = jnp.exp(spread(small[RATE : RATE + 1, :N], heads, (1, inner), size))
    skip_wide = spread(small[SKIP : SKIP + 1, :N], heads, (1, inner), size)
    row_id = lax.broadcasted_iota(jnp.int32, (rows, rows), 0)
    col_id = lax.broadcasted_iota(jnp.int32, (rows, rows), 1)
    below = col_id <= row_id
    w_dt = small[W_DT : W_DT + heads, :]
    w_dt_wide = bf(mm(chosen(inner, size), w_dt))
    w_dt_rows = bf(mm(chosen(N, 1), w_dt))
    loads[1].wait()
    step = softplus(mm(series[...], w_dt_wide, 1, 1) + spread(small[BIAS : BIAS + 1, :N], heads, (1, inner), size))
    shift_n = mm(series[...], w_dt_rows, 1, 1) + spread(small[BIAS : BIAS + 1, :N], heads, (1, N), 1)
    run = mm_left(below.astype(BF16), -step * rate_wide)
    last = run[rows - 1 : rows, :]
    for h in range(heads):
        dec_send[h] = jnp.broadcast_to(last[:, h * size : h * size + 1], (1, N))
    loads[2].wait()
    pre_buf[pl.ds(0, 8), :] = jnp.zeros((8, 2 * inner), F32)
    pre_buf[pl.ds(8, rows), :inner] = bf(mm(series[...], w_in[1])).astype(F32)
    pre_buf[pl.ds(8, rows), inner:] = bf(mm(series[...], w_in[2])).astype(F32)
    rim_send[...] = bf(pre_buf[pl.ds(rows, 8), :])

    pl.semaphore_wait(barrier, greeted)
    push(rim_send, rim_pre, RIM, (nxt, mine))
    push(series.at[pl.ds(rows - 16, 16)], rim_in, RIM_ROWS, (nxt, mine))
    to_row(lambda at: dec_send.at[at // owners_per_head], dec_all, DEC)
    dec_all[place] = dec_send[place // owners_per_head]

    remain = jnp.exp(last - run)
    weight = remain * step

    def conv_row(k):
        return jnp.concatenate([conv_w[0, k, 0:1, :], conv_w[0, k, 1:2, :]], axis=1)


    def convolve(count):
        conv = jnp.concatenate([small[CONV_B : CONV_B + 1, :inner], small[CONV_B + 1 : CONV_B + 2, :inner]], axis=1)
        for k in range(KW):
            conv = conv + conv_row(k) * pre_buf[pl.ds(8 - (KW - 1) + k, count), :]
        conv_sig = sigmoid(conv)
        conv_buf[pl.ds(0, count), :] = conv_sig * (1.0 + conv * (1.0 - conv_sig))
        active = bf(conv * conv_sig).astype(F32)
        act_buf[pl.ds(0, count), :] = active
        return active

    active = convolve(rows)
    first = 16
    later = lax.broadcasted_iota(jnp.int32, (rows, inner), 0) >= first
    own = mm(jnp.where(later, weight * active[:, :inner], 0.0), active[:, inner : inner + N], 0, 0)
    arrived(rim_pre, RIM)
    pre_buf[pl.ds(0, 8), :] = jnp.where(me > 0, rim_pre[...].astype(F32), 0.0)
    active = convolve(first)
    own = own + mm(weight[:first] * active[:, :inner], active[:, inner : inner + N], 0, 0)

    def exchange(own, send, everything, totals, all_totals, out_send, out_all, which, during):
        scan, total, back = which
        reverse = scan == SCAN2
        slabs = (ROW, per_owner, N)
        send[...] = bf(own).reshape(slabs)
        to_row(lambda at: send.at[at], everything, scan)
        everything[place] = send[place]
        kept = during()
        arrived(everything.at[pl.ds(0, ROW - 1)], scan)
        terms = [
            factors[1 if reverse else 2, k] * everything[k].astype(F32) for k in range(ROW)
        ]
        while len(terms) > 1:
            terms = [terms[k] + terms[k + 1] for k in range(0, len(terms), 2)]
        totals[...] = bf(terms[0])
        to_y(lambda peer: totals, all_totals, total)
        all_totals[at_y] = totals[...]
        state = jnp.zeros((per_owner, N), F32)
        for k in range(ROW - 1, -1, -1) if reverse else range(ROW):
            within[k] = state
            state = state * factors[0, k] + everything[k].astype(F32)
        if not reverse:
            arrived(row_factor.at[pl.ds(0, n_y - 1)], FACTOR)
        arrived(all_totals.at[pl.ds(0, n_y - 1)], total)
        outer = jnp.zeros((per_owner, N), F32)
        for k in range(n_y - 1, -1, -1) if reverse else range(n_y):
            new = outer * row_factor[k] + all_totals[k].astype(F32)
            outer = jnp.where(k > at_y if reverse else k < at_y, new, outer)
        def finished(at):
            return bf(within[at] + factors[2 if reverse else 1, at] * outer)

        for peer in row_peers:
            at = lax.rem(peer, ROW)
            out_send[at] = finished(at)
            push(out_send.at[at], out_all.at[place], back, (peer, mine))
        out_all[place] = finished(place)
        return kept

    def collect(out_all, back):
        arrived(out_all.at[pl.ds(0, ROW - 1)], back)
        return out_all[...].reshape(inner, N)

    def by_chip(v, send, lanes):
        v = bf(v).reshape(n_chip, 2, few, v.shape[1])
        for p in range(2):
            send[p, :, :, lanes] = v[:, p]

    def core_stage(send, into, which):
        push(send.at[1 - core], into, which, (me + 1 - 2 * core, mine))

    def y_stage(core_send, core_in, send, everything, which, core_which):
        arrived(core_in, core_which)
        total = core_send[core].astype(F32) + core_in[...].astype(F32)
        send[...] = total.astype(send.dtype).reshape(send.shape)
        to_y(lambda peer: send.at[peer], everything, which)

    def z_stage(y_send, y_all, send, everything, which, y_which):
        arrived(y_all.at[pl.ds(0, n_y - 1)], y_which)
        send[...] = over(y_send[at_y].astype(F32), y_all, at_y, n_y).astype(send.dtype)
        to_z(lambda peer: send.at[peer], everything, which)

    def last_stage(z_send, z_all, which):
        arrived(z_all.at[pl.ds(0, NZ - 1)], which)
        return over(z_send[at_z].astype(F32), z_all, at_z, NZ)

    own_keep[...] = own

    def intra_forward():
        x = bf(act_buf[:, :inner])
        b = bf(act_buf[:, inner : inner + N])
        c = bf(act_buf[:, inner + N :])
        run_t = run.T
        step_t = step.T
        scores = mm(c, b, 1, 1)
        for h in range(heads):
            at = slice(h * size, (h + 1) * size)
            gap = run[:, h * size : h * size + 1] - run_t[h * size : h * size + 1, :]
            decay = jnp.exp(jnp.where(below, gap, -1e30))
            decays[h] = decay
            mixing = scores * decay * step_t[h * size : h * size + 1, :]
            inside_buf[:, at] = mm(mixing, x[:, at])
        gate = bf(mm(series[...], w_in[0])).astype(F32)
        gate_sig = sigmoid(gate)
        for k in (4, 5):
            loads[k].wait()
        gain_grad = small[GAIN : GAIN + 1, :inner] * mm(cot[...], w_out[...])
        arrived(rim_in, RIM_ROWS)
        arrived(dec_all.at[pl.ds(0, ROW - 1)], DEC)
        for row, order in ((1, range(ROW)), (2, range(ROW - 1, -1, -1))):
            log = jnp.zeros((1, N), F32)
            for k in order:
                factors[row, k] = jnp.exp(log)
                log = log + dec_all[k]
        row_factor_send[...] = jnp.exp(log)
        to_y(lambda peer: row_factor_send, row_factor, FACTOR)
        row_factor[at_y] = row_factor_send[...]
        for k in range(ROW):
            factors[0, k] = jnp.exp(dec_all[k])
        return x, b, c, scores, run_t, step_t, jnp.exp(run), gate, gate_sig, gain_grad

    x, b, c, scores, run_t, step_t, grow, gate, gate_sig, gain_grad = exchange(
        own,
        state_send,
        state_all,
        total_send,
        total_all,
        prefix_send,
        prefix_all,
        (SCAN1, TOTAL1, BACK1),
        intra_forward,
    )
    xw = x.astype(F32)
    gate_act = gate * gate_sig
    start = collect(prefix_all, BACK1)

    ssm = inside_buf[...] + grow * mm(c, start, 1, 1)
    y = ssm + skip_wide * xw
    gated = y * gate_act
    ones = jnp.ones((8, inner), BF16)
    power = mm(ones, gated * gated, 1, 1)
    cross = mm(ones, gated * gain_grad, 1, 1)
    norm_send[0:1, :] = power[0:1]
    norm_send[1:2, :] = cross[0:1]
    to_heads(lambda peer: norm_send, norm_all, NORM)
    norm_all[mine] = norm_send[...]
    arrived(norm_all.at[pl.ds(0, n_head - 1)], NORM)
    totals = norm_all[0]
    for p in range(1, n_head):
        totals = totals + norm_all[p]
    inv_row = lax.rsqrt(totals[0:1] / E + EPS)
    coef_row = inv_row * inv_row * inv_row * totals[1:2] / E

    def down(row):
        lanes = jnp.broadcast_to(row, (N, rows)).T
        return jnp.concatenate([lanes] * (inner // N), axis=1)

    inv, coef = down(inv_row), down(coef_row)
    grad_gated = inv * gain_grad - gated * coef
    grad_y = grad_gated * gate_act
    gy = bf(grad_y)
    grown = bf(grow * grad_y)

    def unfold(lanes, at, count):
        def tap(k):
            return conv_row(k)[:, lanes] * pre_buf[pl.ds(at + KW - 1 - k, count), lanes]

        total = tap(0)
        for k in range(1, KW):
            total = total + tap(k)
        return bf(total)

    c_lanes = slice(inner + N, 2 * inner)
    xb_lanes = slice(0, inner + N)
    is_last = me == n_tm - 1

    choose = (
        lax.broadcasted_iota(jnp.int32, (inner, N), 0) // size
        == lax.broadcasted_iota(jnp.int32, (inner, N), 1)
    )
    pick = choose.astype(BF16)
    rate_n = jnp.exp(spread(small[RATE : RATE + 1, :N], heads, (1, N), 1))

    def intra_backward():
        group = jnp.zeros((rows, rows), F32)
        for h in range(heads):
            at = slice(h * size, (h + 1) * size)
            inside_buf[:, at] = mm(scores * decays[h], gy[:, at], 0, 0)
            group = group + decays[h] * mm(gy[:, at], x[:, at], 1, 1) * (
                step_t[h * size : h * size + 1, :]
            )
        grad_conv = (mm(group, b) + mm(grown, start)) * conv_buf[:, c_lanes]
        pre_buf[pl.ds(0, rows), c_lanes] = grad_conv
        rim3_send[...] = grad_conv[0:8]
        push(rim3_send, rim3_in, RIM3, (prv, mine))
        grad_b = mm(group, c, 0, 0)
        normed = bf(gated * inv * small[GAIN : GAIN + 1, :inner])
        grad_gate = bf(grad_gated * y * (gate_sig * (1.0 + gate * (1.0 - gate_sig))))
        by_chip(mm(cot[...], normed, 0, 0), core1_send, slice(0, inner))
        by_chip(mm(series[...], grad_gate, 0, 0), core1_send, slice(inner, 2 * inner))
        part = bf(mm(normed, w_out[...], 1, 1))
        for p in range(n_head):
            layer_send[p] = part[p * quarter : (p + 1) * quarter]
        to_heads(lambda peer: layer_send.at[peer], layer_all, LAYER)
        layer_all[mine] = layer_send[mine]
        arrived(rim3_in, RIM3)
        pre_buf[pl.ds(rows, 8), c_lanes] = jnp.where(is_last, 0.0, rim3_in[...])
        grad_pre_c = unfold(c_lanes, 0, rows)
        by_chip(mm(series[...], grad_pre_c, 0, 0), core1_send, slice(2 * inner, 2 * inner + N))
        core_stage(core1_send, core1_in, CORE1)
        along_y = mm_right(grad_y * ssm, pick, 1, 0, 2)
        final = jnp.exp(run_t[:, rows - 1 : rows]) * start.astype(F32) + own_keep[...]
        base = skip_wide * grad_y + step * inside_buf[...]
        sizes = softplus(shift_n), sigmoid(shift_n)
        return grad_b, grad_gate, grad_pre_c, along_y, *sizes, final, base, bf(weight * xw)

    grad_b, grad_gate, grad_pre_c, along_y, step_n, slope_n, final, base, weighed = exchange(
        mm(grown, c, 0, 0),
        back_send,
        back_all,
        rest_send,
        rest_all,
        suffix_send,
        suffix_all,
        (SCAN2, TOTAL2, BACK2),
        intra_backward,
    )
    y_stage(core1_send, core1_in, y1_send, y1_all, ALONG_Y1, CORE1)
    after = collect(suffix_all, BACK2)

    reached = mm(b, after, 1, 1)
    grad_x = base + weight * reached
    grad_b = grad_b + mm(weighed, after)
    gc = jnp.concatenate([grad_x, grad_b], axis=1) * conv_buf[:, xb_lanes]
    rim2_send[...] = gc[0:8]
    push(rim2_send, rim2_in, RIM2, (prv, mine))
    gc_buf[pl.ds(0, 16), :] = jnp.zeros((16, inner + N), F32)
    gc_buf[pl.ds(16, rows), :] = gc
    gc_buf[pl.ds(16 + rows, 8), :] = jnp.zeros((8, inner + N), F32)

    def unfold_own(at, count):
        total = conv_row(0)[:, xb_lanes] * gc_buf[pl.ds(at + KW - 1, count), :]
        for k in range(1, KW):
            tap = conv_row(k)[:, xb_lanes] * gc_buf[pl.ds(at + KW - 1 - k, count), :]
            total = total + tap
        return bf(total)

    before = unfold_own(0, 16)
    before = jnp.where(me > 0, before, jnp.zeros_like(before))
    pre_own = unfold_own(16, rows)
    by_chip(mm(series[...], pre_own, 0, 0) + mm(rim_in[...], before, 0, 0), core2_send, slice(None))
    core_stage(core2_send, core2_in, CORE2)

    x_back = mm_right(xw * (inside_buf[...] + remain * reached), pick, 1, 0, 2)
    grad_cum = along_y - step_n * x_back
    carried = jnp.sum(
        jnp.where(choose, jnp.sum(after.astype(F32) * final, axis=1, keepdims=True), 0.0),
        axis=0,
        keepdims=True,
    )
    grad_log = mm_left((col_id >= row_id).astype(BF16), grad_cum, 1, 0, 2) + carried
    grad_raw = bf((x_back - rate_n * grad_log) * slope_n)
    thin = mm(series[...], grad_raw, 0, 0).reshape(n_y, NZ, 2, few, N)
    packed = thin[:, 0]
    for z in range(1, NZ):
        packed = packed + pltpu.roll(thin[:, z].reshape(n_y * 2 * few, N), z * ROW, 1).reshape(
            n_y, 2, few, N
        )
    for p in range(2):
        core3_send[p] = packed[:, p]
    core_stage(core3_send, core3_in, CORE3)

    arrived(core2_in, CORE2)
    pair = core2_send[core].astype(F32) + core2_in[...].astype(F32)
    half = inner // 2
    y2_send[...] = bf(pair[:, :, :half]).reshape(y2_send.shape)
    to_y(lambda peer: y2_send.at[peer], y2_all, ALONG_Y2)
    y4_send[...] = bf(pair[:, :, half:inner]).reshape(y4_send.shape)
    to_y(lambda peer: y4_send.at[peer], y4_all, ALONG_Y4)
    thick = bf(pair[:, :, inner:]).reshape(n_y, NZ, few, N)
    for z in range(NZ):
        zb_send[z] = thick[:, z]
    to_z(lambda peer: zb_send.at[peer], zb_all, FIRST_Z)
    z_stage(y1_send, y1_all, z1_send, z1_all, ALONG_Z1, ALONG_Y1)
    y_stage(core3_send, core3_in, y3_send, y3_all, ALONG_Y3, CORE3)

    arrived(rim2_in, RIM2)
    gc_buf[pl.ds(16 + rows, 8), :] = jnp.where(is_last, 0.0, rim2_in[...])
    main = rows - 16
    grad_pre = jnp.concatenate([pre_own[:main], unfold_own(rows, 16)], axis=0)
    grad_bc = jnp.concatenate([grad_pre[:, inner:], grad_pre_c], axis=1)
    grad_rows = bf(
        mm(grad_gate, w_in[0], 1, 1)
        + mm(grad_pre[:, :inner], w_in[1], 1, 1)
        + mm(grad_bc, w_in[2], 1, 1)
        + mm(grad_raw, w_dt_rows)
    )
    for p in range(n_head):
        grow_send[p] = grad_rows[p * quarter : (p + 1) * quarter]
    to_heads(lambda peer: grow_send.at[peer], grow_all, ROWS)
    grow_all[mine] = grow_send[mine]

    def over_heads(everything):
        total = everything[0].astype(F32)
        for p in range(1, n_head):
            total = total + everything[p].astype(F32)
        return total

    z_stage(y2_send, y2_all, z2_send, z2_all, ALONG_Z2, ALONG_Y2)
    z_stage(y4_send, y4_all, z4_send, z4_all, ALONG_Z4, ALONG_Y4)
    arrived(y3_all.at[pl.ds(0, n_y - 1)], ALONG_Y3)
    z3_send[...] = over(y3_send[at_y], y3_all, at_y, n_y)
    to_z(lambda peer: z3_send, z3_all, ALONG_Z3)
    arrived(zb_all.at[pl.ds(0, NZ - 1)], FIRST_Z)
    yb_send[...] = bf(over(zb_send[at_z].astype(F32), zb_all, at_z, NZ))
    to_y(lambda peer: yb_send.at[peer], yb_all, THEN_Y)
    arrived(layer_all.at[pl.ds(0, n_head - 1)], LAYER)
    layer_ref[...] = bf(over_heads(layer_all))
    total1 = last_stage(z1_send, z1_all, ALONG_Z1)
    w_out_ref[...] = total1[:, :inner]
    w_in_ref[0] = total1[:, inner : 2 * inner]
    w_in_ref[2, :, N:] = total1[:, 2 * inner :]
    arrived(grow_all.at[pl.ds(0, n_head - 1)], ROWS)
    rows_ref[...] = over_heads(grow_all)
    w_in_ref[1, :, :half] = last_stage(z2_send, z2_all, ALONG_Z2)
    w_in_ref[1, :, half:] = last_stage(z4_send, z4_all, ALONG_Z4)
    arrived(z3_all.at[pl.ds(0, NZ - 1)], ALONG_Z3)
    total3 = over(z3_send[...], z3_all, at_z, NZ)
    thin = total3
    for z in range(1, NZ):
        thin = jnp.where(at_z == z, pltpu.roll(total3, N - z * ROW, 1), thin)
    w_dt_ref[...] = thin.T[:heads]
    arrived(yb_all.at[pl.ds(0, n_y - 1)], THEN_Y)
    w_in_ref[2, :, :N] = over(yb_send[at_y].astype(F32), yb_all, at_y, n_y)

    departed(rim_pre, RIM)
    departed(rim_in, RIM_ROWS)
    departed(rim2_in, RIM2)
    departed(rim3_in, RIM3)
    for ref, which in (
        (dec_all, DEC),
        (state_all, SCAN1),
        (prefix_all, BACK1),
        (back_all, SCAN2),
        (suffix_all, BACK2),
    ):
        departed(ref.at[pl.ds(0, ROW - 1)], which)
    for ref, which in ((norm_all, NORM), (layer_all, LAYER), (grow_all, ROWS)):
        departed(ref.at[pl.ds(0, n_head - 1)], which)
    for ref, which in (
        (total_all, TOTAL1),
        (rest_all, TOTAL2),
        (y1_all, ALONG_Y1),
        (y2_all, ALONG_Y2),
        (y3_all, ALONG_Y3),
        (y4_all, ALONG_Y4),
        (yb_all, THEN_Y),
        (row_factor, FACTOR),
    ):
        departed(ref.at[pl.ds(0, n_y - 1)], which)
    for ref, which in (
        (z1_all, ALONG_Z1),
        (z2_all, ALONG_Z2),
        (z3_all, ALONG_Z3),
        (z4_all, ALONG_Z4),
        (zb_all, FIRST_Z),
    ):
        departed(ref.at[pl.ds(0, NZ - 1)], which)
    departed(core1_in, CORE1)
    departed(core2_in, CORE2)
    departed(core3_in, CORE3)


def hand_over(*refs):
    given, results, sems = refs[:5], refs[5:10], refs[10]
    stores = [pltpu.make_async_copy(given[k], results[k], sems.at[k]) for k in range(5)]
    for store in stores:
        store.start()
    for store in stores:
        store.wait()


def solution(mesh):
    n_tm, n_head = mesh.shape["tm"], mesh.shape["head"]

    def body(
        series,
        in_weight,
        step_weight,
        step_bias,
        log_rate,
        conv_weight,
        conv_bias,
        skip_gain,
        norm_gain,
        out_weight,
        cotangent,
    ):
        rows, model = series.shape
        inner = out_weight.shape[1]
        heads = step_bias.shape[0]
        few = model // n_tm
        quarter = rows // n_head
        n_chip = n_tm // 2
        n_y = n_tm // ROW
        vmem = pl.BlockSpec(memory_space=pltpu.VMEM)
        left = pl.BlockSpec(memory_space=pl.ANY)
        pieces = [v[None] for v in (step_bias, log_rate, skip_gain, norm_gain)] + [conv_bias]
        pieces.append(step_weight.T.astype(F32))
        height, at = sum(p.shape[0] for p in pieces), 0
        few_rows = jnp.zeros((height, model), F32)
        for p in pieces:
            below = height - at - p.shape[0]
            few_rows = few_rows + jnp.pad(p, ((at, below), (0, model - p.shape[1])))
            at += p.shape[0]
        arrays = (
            series,
            in_weight.transpose(1, 0, 2),
            conv_weight[None],
            out_weight,
            cotangent,
        )
        out_shape = (
            jax.ShapeDtypeStruct((quarter, model), BF16),
            jax.ShapeDtypeStruct((quarter, model), F32),
            jax.ShapeDtypeStruct((3, few, inner), F32),
            jax.ShapeDtypeStruct((heads, few), F32),
            jax.ShapeDtypeStruct((few, inner), F32),
        )

        def sums(width, first):
            return [
                pltpu.VMEM((2, n_chip, few, width), BF16),
                pltpu.VMEM((n_chip, few, width), BF16),
                pltpu.VMEM((n_y, NZ, few, first), BF16),
                pltpu.VMEM((n_y, NZ, few, first), BF16),
                pltpu.VMEM((NZ, few, first), BF16),
                pltpu.VMEM((NZ, few, first), BF16),
            ]

        per_owner = inner // ROW
        slab = pltpu.VMEM((ROW, per_owner, N), BF16)
        scan = [
            slab,
            slab,
            pltpu.VMEM((per_owner, N), BF16),
            pltpu.VMEM((n_y, per_owner, N), BF16),
            slab,
            slab,
        ]
        peers = pltpu.VMEM((n_head, quarter, model), BF16)
        results = pl.pallas_call(
            functools.partial(kernel, n_tm, n_head),
            out_shape=out_shape,
            in_specs=[left] * (1 + len(arrays)),
            out_specs=(vmem,) * 5,
            scratch_shapes=[pltpu.VMEM(few_rows.shape, F32)]
            + [pltpu.VMEM(a.shape, a.dtype) for a in arrays]
            + [
                pltpu.VMEM((16, model), BF16),
                pltpu.VMEM((8, 2 * inner), BF16),
                pltpu.VMEM((8, 2 * inner), BF16),
                pltpu.VMEM((heads, 1, N), F32),
                pltpu.VMEM((ROW, 1, N), F32),
            ]
            + scan
            + scan
            + [
                pltpu.VMEM((ROW, per_owner, N), F32),
                pltpu.VMEM((inner, N), F32),
                pltpu.VMEM((2, rows), F32),
                pltpu.VMEM((n_head, 2, rows), F32),
                peers,
                peers,
                peers,
                peers,
                pltpu.VMEM((8, inner + N), F32),
                pltpu.VMEM((8, inner + N), F32),
                pltpu.VMEM((8, N), F32),
                pltpu.VMEM((8, N), F32),
            ]
            + sums(2 * inner + N, 2 * inner + N)
            + sums(inner + N, inner // 2)
            + sums(inner + N, inner // 2)[2:]
            + [
                pltpu.VMEM((2, n_y, few, N), F32),
                pltpu.VMEM((n_y, few, N), F32),
                pltpu.VMEM((n_y, few, N), F32),
                pltpu.VMEM((n_y, few, N), F32),
                pltpu.VMEM((few, N), F32),
                pltpu.VMEM((NZ, few, N), F32),
                pltpu.VMEM((NZ, n_y, few, N), BF16),
                pltpu.VMEM((NZ, n_y, few, N), BF16),
                pltpu.VMEM((n_y, few, N), BF16),
                pltpu.VMEM((n_y, few, N), BF16),
                pltpu.VMEM((3, ROW, 1, N), F32),
                pltpu.VMEM((1, N), F32),
                pltpu.VMEM((n_y, 1, N), F32),
                pltpu.VMEM((rows + 8, 2 * inner), F32),
                pltpu.VMEM((rows, 2 * inner), F32),
                pltpu.VMEM((rows, 2 * inner), F32),
                pltpu.VMEM((heads, rows, rows), F32),
                pltpu.VMEM((rows, inner), F32),
                pltpu.VMEM((rows + 24, inner + N), F32),
                pltpu.SemaphoreType.DMA((LOADS,)),
                pltpu.SemaphoreType.DMA((COPIES,)),
                pltpu.SemaphoreType.DMA((COPIES,)),
            ],
            compiler_params=pltpu.CompilerParams(collective_id=0, has_side_effects=True, vmem_limit_bytes=GRANT),
        )(few_rows, *arrays)
        layer, rows_grad, w_in, w_dt, w_out = pl.pallas_call(
            hand_over,
            out_shape=out_shape,
            in_specs=[vmem] * 5,
            out_specs=(left,) * 5,
            scratch_shapes=[pltpu.SemaphoreType.DMA((5,))],
            compiler_params=pltpu.CompilerParams(vmem_limit_bytes=1024 * 1024),
        )(*results)
        return (layer, rows_grad, w_in.transpose(1, 0, 2), w_dt.T, w_out)

    in_specs = (
        P("tm", None),
        P(None, None, "head"),
        P(None, "head"),
        P("head"),
        P("head"),
        P(None, None, "head"),
        P(None, "head"),
        P("head"),
        P("head"),
        P(None, "head"),
        P("tm", None),
    )
    out_specs = (
        P(("tm", "head"), None),
        P(("tm", "head"), None),
        P("tm", None, "head"),
        P("tm", "head"),
        P("tm", "head"),
    )
    return jax.shard_map(body, mesh=mesh, in_specs=in_specs, out_specs=out_specs, check_vma=False)
```
